32 devices in a mesh: band: 4 (over x, core), grid: 8 (over z, y).
Axes of the slice: x: 2, y: 2, z: 4, core: 2. Of those that a mesh axis runs over, the one named last changes fastest.
Arguments:
- states: float32 [64, 64, 8, 128], P('band', 'grid'), may hold values from -6 to 6
- potential: float32 [64, 8, 128], P('grid'), may hold values from -1 to 1
- proj_index: int32 [16, 128], replicated, may hold values from 0 to 65535, as said below
- proj_value: float32 [16, 128], replicated, may hold values from 0 to 1
- proj_strength: float32 [16], replicated, may hold values from 0.5 to 4
Outputs:
- filtered: float32 [64, 64, 8, 128], P('band', 'grid')
- gram: float32 [64, 64], P('band')
- hamiltonian: float32 [64, 64], P('band')
The draws below stay inside these ranges and needn't reach their ends.
Inputs may be any that keep to these rules, and one draw needn't show every extreme that they name: `proj_index`: along the first grid dimension every support point lies within 8 planes of its atom's centre plane.
All inputs are finite; a program needn't handle non-finite values.
Results may differ from the reference program's by a relative error of at most 0.0001.
Values sent between devices are 32-bit elements; how exact they have to be, the bound alone decides.
A program may use at most 64 MiB of HBM per device.

```python
import math
import jax
import jax.numpy as jnp
from jax import lax

PL = 8
NY = 8
NZ = 128
RADIUS = 4
DEGREE = 4
NPTS = 128
NATOMS = 16
NX = 64
NPOINTS = 65536
NSTATES = 64


def support_geometry(key):
    subkeys = jax.random.split(jax.random.fold_in(key, 17), 7)
    centre_x = jax.random.randint(subkeys[0], (NATOMS, 1), 0, NX)
    centre_y = jax.random.randint(subkeys[1], (NATOMS, 1), 0, NY)
    centre_z = jax.random.randint(subkeys[2], (NATOMS, 1), 0, NZ)
    offset_x = jax.random.randint(subkeys[3], (NATOMS, NPTS), -PL, PL + 1)
    offset_y = jax.random.randint(subkeys[4], (NATOMS, NPTS), -(NY // 8), NY // 8 + 1)
    offset_z = jax.random.randint(subkeys[5], (NATOMS, NPTS), -(NZ // 8), NZ // 8 + 1)
    coord_x = jnp.clip(centre_x + offset_x, 0, NX - 1)
    coord_y = (centre_y + offset_y) % NY
    coord_z = (centre_z + offset_z) % NZ
    flat_points = (coord_x * (NY * NZ) + coord_y * NZ + coord_z).astype(jnp.int32)
    return (flat_points, offset_x, offset_y, offset_z, subkeys[6])


def draw_proj_index(key, part):
    flat_points, offset_x, offset_y, offset_z, factor_key = support_geometry(key)
    return flat_points


def draw_proj_value(key, part):
    flat_points, offset_x, offset_y, offset_z, factor_key = support_geometry(key)
    reach_x = float(PL)
    reach_z = float(max(NZ // 8, 1))
    scaled_x = offset_x.astype(jnp.float32) / reach_x
    scaled_y = offset_y.astype(jnp.float32)
    scaled_z = offset_z.astype(jnp.float32) / reach_z
    distance = scaled_x * scaled_x + scaled_y * scaled_y + scaled_z * scaled_z
    profile = jnp.exp(-distance)
    factor = jax.random.uniform(factor_key, (NATOMS, NPTS), jnp.float32, 0.5, 1.5)
    unscaled = profile * factor
    return (unscaled / jnp.sqrt(jnp.sum(unscaled * unscaled, axis=1, keepdims=True))).astype(jnp.float32)


def levels(own_key, shape, shards, smallest, top_value):
    level, own = 1.0, jax.random.fold_in(own_key, 6)
    for axis_at, parts in shards:
        heights = jnp.exp(jax.random.uniform(jax.random.fold_in(own, axis_at), (parts,), jnp.float32, smallest / len(shards), top_value / len(shards)))
        level = level * jnp.repeat(heights, shape[axis_at] // parts).reshape([-1 if axis == axis_at else 1 for axis in range(len(shape))])
    return level


def noise(rng, dims, width, bound, shards=(), dtype=jnp.bfloat16):
    drawn = width * jax.random.normal(rng, dims, jnp.float32)
    if shards:
        drawn = drawn * levels(rng, dims, shards, -0.22, 0.18)
    return jnp.clip(drawn, -bound, bound).astype(dtype)


def setup_inputs(seed: int = 0) -> dict:
    seeds = jax.random.split(jax.random.key(seed), 6)
    states = noise(seeds[0], (NSTATES, NX, NY, NZ), 1.0, 6.0, ((0, 4), (1, 8)), jnp.float32)
    potential = jnp.clip(jax.random.uniform(seeds[1], (NX, NY, NZ), jnp.float32, -1.0, 1.0) * levels(seeds[1], (NX, NY, NZ), ((0, 8),), -0.4, 0.0), -1.0, 1.0)
    proj_index = draw_proj_index(jax.random.fold_in(seeds[5], 71), 0)
    proj_value = draw_proj_value(jax.random.fold_in(seeds[5], 71), 0)
    proj_strength = jnp.clip(jnp.exp(jax.random.uniform(seeds[4], (NATOMS,), jnp.float32, math.log(0.5), math.log(4.0))), 0.5, 4.0)
    return {"states": states, "potential": potential, "proj_index": proj_index, "proj_value": proj_value, "proj_strength": proj_strength}


stencil_weights = (-205.0 / 72.0, 1.6, -0.2, 8.0 / 315.0, -1.0 / 560.0)
filter_centre = 10.0
filter_half = 6.0


def kinetic(padded):
    extent = padded.shape[-3] - 2 * RADIUS
    middle = padded[..., RADIUS:RADIUS + extent, :, :]
    grid_rows = middle.shape[-2]
    grid_cols = middle.shape[-1]
    pad_widths = [(0, 0)] * (middle.ndim - 2) + [(RADIUS, RADIUS), (RADIUS, RADIUS)]
    padded_yz = jnp.pad(middle, pad_widths)
    summed = 3.0 * stencil_weights[0] * middle
    for shift_by in range(1, RADIUS + 1):
        neighbours = padded[..., RADIUS + shift_by:RADIUS + shift_by + extent, :, :] + padded[..., RADIUS - shift_by:RADIUS - shift_by + extent, :, :]
        neighbours = neighbours + padded_yz[..., RADIUS + shift_by:RADIUS + shift_by + grid_rows, RADIUS:RADIUS + grid_cols] + padded_yz[..., RADIUS - shift_by:RADIUS - shift_by + grid_rows, RADIUS:RADIUS + grid_cols]
        neighbours = neighbours + padded_yz[..., RADIUS:RADIUS + grid_rows, RADIUS + shift_by:RADIUS + shift_by + grid_cols] + padded_yz[..., RADIUS:RADIUS + grid_rows, RADIUS - shift_by:RADIUS - shift_by + grid_cols]
        summed = summed + stencil_weights[shift_by] * neighbours
    return -0.5 * summed


def reference(states, potential, proj_index, proj_value, proj_strength):
    flat_index = proj_index.astype(jnp.int32)

    def apply_h(field):
        padded = jnp.pad(field, ((RADIUS, RADIUS), (0, 0), (0, 0)))
        kinetic_v = kinetic(padded)
        flat_v = field.reshape(-1)
        picked = flat_v[flat_index]
        coeffs = jnp.sum(proj_value * picked, axis=1)
        added = (proj_strength * coeffs)[:, None] * proj_value
        nonlocal_v = jnp.zeros_like(flat_v).at[flat_index.reshape(-1)].add(added.reshape(-1))
        return kinetic_v + potential * field + nonlocal_v.reshape(field.shape)

    def filter_one(state):
        previous = state
        current = (apply_h(state) - filter_centre * state) / filter_half
        for degree_k in range(1, DEGREE):
            following = 2.0 * (apply_h(current) - filter_centre * current) / filter_half - previous
            previous = current
            current = following
        return current, apply_h(current)

    filtered, images = lax.map(filter_one, states)
    flat_y = filtered.reshape(NSTATES, NPOINTS)
    flat_h = images.reshape(NSTATES, NPOINTS)
    gram = jnp.dot(flat_y, flat_y.T, precision=lax.Precision.HIGHEST) / float(NPOINTS)
    hamiltonian = jnp.dot(flat_h, flat_y.T, precision=lax.Precision.HIGHEST) / float(NPOINTS)
    return filtered, gram, hamiltonian
```

```python
import functools

import jax
import jax.numpy as jnp
from jax import lax
from jax.experimental import pallas as pl
from jax.experimental.pallas import tpu as pltpu
from jax.sharding import PartitionSpec as P

RADIUS = 4
DEGREE = 4
LANES = 128
MESH = pl.DeviceIdType.MESH

stencil_weights = (-205.0 / 72.0, 1.6, -0.2, 8.0 / 315.0, -1.0 / 560.0)
filter_centre = 10.0
filter_half = 6.0


def kernel(
    bands, slabs, planes, rows, cols, atoms, total_points,
    states, potential, index_in, value_in, strength_in,
    out_ref, gram_ref, ham_ref,
    raw, spare_raw, field, spare, pot, index_ref, value_ref, strength_ref, proj,
    coef_mine, coef_far, coef_first, coef_wide, back_y, both, prod, band_sum, mine, grid_sum,
    send, recv, local,
):
    half = states.shape[0] // 2
    area = rows * cols
    chunk = 2 * planes
    me_b, me_g = lax.axis_index("band"), lax.axis_index("grid")
    pair, side = me_g // 2, me_g % 2
    other = 1 - side
    last_pair = slabs // 2 - 1
    has_down, has_up = pair > 0, pair < last_pair
    counter = [0]

    def remote(src, dst, out_slot, in_slot, where):
        return pltpu.make_async_remote_copy(
            src_ref=src, dst_ref=dst, send_sem=send.at[out_slot], recv_sem=recv.at[in_slot],
            device_id=where, device_id_type=MESH,
        )

    def slots(count):
        first = counter[0]
        counter[0] += count
        return first

    def rows_at(plane, count):
        return pl.ds(pl.multiple_of(plane * rows, rows), count * rows)

    def group(g):
        return pl.ds(pl.multiple_of(g * half, half), half)

    partner = (me_b, 2 * pair + other)
    up, down = (me_b, me_g + 2), (me_b, me_g - 2)
    up_other, down_other = (me_b, 2 * pair + 2 + other), (me_b, 2 * pair - 2 + other)
    crossing = [
        (lax.rem(me_b + d, bands), 2 * pair + lax.rem(side + e, 2)) for d in range(1, bands) for e in range(2)
    ]
    barrier = pltpu.get_barrier_semaphore()

    def greet(where):
        pl.semaphore_signal(barrier, inc=1, device_id=where, device_id_type=MESH)

    def greet_pair(one, two):
        greet(one)
        greet(two)

    coef_far[...] = jnp.zeros_like(coef_far)
    coef_first[...] = jnp.zeros_like(coef_first)

    if last_pair > DEGREE:
        for d in range(1, slabs):
            greet((me_b, lax.rem(me_g + d, slabs)))
        expected = len(crossing) + slabs - 1
    else:
        greet(partner)
        pl.when(has_up)(lambda: greet_pair(up, up_other))
        pl.when(has_down)(lambda: greet_pair(down, down_other))
        expected = len(crossing) + 1 + 2 * (has_up.astype(jnp.int32) + has_down.astype(jnp.int32))
    for peer in crossing:
        greet(peer)

    own = [
        pltpu.make_async_copy(states.at[group(side)], raw.at[:, rows_at(RADIUS + side * planes, planes)], local.at[0]),
        pltpu.make_async_copy(states.at[group(other)], spare_raw, local.at[1]),
        pltpu.make_async_copy(index_in, index_ref, local.at[2]),
        pltpu.make_async_copy(value_in, value_ref, local.at[3]),
        pltpu.make_async_copy(potential, pot.at[pl.ds(side * planes, planes)], local.at[4]),
        pltpu.make_async_copy(strength_in, strength_ref, local.at[5]),
    ]
    for copy in own:
        copy.start()

    pl.semaphore_wait(barrier, expected)

    first = slots(5)
    toward, can = 2 * side - 1, jnp.where(side == 1, pair < last_pair, pair > 0)
    outer_at, inner_at = side * (planes - RADIUS), other * RADIUS
    fringes = [
        remote(
            states.at[pl.ds(h * half, half), rows_at(outer_at, RADIUS)],
            raw.at[:, rows_at(other * (RADIUS + chunk), RADIUS)],
            first + h, first + other, (me_b, 2 * (pair + toward) + h),
        )
        for h in range(2)
    ]
    swaps = [
        remote(
            states.at[group(other), rows_at(start, count)], raw.at[:, rows_at(RADIUS + side * planes + start, count)],
            first + 2 + n, first + 2 + n, partner,
        )
        for n, (start, count) in enumerate(((outer_at, RADIUS), (inner_at, planes - RADIUS)))
    ]
    pot_swap = remote(potential, pot.at[pl.ds(side * planes, planes)], first + 4, first + 4, partner)

    def start_fringes():
        for copy in fringes:
            copy.start()

    pl.when(can)(start_fringes)
    for copy in swaps:
        copy.start()
    pot_swap.start()

    points = index_ref.shape[1]
    row_iota = lax.broadcasted_iota(jnp.int32, (chunk * rows, points), 0) + pair * (chunk * rows)
    col_iota = lax.broadcasted_iota(jnp.int32, (cols, points), 0)

    def build(a, carry):
        idx = index_ref[pl.ds(a, 1), :]
        row = lax.div(idx, cols)
        here = row_iota == row
        onehot = jnp.where(col_iota == idx - row * cols, 1.0, 0.0).astype(jnp.bfloat16)
        rest = value_ref[pl.ds(a, 1), :]
        parts = []
        for _ in range(3):
            part = rest.astype(jnp.bfloat16).astype(jnp.float32)
            rest = rest - part
            parts.append(jnp.where(here, part, 0.0).astype(jnp.bfloat16))
        proj[a] = lax.dot_general(
            jnp.concatenate(parts, axis=1), jnp.concatenate([onehot] * 3, axis=1), (((1,), (1,)), ((), ())),
            preferred_element_type=jnp.float32,
        )
        return carry

    own[2].wait()
    own[3].wait()
    lax.fori_loop(0, atoms, build, 0)

    def relayout(src, src_at, dst, dst_at, count):
        def at_plane(n, carry):
            cube = jnp.swapaxes(src[:, rows_at(src_at + n, 1), :], 0, 1)
            for y in range(rows):
                dst[dst_at + n, :, y * cols : (y + 1) * cols] = cube[y]
            return carry

        lax.fori_loop(0, count, at_plane, 0)

    col = lax.broadcasted_iota(jnp.int32, (half, cols), 1)
    wide = coef_mine.shape[-1]
    wide_iota = lax.broadcasted_iota(jnp.int32, (half, wide), 1)
    block = 8

    def cells(plane):
        return [plane[:, y * cols : (y + 1) * cols] for y in range(rows)]

    def project(src, src_at, proj_at, count):
        def atoms_of(j, tile):
            def at_plane(n, sums):
                v = cells(src[src_at + n])
                parts = []
                for i in range(block):
                    s = sums[i]
                    for y in range(rows):
                        s = s + v[y] * proj[j * block + i, pl.ds((proj_at + n) * rows + y, 1), :]
                    parts.append(s)
                return tuple(parts)

            sums = lax.fori_loop(0, count, at_plane, tuple(jnp.zeros((half, cols), jnp.float32) for _ in range(block)))
            for i in range(block):
                tile = jnp.where(wide_iota == j * block + i, jnp.sum(sums[i], axis=1, keepdims=True), tile)
            return tile

        return lax.fori_loop(0, atoms // block, atoms_of, jnp.zeros((half, wide), jnp.float32))

    def local_part(k, p, a, b, low=chunk, high=chunk):
        src = field.at[k]
        cell = cells(src[p + RADIUS])
        ring = [None]
        for d in range(1, RADIUS + 1):
            near = [src[p + RADIUS + s * d] for s, room in ((1, high), (-1, low)) if d <= room]
            ring.append(near[0] + near[1] if len(near) == 2 else near[0] if near else None)
        weight = [-0.5 * a * w for w in stencil_weights]
        result = []
        for y in range(rows):
            v = cell[y]
            t = v * (a * pot[p, y : y + 1, :] + (3.0 * weight[0] + b))
            for d in range(1, RADIUS + 1):
                n = jnp.where(col < cols - d, pltpu.roll(v, cols - d, 1), 0.0)
                if ring[d] is not None:
                    n = n + ring[d][:, y * cols : (y + 1) * cols]
                if y + d < rows:
                    n = n + cell[y + d]
                if y - d >= 0:
                    n = n + cell[y - d]
                n = n + jnp.where(col >= d, pltpu.roll(v, d, 1), 0.0)
                t = t + weight[d] * n
            result.append(t)
        return result

    def nonlocal_part(p, tiles):
        def atoms_of(j, tiles):
            tiles = list(tiles)
            for i in range(block):
                c = coef_wide[j * block + i]
                for y in range(rows):
                    tiles[y] = tiles[y] + c * proj[j * block + i, pl.ds(p * rows + y, 1), :]
            return tuple(tiles)

        return lax.fori_loop(0, atoms // block, atoms_of, tuple(tiles), unroll=atoms // block <= 2)

    def store(k, p, tiles):
        for y in range(rows):
            field[k, p + RADIUS, :, y * cols : (y + 1) * cols] = tiles[y]

    def stored(k, p):
        return cells(field[k, p + RADIUS])

    halo_slots, coef_slots = slots(2 * (DEGREE + 1)), slots(2 * (DEGREE + 1))

    def halo_up(k):
        slot = halo_slots + 2 * k
        return remote(field.at[k, chunk : chunk + RADIUS], field.at[k, 0:RADIUS], slot, slot, up)

    def halo_down(k):
        slot = halo_slots + 2 * k + 1
        return remote(
            field.at[k, RADIUS : 2 * RADIUS], field.at[k, chunk + RADIUS : chunk + 2 * RADIUS], slot, slot, down
        )

    def coef_up(k):
        slot = coef_slots + 2 * k
        return remote(coef_mine.at[k], coef_far.at[k, 0], slot, slot, up)

    def coef_down(k):
        slot = coef_slots + 2 * k + 1
        return remote(coef_mine.at[k], coef_far.at[k, 1], slot, slot, down)

    first_slots = slots(5)
    other_mine = coef_mine.at[DEGREE + 1]
    early = [
        (None, remote(other_mine, coef_first.at[0], first_slots, first_slots, partner)),
        (has_up, remote(coef_mine.at[0], coef_first.at[1], first_slots + 1, first_slots + 1, up)),
        (has_up, remote(other_mine, coef_first.at[2], first_slots + 2, first_slots + 2, up_other)),
        (has_down, remote(coef_mine.at[0], coef_first.at[3], first_slots + 3, first_slots + 3, down)),
        (has_down, remote(other_mine, coef_first.at[4], first_slots + 4, first_slots + 4, down_other)),
    ]

    own[1].wait()
    relayout(spare_raw, 0, spare, 0, planes)
    coef_mine[DEGREE + 1] = project(spare, 0, side * planes, planes)
    own[0].wait()
    relayout(raw, RADIUS + side * planes, field.at[0], RADIUS + side * planes, planes)
    coef_mine[0] = project(field.at[0], RADIUS + side * planes, side * planes, planes)
    for ready, copy in early:
        if ready is None:
            copy.start()
        else:
            pl.when(ready)(copy.start)

    def set_wide(total):
        for a in range(atoms):
            coef_wide[a] = jnp.broadcast_to(total[:, a : a + 1] * strength_ref[:, a : a + 1], (half, cols))

    own[4].wait()
    own[5].wait()
    swaps[0].wait_recv()
    relayout(raw, RADIUS + other * (chunk - RADIUS), field.at[0], RADIUS + other * (chunk - RADIUS), RADIUS)
    swaps[1].wait_recv()
    relayout(
        raw, 2 * RADIUS + other * (planes - RADIUS), field.at[0], 2 * RADIUS + other * (planes - RADIUS),
        planes - RADIUS,
    )
    pot_swap.wait_recv()
    early[0][1].wait_recv()

    def wait_below():
        remote(
            states.at[pl.ds(0, half), rows_at(0, RADIUS)], raw.at[:, rows_at(0, RADIUS)], first, first, partner
        ).wait_recv()
        early[1][1].wait_recv()
        early[2][1].wait_recv()
        relayout(raw, 0, field.at[0], 0, RADIUS)

    def wait_above():
        remote(
            states.at[pl.ds(0, half), rows_at(0, RADIUS)], raw.at[:, rows_at(0, RADIUS)], first, first + 1, partner
        ).wait_recv()
        early[3][1].wait_recv()
        early[4][1].wait_recv()
        relayout(raw, RADIUS + chunk, field.at[0], RADIUS + chunk, RADIUS)

    def clear(at):
        def go():
            field[0, at : at + RADIUS] = jnp.zeros((RADIUS, half, area), jnp.float32)

        return go

    pl.when(has_down)(wait_below)
    pl.when(has_up)(wait_above)
    pl.when(jnp.logical_not(has_down))(clear(0))
    pl.when(jnp.logical_not(has_up))(clear(RADIUS + chunk))
    for k in range(1, DEGREE + 1):
        pl.when(jnp.logical_not(has_down))(
            functools.partial(field.__setitem__, (k, slice(0, RADIUS)), jnp.zeros((RADIUS, half, area), jnp.float32))
        )
        pl.when(jnp.logical_not(has_up))(
            functools.partial(
                field.__setitem__, (k, slice(RADIUS + chunk, 2 * RADIUS + chunk)),
                jnp.zeros((RADIUS, half, area), jnp.float32),
            )
        )

    scale0 = 1.0 / filter_half
    total = coef_mine[0]
    for n in range(5):
        total = total + coef_first[n]
    set_wide(total * scale0)

    def whole(p, carry):
        store(1, p, nonlocal_part(p, local_part(0, p, scale0, -filter_centre * scale0)))
        return carry

    lax.fori_loop(0, RADIUS, whole, 0)
    pl.when(has_down)(halo_down(1).start)
    lax.fori_loop(chunk - RADIUS, chunk, whole, 0)
    pl.when(has_up)(halo_up(1).start)
    lax.fori_loop(RADIUS, chunk - RADIUS, whole, 0)

    def apply(k, final):
        scale = 1.0 if final else 2.0 / filter_half
        shift = 0.0 if final else -filter_centre * scale
        coef_mine[k] = project(field.at[k], RADIUS, 0, chunk)
        pl.when(has_up)(coef_up(k).start)
        pl.when(has_down)(coef_down(k).start)

        def with_last(p, tiles):
            if final:
                return tiles
            old = cells(field[k - 1, p + RADIUS])
            return [tiles[y] - old[y] for y in range(rows)]

        def inner(p, carry):
            store(k + 1, p, with_last(p, local_part(k, p, scale, shift)))
            return carry

        for n in range(RADIUS):
            for p, low, high in ((n, n, chunk), (chunk - 1 - n, chunk, n)):
                store(k + 1, p, with_last(p, local_part(k, p, scale, shift, low, high)))
        lax.fori_loop(RADIUS, chunk - RADIUS, inner, 0)

        pl.when(has_down)(coef_up(k).wait_recv)
        pl.when(has_up)(coef_down(k).wait_recv)
        set_wide((coef_mine[k] + coef_far[k, 0] + coef_far[k, 1]) * scale)

        def add_nonlocal(p, carry):
            store(k + 1, p, nonlocal_part(p, stored(k + 1, p)))
            return carry

        def add_halo(p, planes_in):
            tiles = stored(k + 1, p)
            for w, plane in planes_in:
                far = cells(field[k, plane])
                tiles = [t + (-0.5 * scale * w) * far[y] for y, t in enumerate(tiles)]
            store(k + 1, p, tiles)

        def lower():
            lax.fori_loop(0, RADIUS, add_nonlocal, 0)
            pl.when(has_down)(halo_up(k).wait_recv)
            for p in range(RADIUS):
                add_halo(p, [(stencil_weights[d], RADIUS + p - d) for d in range(p + 1, RADIUS + 1)])

        def upper():
            lax.fori_loop(chunk - RADIUS, chunk, add_nonlocal, 0)
            pl.when(has_up)(halo_down(k).wait_recv)
            for n in range(RADIUS):
                p = chunk - 1 - n
                add_halo(p, [(stencil_weights[d], RADIUS + p + d) for d in range(n + 1, RADIUS + 1)])

        def middle():
            lax.fori_loop(RADIUS, chunk - RADIUS, add_nonlocal, 0)

        return lower, middle, upper

    def step(k, carry):
        lower, middle, upper = apply(k, False)
        lower()
        pl.when(has_down)(halo_down(k + 1).start)
        upper()
        pl.when(has_up)(halo_up(k + 1).start)
        middle()
        return carry

    lax.fori_loop(1, DEGREE, step, 0)

    part = planes // bands
    shares = 2 * bands
    y_out, y_in, h_out, h_in = slots(shares), slots(shares), slots(shares), slots(shares)
    mine_at = me_b * 2 + side

    def share(which, q):
        src = field.at[DEGREE + which, RADIUS + q * part : RADIUS + (q + 1) * part]
        dst = both.at[which, :, group(mine_at)]
        is_mine = jnp.logical_and(me_b == q % bands, side == q // bands)
        away = remote(
            src, dst, (y_out, h_out)[which] + q, (y_in, h_in)[which] + mine_at, (q % bands, 2 * pair + q // bands)
        )
        return is_mine, away, pltpu.make_async_copy(src, dst, local.at[which])

    def send_share(which, q):
        is_mine, away, keep = share(which, q)
        pl.when(is_mine)(keep.start)
        pl.when(jnp.logical_not(is_mine))(away.start)

    def take_shares(which):
        for q in range(shares):
            sender = q
            is_mine = jnp.logical_and(me_b == sender // 2, side == sender % 2)
            src = field.at[DEGREE + which, RADIUS : RADIUS + part]
            dst = both.at[which, :, pl.ds(sender * half, half)]
            come = remote(src, dst, y_out, (y_in, h_in)[which] + sender, partner)
            pl.when(is_mine)(pltpu.make_async_copy(src, dst, local.at[which]).wait)
            pl.when(jnp.logical_not(is_mine))(come.wait_recv)

    def sent_shares(which):
        for q in range(shares):
            is_mine, away, keep = share(which, q)
            pl.when(jnp.logical_not(is_mine))(away.wait_send)

    for q in range(shares):
        send_share(0, q)
    lower, middle, upper = apply(DEGREE, True)
    inside = [q for q in range(shares) if q * part >= RADIUS and (q + 1) * part <= chunk - RADIUS]
    middle()
    for q in inside:
        send_share(1, q)
    lower()
    for q in range(shares // 2):
        if q not in inside:
            send_share(1, q)
    upper()
    for q in range(shares // 2, shares):
        if q not in inside:
            send_share(1, q)

    back_slot = slots(1)
    back = remote(
        field.at[DEGREE, pl.ds(RADIUS + other * planes, planes)], back_y, back_slot, back_slot, partner
    )
    back.start()

    def inner_rows(left, right):
        return lax.dot_general(
            left, right, (((1,), (1,)), ((), ())),
            precision=lax.Precision.HIGHEST, preferred_element_type=jnp.float32,
        )

    states_all = bands * 2 * half
    take_shares(0)
    total = inner_rows(both[0, 0], both[0, 0])
    for i in range(1, part):
        total = total + inner_rows(both[0, i], both[0, i])
    prod[:, :states_all] = total
    take_shares(1)
    total = inner_rows(both[1, 0], both[0, 0])
    for i in range(1, part):
        total = total + inner_rows(both[1, i], both[0, i])
    prod[:, states_all:] = total

    rows_of = 2 * half
    r_slot, g_slot = slots(bands), slots(slabs)
    band_copies = []
    for d in range(1, bands):
        to_b = lax.rem(me_b + d, bands)
        copy = remote(
            prod.at[pl.ds(pl.multiple_of(to_b * rows_of, rows_of), rows_of)], band_sum.at[d],
            r_slot + d, r_slot + d, (to_b, me_g),
        )
        copy.start()
        band_copies.append(copy)
    total = prod[pl.ds(pl.multiple_of(me_b * rows_of, rows_of), rows_of), :]
    for copy in band_copies:
        copy.wait_recv()
    for d in range(1, bands):
        total = total + band_sum[d]
    mine[...] = total
    grid_copies = []
    for d in range(1, slabs):
        copy = remote(mine, grid_sum.at[d], g_slot + d, g_slot + d, (me_b, lax.rem(me_g + d, slabs)))
        copy.start()
        grid_copies.append(copy)

    def put_out(src, src_at, g):
        def at_plane(p, carry):
            cube = jnp.stack(cells(src[src_at + p]))
            out_ref[group(g), rows_at(p, 1), :] = jnp.swapaxes(cube, 0, 1)
            return carry

        lax.fori_loop(0, planes, at_plane, 0)

    put_out(field.at[DEGREE], RADIUS + side * planes, side)
    back.wait_recv()
    put_out(back_y, 0, other)
    for copy in grid_copies:
        copy.wait_recv()
    for d in range(1, slabs):
        total = total + grid_sum[d]
    total = total / total_points
    gram_ref[...] = total[:, :states_all]
    ham_ref[...] = total[:, states_all:]

    for copy in swaps + [pot_swap, early[0][1], back] + band_copies + grid_copies:
        copy.wait_send()
    for copy in fringes:
        pl.when(can)(copy.wait_send)
    for ready, copy in early[1:]:
        pl.when(ready)(copy.wait_send)
    for k in range(1, DEGREE + 1):
        for ready, copy in (
            (has_up, halo_up(k)), (has_down, halo_down(k)), (has_up, coef_up(k)), (has_down, coef_down(k))
        ):
            pl.when(ready)(copy.wait_send)
    sent_shares(0)
    sent_shares(1)


def per_device(bands, slabs, states, potential, proj_index, proj_value, proj_strength):
    state_count, planes, rows, cols = states.shape
    area = rows * cols
    points = planes * area
    atoms, support = proj_index.shape
    half = state_count // 2
    chunk = 2 * planes
    wide = -(-atoms // LANES) * LANES
    all_states = bands * state_count
    strength = proj_strength.reshape(1, atoms)
    slots = 5 + 4 * (DEGREE + 1) + 5 + 8 * bands + 1 + bands + slabs
    vmem, hbm = pl.BlockSpec(memory_space=pltpu.VMEM), pl.BlockSpec(memory_space=pltpu.HBM)
    f32 = jnp.float32
    out, gram, ham = pl.pallas_call(
        functools.partial(
            kernel, bands, slabs, planes, rows, cols, atoms, float(points * slabs)
        ),
        out_shape=(
            jax.ShapeDtypeStruct((state_count, planes * rows, cols), f32),
            jax.ShapeDtypeStruct((state_count, all_states), f32),
            jax.ShapeDtypeStruct((state_count, all_states), f32),
        ),
        in_specs=[hbm, hbm, hbm, hbm, hbm],
        out_specs=(vmem, vmem, vmem),
        scratch_shapes=[
            pltpu.VMEM((half, (chunk + 2 * RADIUS) * rows, cols), f32),
            pltpu.VMEM((half, planes * rows, cols), f32),
            pltpu.VMEM((DEGREE + 2, chunk + 2 * RADIUS, half, area), f32),
            pltpu.VMEM((planes, half, area), f32),
            pltpu.VMEM((chunk, rows, cols), f32),
            pltpu.VMEM((atoms, support), jnp.int32),
            pltpu.VMEM((atoms, support), f32),
            pltpu.VMEM((1, atoms), f32),
            pltpu.VMEM((atoms, chunk * rows, cols), f32),
            pltpu.VMEM((DEGREE + 2, half, wide), f32),
            pltpu.VMEM((DEGREE + 1, 2, half, wide), f32),
            pltpu.VMEM((5, half, wide), f32),
            pltpu.VMEM((atoms, half, cols), f32),
            pltpu.VMEM((planes, half, area), f32),
            pltpu.VMEM((2, planes // bands, all_states, area), f32),
            pltpu.VMEM((all_states, 2 * all_states), f32),
            pltpu.VMEM((bands, state_count, 2 * all_states), f32),
            pltpu.VMEM((state_count, 2 * all_states), f32),
            pltpu.VMEM((slabs, state_count, 2 * all_states), f32),
            pltpu.SemaphoreType.DMA((slots,)),
            pltpu.SemaphoreType.DMA((slots,)),
            pltpu.SemaphoreType.DMA((6,)),
        ],
        compiler_params=pltpu.CompilerParams(
            collective_id=0, has_side_effects=True, vmem_limit_bytes=48 * 1024 * 1024
        ),
    )(*(pltpu.with_memory_space_constraint(x, pltpu.HBM) for x in (states.reshape(state_count, planes * rows, cols), potential, proj_index, proj_value, strength)))

    def place(*refs):
        moves = [pltpu.make_async_copy(refs[n], refs[3 + n], refs[6].at[n]) for n in range(3)]
        for move in moves:
            move.start()
        for move in moves:
            move.wait()

    out, gram, ham = pl.pallas_call(
        place,
        out_shape=tuple(jax.ShapeDtypeStruct(x.shape, f32) for x in (out, gram, ham)),
        in_specs=[vmem] * 3,
        out_specs=(hbm,) * 3,
        scratch_shapes=[pltpu.SemaphoreType.DMA((3,))],
    )(*(pltpu.with_memory_space_constraint(x, pltpu.VMEM) for x in (out, gram, ham)))
    return out.reshape(states.shape), gram, ham


def solution(mesh):
    in_specs = (P("band", "grid", None, None), P("grid", None, None), P(), P(), P())
    out_specs = (P("band", "grid", None, None), P("band", None), P("band", None))
    return jax.shard_map(
        functools.partial(per_device, mesh.shape["band"], mesh.shape["grid"]),
        mesh=mesh, in_specs=in_specs, out_specs=out_specs, check_vma=False,
    )
```

```python
import functools

import jax
import jax.numpy as jnp
from jax import lax
from jax.experimental import pallas as pl
from jax.experimental.pallas import tpu as pltpu
from jax.sharding import PartitionSpec as P

RADIUS = 4
DEGREE = 4
LANES = 128
MESH = pl.DeviceIdType.MESH

stencil_weights = (-205.0 / 72.0, 1.6, -0.2, 8.0 / 315.0, -1.0 / 560.0)
filter_centre = 10.0
filter_half = 6.0


def kernel(
    bands, slabs, planes, rows, cols, atoms, total_points,
    states, potential, index_in, value_in, strength_in,
    out_ref, gram_ref, ham_ref,
    raw, spare_raw, field, spare, pot, index_ref, value_ref, strength_ref, proj, parts_ref, shift_ref, across,
    coef_mine, coef_far, coef_first, back_y, both, prod, band_sum, mine, grid_sum,
    send, recv, local,
):
    half = states.shape[0] // 2
    area = rows * cols
    chunk = 2 * planes
    me_b, me_g = lax.axis_index("band"), lax.axis_index("grid")
    pair, side = me_g // 2, me_g % 2
    other = 1 - side
    last_pair = slabs // 2 - 1
    has_down, has_up = pair > 0, pair < last_pair
    counter = [0]

    def remote(src, dst, out_slot, in_slot, where):
        return pltpu.make_async_remote_copy(
            src_ref=src, dst_ref=dst, send_sem=send.at[out_slot], recv_sem=recv.at[in_slot],
            device_id=where, device_id_type=MESH,
        )

    def slots(count):
        first = counter[0]
        counter[0] += count
        return first

    def rows_at(plane, count):
        return pl.ds(pl.multiple_of(plane * rows, rows), count * rows)

    def group(g):
        return pl.ds(pl.multiple_of(g * half, half), half)

    partner = (me_b, 2 * pair + other)
    up, down = (me_b, me_g + 2), (me_b, me_g - 2)
    up_other, down_other = (me_b, 2 * pair + 2 + other), (me_b, 2 * pair - 2 + other)
    crossing = [
        (lax.rem(me_b + d, bands), 2 * pair + lax.rem(side + e, 2)) for d in range(1, bands) for e in range(2)
    ]
    barrier = pltpu.get_barrier_semaphore()

    def greet(where):
        pl.semaphore_signal(barrier, inc=1, device_id=where, device_id_type=MESH)

    def greet_pair(one, two):
        greet(one)
        greet(two)

    coef_far[...] = jnp.zeros_like(coef_far)
    coef_first[...] = jnp.zeros_like(coef_first)

    if last_pair > DEGREE:
        for d in range(1, slabs):
            greet((me_b, lax.rem(me_g + d, slabs)))
        expected = len(crossing) + slabs - 1
    else:
        greet(partner)
        pl.when(has_up)(lambda: greet_pair(up, up_other))
        pl.when(has_down)(lambda: greet_pair(down, down_other))
        expected = len(crossing) + 1 + 2 * (has_up.astype(jnp.int32) + has_down.astype(jnp.int32))
    for peer in crossing:
        greet(peer)

    own = [
        pltpu.make_async_copy(states.at[group(side)], raw.at[:, rows_at(RADIUS + side * planes, planes)], local.at[0]),
        pltpu.make_async_copy(states.at[group(other)], spare_raw, local.at[1]),
        pltpu.make_async_copy(index_in, index_ref, local.at[2]),
        pltpu.make_async_copy(value_in, value_ref, local.at[3]),
        pltpu.make_async_copy(potential, pot.at[pl.ds(side * planes, planes)], local.at[4]),
        pltpu.make_async_copy(strength_in, strength_ref, local.at[5]),
    ]
    for copy in own:
        copy.start()

    pl.semaphore_wait(barrier, expected)

    first = slots(5)
    toward, can = 2 * side - 1, jnp.where(side == 1, pair < last_pair, pair > 0)
    outer_at, inner_at = side * (planes - RADIUS), other * RADIUS
    fringes = [
        remote(
            states.at[pl.ds(h * half, half), rows_at(outer_at, RADIUS)],
            raw.at[:, rows_at(other * (RADIUS + chunk), RADIUS)],
            first + h, first + other, (me_b, 2 * (pair + toward) + h),
        )
        for h in range(2)
    ]
    swaps = [
        remote(
            states.at[group(other), rows_at(start, count)], raw.at[:, rows_at(RADIUS + side * planes + start, count)],
            first + 2 + n, first + 2 + n, partner,
        )
        for n, (start, count) in enumerate(((outer_at, RADIUS), (inner_at, planes - RADIUS)))
    ]
    pot_swap = remote(potential, pot.at[pl.ds(side * planes, planes)], first + 4, first + 4, partner)

    def start_fringes():
        for copy in fringes:
            copy.start()

    pl.when(can)(start_fringes)
    for copy in swaps:
        copy.start()
    pot_swap.start()

    points = index_ref.shape[1]
    row_iota = lax.broadcasted_iota(jnp.int32, (chunk * rows, points), 0) + pair * (chunk * rows)
    col_iota = lax.broadcasted_iota(jnp.int32, (cols, points), 0)

    def build(a, carry):
        idx = index_ref[pl.ds(a, 1), :]
        row = lax.div(idx, cols)
        here = row_iota == row
        onehot = jnp.where(col_iota == idx - row * cols, 1.0, 0.0).astype(jnp.bfloat16)
        rest = value_ref[pl.ds(a, 1), :]
        parts = []
        for _ in range(3):
            part = rest.astype(jnp.bfloat16).astype(jnp.float32)
            rest = rest - part
            parts.append(jnp.where(here, part, 0.0).astype(jnp.bfloat16))
        proj[a] = lax.dot_general(
            jnp.concatenate(parts, axis=1), jnp.concatenate([onehot] * 3, axis=1), (((1,), (1,)), ((), ())),
            preferred_element_type=jnp.float32,
        )
        return carry

    own[2].wait()
    own[3].wait()
    lax.fori_loop(0, atoms, build, 0, unroll=4)
    pack = 16

    def split(v):
        high = v.astype(jnp.bfloat16)
        return high, (v - high.astype(jnp.float32)).astype(jnp.bfloat16)

    def arrange(p, carry):
        for j in range(0, atoms, pack):
            cubes = [jnp.swapaxes(proj[j + i : j + i + 8, rows_at(p, 1), :], 0, 1) for i in range(0, pack, 8)]
            for y in range(rows):
                high, low = split(jnp.concatenate([cube[y] for cube in cubes], axis=0))
                parts_ref[p, j : j + pack, y * cols : (y + 1) * cols] = high
                parts_ref[p, atoms + j : atoms + j + pack, y * cols : (y + 1) * cols] = low
        return carry

    lax.fori_loop(0, chunk, arrange, 0, unroll=2)

    apart = jnp.abs(
        lax.broadcasted_iota(jnp.int32, (cols, cols), 0) - lax.broadcasted_iota(jnp.int32, (cols, cols), 1)
    )
    band = jnp.zeros((cols, cols), jnp.float32)
    for d in range(1, RADIUS + 1):
        band = jnp.where(apart == d, stencil_weights[d], band)
    band_high, band_low = split(band)
    shift_ref[:cols, :cols] = band_high
    shift_ref[cols:, :cols] = band_high
    shift_ref[:cols, cols:] = band_low
    shift_ref[cols:, cols:] = jnp.zeros((cols, cols), jnp.bfloat16)

    def relayout(src, src_at, dst, dst_at, count):
        def at_plane(n, carry):
            cube = jnp.swapaxes(src[:, rows_at(src_at + n, 1), :], 0, 1)
            for y in range(rows):
                dst[dst_at + n, :, y * cols : (y + 1) * cols] = cube[y]
            return carry

        lax.fori_loop(0, count, at_plane, 0)

    wide = coef_mine.shape[-1]

    def cells(plane):
        return [plane[:, y * cols : (y + 1) * cols] for y in range(rows)]

    def stack(one, two, axis):
        return jnp.concatenate([one.astype(jnp.float32), two.astype(jnp.float32)], axis=axis).astype(jnp.bfloat16)

    def project(src, src_at, proj_at, count):
        total = jnp.zeros((2 * half, 2 * atoms), jnp.float32)
        for n in range(count):
            total = total + lax.dot_general(
                stack(*split(src[src_at + n]), 0), parts_ref[proj_at + n], (((1,), (1,)), ((), ())),
                preferred_element_type=jnp.float32,
            )
        result = total[:half, :atoms] + total[:half, atoms:] + total[half:, :atoms]
        if wide == atoms:
            return result
        return jnp.concatenate([result, jnp.zeros((half, wide - atoms), jnp.float32)], axis=1)

    def sum_across(k):
        rows_all = jnp.concatenate([cell for p in range(chunk) for cell in cells(field[k, RADIUS + p])], axis=0)
        both_parts = lax.dot_general(
            jnp.concatenate(split(rows_all), axis=1), shift_ref[...], (((1,), (0,)), ((), ())),
            preferred_element_type=jnp.float32,
        )
        z = both_parts[:, :cols] + both_parts[:, cols:]
        for p in range(chunk):
            for y in range(rows):
                at = (p * rows + y) * half
                across[p, :, y * cols : (y + 1) * cols] = z[at : at + half]

    def local_part(k, p, a, b, low=chunk, high=chunk):
        src = field.at[k]
        cell = cells(src[p + RADIUS])
        line = cells(across[p])
        ring = [None]
        for d in range(1, RADIUS + 1):
            near = [src[p + RADIUS + s * d] for s, room in ((1, high), (-1, low)) if d <= room]
            ring.append(near[0] + near[1] if len(near) == 2 else near[0] if near else None)
        weight = [-0.5 * a * w for w in stencil_weights]
        result = []
        for y in range(rows):
            v = cell[y]
            t = v * (a * pot[p, y : y + 1, :] + (3.0 * weight[0] + b)) + (-0.5 * a) * line[y]
            for d in range(1, RADIUS + 1):
                terms = [cell[y + s * d] for s in (1, -1) if 0 <= y + s * d < rows]
                if ring[d] is not None:
                    terms.append(ring[d][:, y * cols : (y + 1) * cols])
                if terms:
                    t = t + weight[d] * functools.reduce(jnp.add, terms)
            result.append(t)
        return result

    def store(k, p, tiles):
        for y in range(rows):
            field[k, p + RADIUS, :, y * cols : (y + 1) * cols] = tiles[y]

    def stored(k, p):
        return cells(field[k, p + RADIUS])

    halo_slots, coef_slots = slots(2 * (DEGREE + 1)), slots(2 * (DEGREE + 1))

    def halo_up(k):
        slot = halo_slots + 2 * k
        return remote(field.at[k, chunk : chunk + RADIUS], field.at[k, 0:RADIUS], slot, slot, up)

    def halo_down(k):
        slot = halo_slots + 2 * k + 1
        return remote(
            field.at[k, RADIUS : 2 * RADIUS], field.at[k, chunk + RADIUS : chunk + 2 * RADIUS], slot, slot, down
        )

    def coef_up(k):
        slot = coef_slots + 2 * k
        return remote(coef_mine.at[k], coef_far.at[k, 0], slot, slot, up)

    def coef_down(k):
        slot = coef_slots + 2 * k + 1
        return remote(coef_mine.at[k], coef_far.at[k, 1], slot, slot, down)

    first_slots = slots(5)
    other_mine = coef_mine.at[DEGREE + 1]
    early = [
        (None, remote(other_mine, coef_first.at[0], first_slots, first_slots, partner)),
        (has_up, remote(coef_mine.at[0], coef_first.at[1], first_slots + 1, first_slots + 1, up)),
        (has_up, remote(other_mine, coef_first.at[2], first_slots + 2, first_slots + 2, up_other)),
        (has_down, remote(coef_mine.at[0], coef_first.at[3], first_slots + 3, first_slots + 3, down)),
        (has_down, remote(other_mine, coef_first.at[4], first_slots + 4, first_slots + 4, down_other)),
    ]

    own[1].wait()
    relayout(spare_raw, 0, spare, 0, planes)
    coef_mine[DEGREE + 1] = project(spare, 0, side * planes, planes)
    own[0].wait()
    relayout(raw, RADIUS + side * planes, field.at[0], RADIUS + side * planes, planes)
    coef_mine[0] = project(field.at[0], RADIUS + side * planes, side * planes, planes)
    for ready, copy in early:
        if ready is None:
            copy.start()
        else:
            pl.when(ready)(copy.start)

    def spread_of(total):
        high, low = split(total[:, :atoms] * strength_ref[...])
        return stack(stack(high, high, 1), stack(low, jnp.zeros_like(low), 1), 0)

    def add_nonlocal(k, spread, first_plane, count):
        for p in range(first_plane, first_plane + count):
            both_parts = lax.dot_general(
                spread, parts_ref[p], (((1,), (0,)), ((), ())), preferred_element_type=jnp.float32
            )
            field[k, p + RADIUS] = field[k, p + RADIUS] + (both_parts[:half] + both_parts[half:])

    own[4].wait()
    own[5].wait()
    swaps[0].wait_recv()
    relayout(raw, RADIUS + other * (chunk - RADIUS), field.at[0], RADIUS + other * (chunk - RADIUS), RADIUS)
    swaps[1].wait_recv()
    relayout(
        raw, 2 * RADIUS + other * (planes - RADIUS), field.at[0], 2 * RADIUS + other * (planes - RADIUS),
        planes - RADIUS,
    )
    pot_swap.wait_recv()
    early[0][1].wait_recv()

    def wait_below():
        remote(
            states.at[pl.ds(0, half), rows_at(0, RADIUS)], raw.at[:, rows_at(0, RADIUS)], first, first, partner
        ).wait_recv()
        early[1][1].wait_recv()
        early[2][1].wait_recv()
        relayout(raw, 0, field.at[0], 0, RADIUS)

    def wait_above():
        remote(
            states.at[pl.ds(0, half), rows_at(0, RADIUS)], raw.at[:, rows_at(0, RADIUS)], first, first + 1, partner
        ).wait_recv()
        early[3][1].wait_recv()
        early[4][1].wait_recv()
        relayout(raw, RADIUS + chunk, field.at[0], RADIUS + chunk, RADIUS)

    def clear(at):
        def go():
            field[0, at : at + RADIUS] = jnp.zeros((RADIUS, half, area), jnp.float32)

        return go

    pl.when(has_down)(wait_below)
    pl.when(has_up)(wait_above)
    pl.when(jnp.logical_not(has_down))(clear(0))
    pl.when(jnp.logical_not(has_up))(clear(RADIUS + chunk))
    for k in range(1, DEGREE + 1):
        pl.when(jnp.logical_not(has_down))(
            functools.partial(field.__setitem__, (k, slice(0, RADIUS)), jnp.zeros((RADIUS, half, area), jnp.float32))
        )
        pl.when(jnp.logical_not(has_up))(
            functools.partial(
                field.__setitem__, (k, slice(RADIUS + chunk, 2 * RADIUS + chunk)),
                jnp.zeros((RADIUS, half, area), jnp.float32),
            )
        )

    scale0 = 1.0 / filter_half
    total = coef_mine[0]
    for n in range(5):
        total = total + coef_first[n]
    spread0 = spread_of(total * scale0)
    sum_across(0)

    def whole(p, carry):
        store(1, p, local_part(0, p, scale0, -filter_centre * scale0))
        return carry

    lax.fori_loop(0, RADIUS, whole, 0)
    add_nonlocal(1, spread0, 0, RADIUS)
    pl.when(has_down)(halo_down(1).start)
    lax.fori_loop(chunk - RADIUS, chunk, whole, 0)
    add_nonlocal(1, spread0, chunk - RADIUS, RADIUS)
    pl.when(has_up)(halo_up(1).start)
    lax.fori_loop(RADIUS, chunk - RADIUS, whole, 0)
    add_nonlocal(1, spread0, RADIUS, chunk - 2 * RADIUS)

    def apply(k, final):
        scale = 1.0 if final else 2.0 / filter_half
        shift = 0.0 if final else -filter_centre * scale
        coef_mine[k] = project(field.at[k], RADIUS, 0, chunk)
        pl.when(has_up)(coef_up(k).start)
        pl.when(has_down)(coef_down(k).start)

        sum_across(k)

        def with_last(p, tiles):
            if final:
                return tiles
            old = cells(field[k - 1, p + RADIUS])
            return [tiles[y] - old[y] for y in range(rows)]

        def inner(p, carry):
            store(k + 1, p, with_last(p, local_part(k, p, scale, shift)))
            return carry

        for n in range(RADIUS):
            for p, low, high in ((n, n, chunk), (chunk - 1 - n, chunk, n)):
                store(k + 1, p, with_last(p, local_part(k, p, scale, shift, low, high)))
        lax.fori_loop(RADIUS, chunk - RADIUS, inner, 0)

        pl.when(has_down)(coef_up(k).wait_recv)
        pl.when(has_up)(coef_down(k).wait_recv)
        spread = spread_of((coef_mine[k] + coef_far[k, 0] + coef_far[k, 1]) * scale)

        def add_halo(p, planes_in):
            tiles = stored(k + 1, p)
            for w, plane in planes_in:
                far = cells(field[k, plane])
                tiles = [t + (-0.5 * scale * w) * far[y] for y, t in enumerate(tiles)]
            store(k + 1, p, tiles)

        def lower():
            add_nonlocal(k + 1, spread, 0, RADIUS)
            pl.when(has_down)(halo_up(k).wait_recv)
            for p in range(RADIUS):
                add_halo(p, [(stencil_weights[d], RADIUS + p - d) for d in range(p + 1, RADIUS + 1)])

        def upper():
            add_nonlocal(k + 1, spread, chunk - RADIUS, RADIUS)
            pl.when(has_up)(halo_down(k).wait_recv)
            for n in range(RADIUS):
                p = chunk - 1 - n
                add_halo(p, [(stencil_weights[d], RADIUS + p + d) for d in range(n + 1, RADIUS + 1)])

        def middle():
            add_nonlocal(k + 1, spread, RADIUS, chunk - 2 * RADIUS)

        return lower, middle, upper

    def step(k, carry):
        lower, middle, upper = apply(k, False)
        lower()
        pl.when(has_down)(halo_down(k + 1).start)
        upper()
        pl.when(has_up)(halo_up(k + 1).start)
        middle()
        return carry

    lax.fori_loop(1, DEGREE, step, 0)

    part = planes // bands
    shares = 2 * bands
    y_out, y_in, h_out, h_in = slots(shares), slots(shares), slots(shares), slots(shares)
    mine_at = me_b * 2 + side

    def share(which, q):
        src = field.at[DEGREE + which, RADIUS + q * part : RADIUS + (q + 1) * part]
        dst = both.at[which, :, group(mine_at)]
        is_mine = jnp.logical_and(me_b == q % bands, side == q // bands)
        away = remote(
            src, dst, (y_out, h_out)[which] + q, (y_in, h_in)[which] + mine_at, (q % bands, 2 * pair + q // bands)
        )
        return is_mine, away, pltpu.make_async_copy(src, dst, local.at[which])

    def send_share(which, q):
        is_mine, away, keep = share(which, q)
        pl.when(is_mine)(keep.start)
        pl.when(jnp.logical_not(is_mine))(away.start)

    def take_shares(which):
        for q in range(shares):
            sender = q
            is_mine = jnp.logical_and(me_b == sender // 2, side == sender % 2)
            src = field.at[DEGREE + which, RADIUS : RADIUS + part]
            dst = both.at[which, :, pl.ds(sender * half, half)]
            come = remote(src, dst, y_out, (y_in, h_in)[which] + sender, partner)
            pl.when(is_mine)(pltpu.make_async_copy(src, dst, local.at[which]).wait)
            pl.when(jnp.logical_not(is_mine))(come.wait_recv)

    def sent_shares(which):
        for q in range(shares):
            is_mine, away, keep = share(which, q)
            pl.when(jnp.logical_not(is_mine))(away.wait_send)

    for q in range(shares):
        send_share(0, q)
    lower, middle, upper = apply(DEGREE, True)
    inside = [q for q in range(shares) if q * part >= RADIUS and (q + 1) * part <= chunk - RADIUS]
    middle()
    for q in inside:
        send_share(1, q)
    lower()
    for q in range(shares // 2):
        if q not in inside:
            send_share(1, q)
    upper()
    for q in range(shares // 2, shares):
        if q not in inside:
            send_share(1, q)

    back_slot = slots(1)
    back = remote(
        field.at[DEGREE, pl.ds(RADIUS + other * planes, planes)], back_y, back_slot, back_slot, partner
    )
    back.start()

    def inner_rows(left, right):
        return lax.dot_general(
            left, right, (((1,), (1,)), ((), ())),
            precision=lax.Precision.HIGH, preferred_element_type=jnp.float32,
        )

    states_all = bands * 2 * half
    take_shares(0)
    total = inner_rows(both[0, 0], both[0, 0])
    for i in range(1, part):
        total = total + inner_rows(both[0, i], both[0, i])
    prod[:, :states_all] = total
    take_shares(1)
    total = inner_rows(both[1, 0], both[0, 0])
    for i in range(1, part):
        total = total + inner_rows(both[1, i], both[0, i])
    prod[:, states_all:] = total

    rows_of = 2 * half
    r_slot, g_slot = slots(bands), slots(slabs)
    band_copies = []
    for d in range(1, bands):
        to_b = lax.rem(me_b + d, bands)
        copy = remote(
            prod.at[pl.ds(pl.multiple_of(to_b * rows_of, rows_of), rows_of)], band_sum.at[d],
            r_slot + d, r_slot + d, (to_b, me_g),
        )
        copy.start()
        band_copies.append(copy)
    total = prod[pl.ds(pl.multiple_of(me_b * rows_of, rows_of), rows_of), :]
    for copy in band_copies:
        copy.wait_recv()
    for d in range(1, bands):
        total = total + band_sum[d]
    mine[...] = total
    grid_copies = []
    for d in range(1, slabs):
        copy = remote(mine, grid_sum.at[d], g_slot + d, g_slot + d, (me_b, lax.rem(me_g + d, slabs)))
        copy.start()
        grid_copies.append(copy)

    def put_out(src, src_at, g):
        def at_plane(p, carry):
            cube = jnp.stack(cells(src[src_at + p]))
            out_ref[group(g), rows_at(p, 1), :] = jnp.swapaxes(cube, 0, 1)
            return carry

        lax.fori_loop(0, planes, at_plane, 0)

    put_out(field.at[DEGREE], RADIUS + side * planes, side)
    back.wait_recv()
    put_out(back_y, 0, other)
    for copy in swaps + [pot_swap, early[0][1], back] + band_copies:
        copy.wait_send()
    for copy in fringes:
        pl.when(can)(copy.wait_send)
    for ready, copy in early[1:]:
        pl.when(ready)(copy.wait_send)
    for k in range(1, DEGREE + 1):
        for ready, copy in (
            (has_up, halo_up(k)), (has_down, halo_down(k)), (has_up, coef_up(k)), (has_down, coef_down(k))
        ):
            pl.when(ready)(copy.wait_send)
    sent_shares(0)
    sent_shares(1)
    for copy in grid_copies:
        copy.wait_recv()
    for d in range(1, slabs):
        total = total + grid_sum[d]
    total = total / total_points
    gram_ref[...] = total[:, :states_all]
    ham_ref[...] = total[:, states_all:]

    for copy in grid_copies:
        copy.wait_send()


def per_device(bands, slabs, states, potential, proj_index, proj_value, proj_strength):
    state_count, planes, rows, cols = states.shape
    area = rows * cols
    points = planes * area
    atoms, support = proj_index.shape
    half = state_count // 2
    chunk = 2 * planes
    wide = -(-atoms // LANES) * LANES
    all_states = bands * state_count
    strength = proj_strength.reshape(1, atoms)
    slots = 5 + 4 * (DEGREE + 1) + 5 + 8 * bands + 1 + bands + slabs
    vmem, hbm = pl.BlockSpec(memory_space=pltpu.VMEM), pl.BlockSpec(memory_space=pltpu.HBM)
    f32 = jnp.float32
    out, gram, ham = pl.pallas_call(
        functools.partial(
            kernel, bands, slabs, planes, rows, cols, atoms, float(points * slabs)
        ),
        out_shape=(
            jax.ShapeDtypeStruct((state_count, planes * rows, cols), f32),
            jax.ShapeDtypeStruct((state_count, all_states), f32),
            jax.ShapeDtypeStruct((state_count, all_states), f32),
        ),
        in_specs=[hbm, hbm, hbm, hbm, hbm],
        out_specs=(vmem, vmem, vmem),
        scratch_shapes=[
            pltpu.VMEM((half, (chunk + 2 * RADIUS) * rows, cols), f32),
            pltpu.VMEM((half, planes * rows, cols), f32),
            pltpu.VMEM((DEGREE + 2, chunk + 2 * RADIUS, half, area), f32),
            pltpu.VMEM((planes, half, area), f32),
            pltpu.VMEM((chunk, rows, cols), f32),
            pltpu.VMEM((atoms, support), jnp.int32),
            pltpu.VMEM((atoms, support), f32),
            pltpu.VMEM((1, atoms), f32),
            pltpu.VMEM((atoms, chunk * rows, cols), f32),
            pltpu.VMEM((chunk, 2 * atoms, area), jnp.bfloat16),
            pltpu.VMEM((2 * cols, 2 * cols), jnp.bfloat16),
            pltpu.VMEM((chunk, half, area), f32),
            pltpu.VMEM((DEGREE + 2, half, wide), f32),
            pltpu.VMEM((DEGREE + 1, 2, half, wide), f32),
            pltpu.VMEM((5, half, wide), f32),
            pltpu.VMEM((planes, half, area), f32),
            pltpu.VMEM((2, planes // bands, all_states, area), f32),
            pltpu.VMEM((all_states, 2 * all_states), f32),
            pltpu.VMEM((bands, state_count, 2 * all_states), f32),
            pltpu.VMEM((state_count, 2 * all_states), f32),
            pltpu.VMEM((slabs, state_count, 2 * all_states), f32),
            pltpu.SemaphoreType.DMA((slots,)),
            pltpu.SemaphoreType.DMA((slots,)),
            pltpu.SemaphoreType.DMA((6,)),
        ],
        compiler_params=pltpu.CompilerParams(
            collective_id=0, has_side_effects=True, vmem_limit_bytes=48 * 1024 * 1024
        ),
    )(*(pltpu.with_memory_space_constraint(x, pltpu.HBM) for x in (states.reshape(state_count, planes * rows, cols), potential, proj_index, proj_value, strength)))

    def place(*refs):
        moves = [pltpu.make_async_copy(refs[n], refs[3 + n], refs[6].at[n]) for n in range(3)]
        for move in moves:
            move.start()
        for move in moves:
            move.wait()

    out, gram, ham = pl.pallas_call(
        place,
        out_shape=tuple(jax.ShapeDtypeStruct(x.shape, f32) for x in (out, gram, ham)),
        in_specs=[vmem] * 3,
        out_specs=(hbm,) * 3,
        scratch_shapes=[pltpu.SemaphoreType.DMA((3,))],
    )(*(pltpu.with_memory_space_constraint(x, pltpu.VMEM) for x in (out, gram, ham)))
    return out.reshape(states.shape), gram, ham


def solution(mesh):
    in_specs = (P("band", "grid", None, None), P("grid", None, None), P(), P(), P())
    out_specs = (P("band", "grid", None, None), P("band", None), P("band", None))
    return jax.shard_map(
        functools.partial(per_device, mesh.shape["band"], mesh.shape["grid"]),
        mesh=mesh, in_specs=in_specs, out_specs=out_specs, check_vma=False,
    )
```

```python
import functools

import jax
import jax.numpy as jnp
from jax import lax
from jax.experimental import pallas as pl
from jax.experimental.pallas import tpu as pltpu
from jax.sharding import PartitionSpec as P

RADIUS = 4
DEGREE = 4
LANES = 128
MESH = pl.DeviceIdType.MESH

stencil_weights = (-205.0 / 72.0, 1.6, -0.2, 8.0 / 315.0, -1.0 / 560.0)
filter_centre = 10.0
filter_half = 6.0


def kernel(
    bands, slabs, planes, rows, cols, atoms, total_points,
    states, potential, index_in, value_in, strength_in,
    out_ref, gram_ref, ham_ref,
    raw, spare_raw, field, spare, pot, index_ref, value_ref, strength_ref, proj, parts_ref, shift_ref, across,
    coef_mine, coef_far, coef_first, back_y, both, prod, band_sum, mine, grid_sum,
    send, recv, local,
):
    half = states.shape[0] // 2
    area = rows * cols
    chunk = 2 * planes
    me_b, me_g = lax.axis_index("band"), lax.axis_index("grid")
    pair, side = me_g // 2, me_g % 2
    other = 1 - side
    last_pair = slabs // 2 - 1
    has_down, has_up = pair > 0, pair < last_pair
    counter = [0]

    def remote(src, dst, out_slot, in_slot, where):
        return pltpu.make_async_remote_copy(
            src_ref=src, dst_ref=dst, send_sem=send.at[out_slot], recv_sem=recv.at[in_slot],
            device_id=where, device_id_type=MESH,
        )

    def slots(count):
        first = counter[0]
        counter[0] += count
        return first

    def rows_at(plane, count):
        return pl.ds(pl.multiple_of(plane * rows, rows), count * rows)

    def group(g):
        return pl.ds(pl.multiple_of(g * half, half), half)

    partner = (me_b, 2 * pair + other)
    up, down = (me_b, me_g + 2), (me_b, me_g - 2)
    up_other, down_other = (me_b, 2 * pair + 2 + other), (me_b, 2 * pair - 2 + other)
    crossing = [
        (lax.rem(me_b + d, bands), 2 * pair + lax.rem(side + e, 2)) for d in range(1, bands) for e in range(2)
    ]
    barrier = pltpu.get_barrier_semaphore()

    def greet(where):
        pl.semaphore_signal(barrier, inc=1, device_id=where, device_id_type=MESH)

    def greet_pair(one, two):
        greet(one)
        greet(two)

    coef_far[...] = jnp.zeros_like(coef_far)
    coef_first[...] = jnp.zeros_like(coef_first)

    if last_pair > DEGREE:
        for d in range(1, slabs):
            greet((me_b, lax.rem(me_g + d, slabs)))
        expected = len(crossing) + slabs - 1
    else:
        greet(partner)
        pl.when(has_up)(lambda: greet_pair(up, up_other))
        pl.when(has_down)(lambda: greet_pair(down, down_other))
        expected = len(crossing) + 1 + 2 * (has_up.astype(jnp.int32) + has_down.astype(jnp.int32))
    for peer in crossing:
        greet(peer)

    own = [
        pltpu.make_async_copy(states.at[group(side)], raw.at[:, rows_at(RADIUS + side * planes, planes)], local.at[0]),
        pltpu.make_async_copy(states.at[group(other)], spare_raw, local.at[1]),
        pltpu.make_async_copy(index_in, index_ref, local.at[2]),
        pltpu.make_async_copy(value_in, value_ref, local.at[3]),
        pltpu.make_async_copy(potential, pot.at[pl.ds(side * planes, planes)], local.at[4]),
        pltpu.make_async_copy(strength_in, strength_ref, local.at[5]),
    ]
    for copy in own:
        copy.start()

    pl.semaphore_wait(barrier, expected)

    first = slots(5)
    toward, can = 2 * side - 1, jnp.where(side == 1, pair < last_pair, pair > 0)
    outer_at, inner_at = side * (planes - RADIUS), other * RADIUS
    fringes = [
        remote(
            states.at[pl.ds(h * half, half), rows_at(outer_at, RADIUS)],
            raw.at[:, rows_at(other * (RADIUS + chunk), RADIUS)],
            first + h, first + other, (me_b, 2 * (pair + toward) + h),
        )
        for h in range(2)
    ]
    swaps = [
        remote(
            states.at[group(other), rows_at(start, count)], raw.at[:, rows_at(RADIUS + side * planes + start, count)],
            first + 2 + n, first + 2 + n, partner,
        )
        for n, (start, count) in enumerate(((outer_at, RADIUS), (inner_at, planes - RADIUS)))
    ]
    pot_swap = remote(potential, pot.at[pl.ds(side * planes, planes)], first + 4, first + 4, partner)

    def start_fringes():
        for copy in fringes:
            copy.start()

    pl.when(can)(start_fringes)
    for copy in swaps:
        copy.start()
    pot_swap.start()

    points = index_ref.shape[1]
    row_iota = lax.broadcasted_iota(jnp.int32, (chunk * rows, points), 0) + pair * (chunk * rows)
    col_iota = lax.broadcasted_iota(jnp.int32, (cols, points), 0)

    def build(a, carry):
        idx = index_ref[pl.ds(a, 1), :]
        row = lax.div(idx, cols)
        here = row_iota == row
        onehot = jnp.where(col_iota == idx - row * cols, 1.0, 0.0).astype(jnp.bfloat16)
        rest = value_ref[pl.ds(a, 1), :]
        parts = []
        for _ in range(3):
            part = rest.astype(jnp.bfloat16).astype(jnp.float32)
            rest = rest - part
            parts.append(jnp.where(here, part, 0.0).astype(jnp.bfloat16))
        proj[a] = lax.dot_general(
            jnp.concatenate(parts, axis=1), jnp.concatenate([onehot] * 3, axis=1), (((1,), (1,)), ((), ())),
            preferred_element_type=jnp.float32,
        )
        return carry

    own[2].wait()
    own[3].wait()
    lax.fori_loop(0, atoms, build, 0, unroll=4)
    pack = 16

    def split(v):
        high = v.astype(jnp.bfloat16)
        return high, (v - high.astype(jnp.float32)).astype(jnp.bfloat16)

    def arrange(p, carry):
        for j in range(0, atoms, pack):
            cubes = [jnp.swapaxes(proj[j + i : j + i + 8, rows_at(p, 1), :], 0, 1) for i in range(0, pack, 8)]
            for y in range(rows):
                high, low = split(jnp.concatenate([cube[y] for cube in cubes], axis=0))
                parts_ref[p, j : j + pack, y * cols : (y + 1) * cols] = high
                parts_ref[p, atoms + j : atoms + j + pack, y * cols : (y + 1) * cols] = low
        return carry

    lax.fori_loop(0, chunk, arrange, 0, unroll=2)

    apart = jnp.abs(
        lax.broadcasted_iota(jnp.int32, (cols, cols), 0) - lax.broadcasted_iota(jnp.int32, (cols, cols), 1)
    )
    band = jnp.zeros((cols, cols), jnp.float32)
    for d in range(1, RADIUS + 1):
        band = jnp.where(apart == d, stencil_weights[d], band)
    band_high, band_low = split(band)
    shift_ref[:cols, :cols] = band_high
    shift_ref[cols:, :cols] = band_high
    shift_ref[:cols, cols:] = band_low
    shift_ref[cols:, cols:] = jnp.zeros((cols, cols), jnp.bfloat16)

    def relayout(src, src_at, dst, dst_at, count):
        def at_plane(n, carry):
            cube = jnp.swapaxes(src[:, rows_at(src_at + n, 1), :], 0, 1)
            for y in range(rows):
                dst[dst_at + n, :, y * cols : (y + 1) * cols] = cube[y]
            return carry

        lax.fori_loop(0, count, at_plane, 0)

    wide = coef_mine.shape[-1]

    def cells(plane):
        return [plane[:, y * cols : (y + 1) * cols] for y in range(rows)]

    def stack(one, two, axis):
        return jnp.concatenate([one.astype(jnp.float32), two.astype(jnp.float32)], axis=axis).astype(jnp.bfloat16)

    def project(src, src_at, proj_at, count):
        total = jnp.zeros((2 * half, 2 * atoms), jnp.float32)
        for n in range(count):
            total = total + lax.dot_general(
                stack(*split(src[src_at + n]), 0), parts_ref[proj_at + n], (((1,), (1,)), ((), ())),
                preferred_element_type=jnp.float32,
            )
        result = total[:half, :atoms] + total[:half, atoms:] + total[half:, :atoms]
        if wide == atoms:
            return result
        return jnp.concatenate([result, jnp.zeros((half, wide - atoms), jnp.float32)], axis=1)

    def sum_across(k):
        rows_all = jnp.concatenate([cell for p in range(chunk) for cell in cells(field[k, RADIUS + p])], axis=0)
        both_parts = lax.dot_general(
            jnp.concatenate(split(rows_all), axis=1), shift_ref[...], (((1,), (0,)), ((), ())),
            preferred_element_type=jnp.float32,
        )
        z = both_parts[:, :cols] + both_parts[:, cols:]
        for p in range(chunk):
            for y in range(rows):
                at = (p * rows + y) * half
                across[p, :, y * cols : (y + 1) * cols] = z[at : at + half]

    def local_part(k, p, a, b, low=chunk, high=chunk):
        src = field.at[k]
        cell = cells(src[p + RADIUS])
        line = cells(across[p])
        ring = [None]
        for d in range(1, RADIUS + 1):
            near = [src[p + RADIUS + s * d] for s, room in ((1, high), (-1, low)) if d <= room]
            ring.append(near[0] + near[1] if len(near) == 2 else near[0] if near else None)
        weight = [-0.5 * a * w for w in stencil_weights]
        result = []
        for y in range(rows):
            v = cell[y]
            t = v * (a * pot[p, y : y + 1, :] + (3.0 * weight[0] + b)) + (-0.5 * a) * line[y]
            for d in range(1, RADIUS + 1):
                terms = [cell[y + s * d] for s in (1, -1) if 0 <= y + s * d < rows]
                if ring[d] is not None:
                    terms.append(ring[d][:, y * cols : (y + 1) * cols])
                if terms:
                    t = t + weight[d] * functools.reduce(jnp.add, terms)
            result.append(t)
        return result

    def store(k, p, tiles):
        for y in range(rows):
            field[k, p + RADIUS, :, y * cols : (y + 1) * cols] = tiles[y]

    def stored(k, p):
        return cells(field[k, p + RADIUS])

    halo_slots, coef_slots = slots(2 * (DEGREE + 1)), slots(2 * (DEGREE + 1))

    def halo_up(k):
        slot = halo_slots + 2 * k
        return remote(field.at[k, chunk : chunk + RADIUS], field.at[k, 0:RADIUS], slot, slot, up)

    def halo_down(k):
        slot = halo_slots + 2 * k + 1
        return remote(
            field.at[k, RADIUS : 2 * RADIUS], field.at[k, chunk + RADIUS : chunk + 2 * RADIUS], slot, slot, down
        )

    def coef_up(k):
        slot = coef_slots + 2 * k
        return remote(coef_mine.at[k], coef_far.at[k, 0], slot, slot, up)

    def coef_down(k):
        slot = coef_slots + 2 * k + 1
        return remote(coef_mine.at[k], coef_far.at[k, 1], slot, slot, down)

    first_slots = slots(5)
    other_mine = coef_mine.at[DEGREE + 1]
    early = [
        (None, remote(other_mine, coef_first.at[0], first_slots, first_slots, partner)),
        (has_up, remote(coef_mine.at[0], coef_first.at[1], first_slots + 1, first_slots + 1, up)),
        (has_up, remote(other_mine, coef_first.at[2], first_slots + 2, first_slots + 2, up_other)),
        (has_down, remote(coef_mine.at[0], coef_first.at[3], first_slots + 3, first_slots + 3, down)),
        (has_down, remote(other_mine, coef_first.at[4], first_slots + 4, first_slots + 4, down_other)),
    ]

    own[1].wait()
    relayout(spare_raw, 0, spare, 0, planes)
    coef_mine[DEGREE + 1] = project(spare, 0, side * planes, planes)
    own[0].wait()
    relayout(raw, RADIUS + side * planes, field.at[0], RADIUS + side * planes, planes)
    coef_mine[0] = project(field.at[0], RADIUS + side * planes, side * planes, planes)
    for ready, copy in early:
        if ready is None:
            copy.start()
        else:
            pl.when(ready)(copy.start)

    def spread_of(total):
        high, low = split(total[:, :atoms] * strength_ref[...])
        return stack(stack(high, high, 1), stack(low, jnp.zeros_like(low), 1), 0)

    def add_nonlocal(k, spread, first_plane, count):
        for p in range(first_plane, first_plane + count):
            both_parts = lax.dot_general(
                spread, parts_ref[p], (((1,), (0,)), ((), ())), preferred_element_type=jnp.float32
            )
            field[k, p + RADIUS] = field[k, p + RADIUS] + (both_parts[:half] + both_parts[half:])

    own[4].wait()
    own[5].wait()
    swaps[0].wait_recv()
    relayout(raw, RADIUS + other * (chunk - RADIUS), field.at[0], RADIUS + other * (chunk - RADIUS), RADIUS)
    swaps[1].wait_recv()
    relayout(
        raw, 2 * RADIUS + other * (planes - RADIUS), field.at[0], 2 * RADIUS + other * (planes - RADIUS),
        planes - RADIUS,
    )
    pot_swap.wait_recv()
    early[0][1].wait_recv()

    def wait_below():
        remote(
            states.at[pl.ds(0, half), rows_at(0, RADIUS)], raw.at[:, rows_at(0, RADIUS)], first, first, partner
        ).wait_recv()
        early[1][1].wait_recv()
        early[2][1].wait_recv()
        relayout(raw, 0, field.at[0], 0, RADIUS)

    def wait_above():
        remote(
            states.at[pl.ds(0, half), rows_at(0, RADIUS)], raw.at[:, rows_at(0, RADIUS)], first, first + 1, partner
        ).wait_recv()
        early[3][1].wait_recv()
        early[4][1].wait_recv()
        relayout(raw, RADIUS + chunk, field.at[0], RADIUS + chunk, RADIUS)

    def clear(at):
        def go():
            field[0, at : at + RADIUS] = jnp.zeros((RADIUS, half, area), jnp.float32)

        return go

    pl.when(has_down)(wait_below)
    pl.when(has_up)(wait_above)
    pl.when(jnp.logical_not(has_down))(clear(0))
    pl.when(jnp.logical_not(has_up))(clear(RADIUS + chunk))
    for k in range(1, DEGREE + 1):
        pl.when(jnp.logical_not(has_down))(
            functools.partial(field.__setitem__, (k, slice(0, RADIUS)), jnp.zeros((RADIUS, half, area), jnp.float32))
        )
        pl.when(jnp.logical_not(has_up))(
            functools.partial(
                field.__setitem__, (k, slice(RADIUS + chunk, 2 * RADIUS + chunk)),
                jnp.zeros((RADIUS, half, area), jnp.float32),
            )
        )

    scale0 = 1.0 / filter_half
    total = coef_mine[0]
    for n in range(5):
        total = total + coef_first[n]
    spread0 = spread_of(total * scale0)
    sum_across(0)

    def whole(p, carry):
        store(1, p, local_part(0, p, scale0, -filter_centre * scale0))
        return carry

    lax.fori_loop(0, RADIUS, whole, 0)
    add_nonlocal(1, spread0, 0, RADIUS)
    pl.when(has_down)(halo_down(1).start)
    lax.fori_loop(chunk - RADIUS, chunk, whole, 0)
    add_nonlocal(1, spread0, chunk - RADIUS, RADIUS)
    pl.when(has_up)(halo_up(1).start)
    lax.fori_loop(RADIUS, chunk - RADIUS, whole, 0)
    add_nonlocal(1, spread0, RADIUS, chunk - 2 * RADIUS)

    def apply(k, final):
        scale = 1.0 if final else 2.0 / filter_half
        shift = 0.0 if final else -filter_centre * scale
        coef_mine[k] = project(field.at[k], RADIUS, 0, chunk)
        pl.when(has_up)(coef_up(k).start)
        pl.when(has_down)(coef_down(k).start)

        sum_across(k)

        def with_last(p, tiles):
            if final:
                return tiles
            old = cells(field[k - 1, p + RADIUS])
            return [tiles[y] - old[y] for y in range(rows)]

        def inner(p, carry):
            store(k + 1, p, with_last(p, local_part(k, p, scale, shift)))
            return carry

        for n in range(RADIUS):
            for p, low, high in ((n, n, chunk), (chunk - 1 - n, chunk, n)):
                store(k + 1, p, with_last(p, local_part(k, p, scale, shift, low, high)))
        lax.fori_loop(RADIUS, chunk - RADIUS, inner, 0)

        pl.when(has_down)(coef_up(k).wait_recv)
        pl.when(has_up)(coef_down(k).wait_recv)
        spread = spread_of((coef_mine[k] + coef_far[k, 0] + coef_far[k, 1]) * scale)

        def add_halo(p, planes_in):
            tiles = stored(k + 1, p)
            for w, plane in planes_in:
                far = cells(field[k, plane])
                tiles = [t + (-0.5 * scale * w) * far[y] for y, t in enumerate(tiles)]
            store(k + 1, p, tiles)

        def lower():
            add_nonlocal(k + 1, spread, 0, RADIUS)
            pl.when(has_down)(halo_up(k).wait_recv)
            for p in range(RADIUS):
                add_halo(p, [(stencil_weights[d], RADIUS + p - d) for d in range(p + 1, RADIUS + 1)])

        def upper():
            add_nonlocal(k + 1, spread, chunk - RADIUS, RADIUS)
            pl.when(has_up)(halo_down(k).wait_recv)
            for n in range(RADIUS):
                p = chunk - 1 - n
                add_halo(p, [(stencil_weights[d], RADIUS + p + d) for d in range(n + 1, RADIUS + 1)])

        def middle():
            add_nonlocal(k + 1, spread, RADIUS, chunk - 2 * RADIUS)

        return lower, middle, upper

    def step(k, carry):
        lower, middle, upper = apply(k, False)
        lower()
        pl.when(has_down)(halo_down(k + 1).start)
        upper()
        pl.when(has_up)(halo_up(k + 1).start)
        middle()
        return carry

    lax.fori_loop(1, DEGREE, step, 0)

    part = planes // bands
    shares = 2 * bands
    y_out, y_in, h_out, h_in = slots(shares), slots(shares), slots(shares), slots(shares)
    mine_at = me_b * 2 + side

    def share(which, q):
        src = field.at[DEGREE + which, RADIUS + q * part : RADIUS + (q + 1) * part]
        dst = both.at[which, :, group(mine_at)]
        is_mine = jnp.logical_and(me_b == q % bands, side == q // bands)
        away = remote(
            src, dst, (y_out, h_out)[which] + q, (y_in, h_in)[which] + mine_at, (q % bands, 2 * pair + q // bands)
        )
        return is_mine, away, pltpu.make_async_copy(src, dst, local.at[which])

    def send_share(which, q):
        is_mine, away, keep = share(which, q)
        pl.when(is_mine)(keep.start)
        pl.when(jnp.logical_not(is_mine))(away.start)

    def take_shares(which):
        for q in range(shares):
            sender = q
            is_mine = jnp.logical_and(me_b == sender // 2, side == sender % 2)
            src = field.at[DEGREE + which, RADIUS : RADIUS + part]
            dst = both.at[which, :, pl.ds(sender * half, half)]
            come = remote(src, dst, y_out, (y_in, h_in)[which] + sender, partner)
            pl.when(is_mine)(pltpu.make_async_copy(src, dst, local.at[which]).wait)
            pl.when(jnp.logical_not(is_mine))(come.wait_recv)

    def sent_shares(which):
        for q in range(shares):
            is_mine, away, keep = share(which, q)
            pl.when(jnp.logical_not(is_mine))(away.wait_send)

    for q in range(shares):
        send_share(0, q)
    lower, middle, upper = apply(DEGREE, True)
    inside = [q for q in range(shares) if q * part >= RADIUS and (q + 1) * part <= chunk - RADIUS]
    middle()
    for q in inside:
        send_share(1, q)
    lower()
    for q in range(shares // 2):
        if q not in inside:
            send_share(1, q)
    upper()
    for q in range(shares // 2, shares):
        if q not in inside:
            send_share(1, q)

    back_slot = slots(bands)
    my_planes = back_y.at[pl.ds(me_b * part, part)]

    def gathered_of(b):
        return both.at[0, :, group(b * 2 + other)]

    backs = [
        remote(
            gathered_of(lax.rem(me_b + d, bands)), my_planes, back_slot + d, back_slot + d,
            (lax.rem(me_b + d, bands), me_g),
        )
        for d in range(1, bands)
    ]
    backs.append(pltpu.make_async_copy(gathered_of(me_b), my_planes, local.at[2]))

    def start_backs():
        for copy in backs:
            copy.start()

    def inner_rows(left, right):
        return lax.dot_general(
            left, right, (((1,), (1,)), ((), ())),
            precision=lax.Precision.HIGH, preferred_element_type=jnp.float32,
        )

    states_all = bands * 2 * half
    take_shares(0)
    total = inner_rows(both[0, 0], both[0, 0])
    for i in range(1, part):
        total = total + inner_rows(both[0, i], both[0, i])
    prod[:, :states_all] = total
    take_shares(1)
    total = inner_rows(both[1, 0], both[0, 0])
    for i in range(1, part):
        total = total + inner_rows(both[1, i], both[0, i])
    prod[:, states_all:] = total

    rows_of = 2 * half
    r_slot, g_slot = slots(bands), slots(slabs)
    band_copies = []
    for d in range(1, bands):
        to_b = lax.rem(me_b + d, bands)
        copy = remote(
            prod.at[pl.ds(pl.multiple_of(to_b * rows_of, rows_of), rows_of)], band_sum.at[d],
            r_slot + d, r_slot + d, (to_b, me_g),
        )
        copy.start()
        band_copies.append(copy)
    start_backs()
    total = prod[pl.ds(pl.multiple_of(me_b * rows_of, rows_of), rows_of), :]
    for copy in band_copies:
        copy.wait_recv()
    for d in range(1, bands):
        total = total + band_sum[d]
    mine[...] = total
    grid_copies = []
    for d in range(1, slabs):
        copy = remote(mine, grid_sum.at[d], g_slot + d, g_slot + d, (me_b, lax.rem(me_g + d, slabs)))
        copy.start()
        grid_copies.append(copy)

    def put_out(src, src_at, g):
        def at_plane(p, carry):
            cube = jnp.stack(cells(src[src_at + p]))
            out_ref[group(g), rows_at(p, 1), :] = jnp.swapaxes(cube, 0, 1)
            return carry

        lax.fori_loop(0, planes, at_plane, 0)

    put_out(field.at[DEGREE], RADIUS + side * planes, side)
    for copy in backs[:-1]:
        copy.wait_recv()
    backs[-1].wait()
    put_out(back_y, 0, other)
    for copy in swaps + [pot_swap, early[0][1]] + backs[:-1] + band_copies:
        copy.wait_send()
    for copy in fringes:
        pl.when(can)(copy.wait_send)
    for ready, copy in early[1:]:
        pl.when(ready)(copy.wait_send)
    for k in range(1, DEGREE + 1):
        for ready, copy in (
            (has_up, halo_up(k)), (has_down, halo_down(k)), (has_up, coef_up(k)), (has_down, coef_down(k))
        ):
            pl.when(ready)(copy.wait_send)
    sent_shares(0)
    sent_shares(1)
    for copy in grid_copies:
        copy.wait_recv()
    for d in range(1, slabs):
        total = total + grid_sum[d]
    total = total / total_points
    gram_ref[...] = total[:, :states_all]
    ham_ref[...] = total[:, states_all:]

    for copy in grid_copies:
        copy.wait_send()


def per_device(bands, slabs, states, potential, proj_index, proj_value, proj_strength):
    state_count, planes, rows, cols = states.shape
    area = rows * cols
    points = planes * area
    atoms, support = proj_index.shape
    half = state_count // 2
    chunk = 2 * planes
    wide = -(-atoms // LANES) * LANES
    all_states = bands * state_count
    strength = proj_strength.reshape(1, atoms)
    slots = 5 + 4 * (DEGREE + 1) + 5 + 10 * bands + slabs
    vmem, hbm = pl.BlockSpec(memory_space=pltpu.VMEM), pl.BlockSpec(memory_space=pltpu.HBM)
    f32 = jnp.float32
    out, gram, ham = pl.pallas_call(
        functools.partial(
            kernel, bands, slabs, planes, rows, cols, atoms, float(points * slabs)
        ),
        out_shape=(
            jax.ShapeDtypeStruct((state_count, planes * rows, cols), f32),
            jax.ShapeDtypeStruct((state_count, all_states), f32),
            jax.ShapeDtypeStruct((state_count, all_states), f32),
        ),
        in_specs=[hbm, hbm, hbm, hbm, hbm],
        out_specs=(vmem, vmem, vmem),
        scratch_shapes=[
            pltpu.VMEM((half, (chunk + 2 * RADIUS) * rows, cols), f32),
            pltpu.VMEM((half, planes * rows, cols), f32),
            pltpu.VMEM((DEGREE + 2, chunk + 2 * RADIUS, half, area), f32),
            pltpu.VMEM((planes, half, area), f32),
            pltpu.VMEM((chunk, rows, cols), f32),
            pltpu.VMEM((atoms, support), jnp.int32),
            pltpu.VMEM((atoms, support), f32),
            pltpu.VMEM((1, atoms), f32),
            pltpu.VMEM((atoms, chunk * rows, cols), f32),
            pltpu.VMEM((chunk, 2 * atoms, area), jnp.bfloat16),
            pltpu.VMEM((2 * cols, 2 * cols), jnp.bfloat16),
            pltpu.VMEM((chunk, half, area), f32),
            pltpu.VMEM((DEGREE + 2, half, wide), f32),
            pltpu.VMEM((DEGREE + 1, 2, half, wide), f32),
            pltpu.VMEM((5, half, wide), f32),
            pltpu.VMEM((planes, half, area), f32),
            pltpu.VMEM((2, planes // bands, all_states, area), f32),
            pltpu.VMEM((all_states, 2 * all_states), f32),
            pltpu.VMEM((bands, state_count, 2 * all_states), f32),
            pltpu.VMEM((state_count, 2 * all_states), f32),
            pltpu.VMEM((slabs, state_count, 2 * all_states), f32),
            pltpu.SemaphoreType.DMA((slots,)),
            pltpu.SemaphoreType.DMA((slots,)),
            pltpu.SemaphoreType.DMA((6,)),
        ],
        compiler_params=pltpu.CompilerParams(
            collective_id=0, has_side_effects=True, vmem_limit_bytes=48 * 1024 * 1024
        ),
    )(*(pltpu.with_memory_space_constraint(x, pltpu.HBM) for x in (states.reshape(state_count, planes * rows, cols), potential, proj_index, proj_value, strength)))

    def place(*refs):
        moves = [pltpu.make_async_copy(refs[n], refs[3 + n], refs[6].at[n]) for n in range(3)]
        for move in moves:
            move.start()
        for move in moves:
            move.wait()

    out, gram, ham = pl.pallas_call(
        place,
        out_shape=tuple(jax.ShapeDtypeStruct(x.shape, f32) for x in (out, gram, ham)),
        in_specs=[vmem] * 3,
        out_specs=(hbm,) * 3,
        scratch_shapes=[pltpu.SemaphoreType.DMA((3,))],
    )(*(pltpu.with_memory_space_constraint(x, pltpu.VMEM) for x in (out, gram, ham)))
    return out.reshape(states.shape), gram, ham


def solution(mesh):
    in_specs = (P("band", "grid", None, None), P("grid", None, None), P(), P(), P())
    out_specs = (P("band", "grid", None, None), P("band", None), P("band", None))
    return jax.shard_map(
        functools.partial(per_device, mesh.shape["band"], mesh.shape["grid"]),
        mesh=mesh, in_specs=in_specs, out_specs=out_specs, check_vma=False,
    )
```

```python
import functools

import jax
import jax.numpy as jnp
from jax import lax
from jax.experimental import pallas as pl
from jax.experimental.pallas import tpu as pltpu
from jax.sharding import PartitionSpec as P

RADIUS = 4
DEGREE = 4
LANES = 128
MESH = pl.DeviceIdType.MESH

stencil_weights = (-205.0 / 72.0, 1.6, -0.2, 8.0 / 315.0, -1.0 / 560.0)
filter_centre = 10.0
filter_half = 6.0


def kernel(
    bands, slabs, planes, rows, cols, atoms, total_points,
    states, potential, index_in, value_in, strength_in,
    out_ref, gram_ref, ham_ref,
    raw, spare_raw, field, spare, pot, index_ref, value_ref, strength_ref, proj, parts_ref, shift_ref, across,
    coef_mine, coef_far, coef_first, overlap, extra, back_y, both, prod, band_sum, mine, grid_sum,
    send, recv, local,
):
    half = states.shape[0] // 2
    area = rows * cols
    chunk = 2 * planes
    me_b, me_g = lax.axis_index("band"), lax.axis_index("grid")
    pair, side = me_g // 2, me_g % 2
    other = 1 - side
    last_pair = slabs // 2 - 1
    has_down, has_up = pair > 0, pair < last_pair
    counter = [0]

    def remote(src, dst, out_slot, in_slot, where):
        return pltpu.make_async_remote_copy(
            src_ref=src, dst_ref=dst, send_sem=send.at[out_slot], recv_sem=recv.at[in_slot],
            device_id=where, device_id_type=MESH,
        )

    def slots(count):
        first = counter[0]
        counter[0] += count
        return first

    def rows_at(plane, count):
        return pl.ds(pl.multiple_of(plane * rows, rows), count * rows)

    def group(g):
        return pl.ds(pl.multiple_of(g * half, half), half)

    partner = (me_b, 2 * pair + other)
    up, down = (me_b, me_g + 2), (me_b, me_g - 2)
    up_other, down_other = (me_b, 2 * pair + 2 + other), (me_b, 2 * pair - 2 + other)
    crossing = [
        (lax.rem(me_b + d, bands), 2 * pair + lax.rem(side + e, 2)) for d in range(1, bands) for e in range(2)
    ]
    barrier = pltpu.get_barrier_semaphore()

    def greet(where):
        pl.semaphore_signal(barrier, inc=1, device_id=where, device_id_type=MESH)

    def greet_pair(one, two):
        greet(one)
        greet(two)

    coef_far[...] = jnp.zeros_like(coef_far)
    coef_first[...] = jnp.zeros_like(coef_first)

    if last_pair > DEGREE:
        for d in range(1, slabs):
            greet((me_b, lax.rem(me_g + d, slabs)))
        expected = len(crossing) + slabs - 1
    else:
        greet(partner)
        pl.when(has_up)(lambda: greet_pair(up, up_other))
        pl.when(has_down)(lambda: greet_pair(down, down_other))
        expected = len(crossing) + 1 + 2 * (has_up.astype(jnp.int32) + has_down.astype(jnp.int32))
    for peer in crossing:
        greet(peer)

    own = [
        pltpu.make_async_copy(states.at[group(side)], raw.at[:, rows_at(RADIUS + side * planes, planes)], local.at[0]),
        pltpu.make_async_copy(states.at[group(other)], spare_raw, local.at[1]),
        pltpu.make_async_copy(index_in, index_ref, local.at[2]),
        pltpu.make_async_copy(value_in, value_ref, local.at[3]),
        pltpu.make_async_copy(potential, pot.at[pl.ds(side * planes, planes)], local.at[4]),
        pltpu.make_async_copy(strength_in, strength_ref, local.at[5]),
    ]
    for copy in own:
        copy.start()

    pl.semaphore_wait(barrier, expected)

    first = slots(5)
    toward, can = 2 * side - 1, jnp.where(side == 1, pair < last_pair, pair > 0)
    outer_at, inner_at = side * (planes - RADIUS), other * RADIUS
    fringes = [
        remote(
            states.at[pl.ds(h * half, half), rows_at(outer_at, RADIUS)],
            raw.at[:, rows_at(other * (RADIUS + chunk), RADIUS)],
            first + h, first + other, (me_b, 2 * (pair + toward) + h),
        )
        for h in range(2)
    ]
    swaps = [
        remote(
            states.at[group(other), rows_at(start, count)], raw.at[:, rows_at(RADIUS + side * planes + start, count)],
            first + 2 + n, first + 2 + n, partner,
        )
        for n, (start, count) in enumerate(((outer_at, RADIUS), (inner_at, planes - RADIUS)))
    ]
    pot_swap = remote(potential, pot.at[pl.ds(side * planes, planes)], first + 4, first + 4, partner)

    def start_fringes():
        for copy in fringes:
            copy.start()

    pl.when(can)(start_fringes)
    for copy in swaps:
        copy.start()
    pot_swap.start()

    points = index_ref.shape[1]
    row_iota = lax.broadcasted_iota(jnp.int32, (chunk * rows, points), 0) + pair * (chunk * rows)
    col_iota = lax.broadcasted_iota(jnp.int32, (cols, points), 0)

    def build(a, carry):
        idx = index_ref[pl.ds(a, 1), :]
        row = lax.div(idx, cols)
        here = row_iota == row
        onehot = jnp.where(col_iota == idx - row * cols, 1.0, 0.0).astype(jnp.bfloat16)
        rest = value_ref[pl.ds(a, 1), :]
        parts = []
        for _ in range(3):
            part = rest.astype(jnp.bfloat16).astype(jnp.float32)
            rest = rest - part
            parts.append(jnp.where(here, part, 0.0).astype(jnp.bfloat16))
        proj[a] = lax.dot_general(
            jnp.concatenate(parts, axis=1), jnp.concatenate([onehot] * 3, axis=1), (((1,), (1,)), ((), ())),
            preferred_element_type=jnp.float32,
        )
        return carry

    own[2].wait()
    own[3].wait()
    lax.fori_loop(0, atoms, build, 0, unroll=4)
    pack = 16

    def split(v):
        high = v.astype(jnp.bfloat16)
        return high, (v - high.astype(jnp.float32)).astype(jnp.bfloat16)

    def arrange(p, carry):
        for j in range(0, atoms, pack):
            cubes = [jnp.swapaxes(proj[j + i : j + i + 8, rows_at(p, 1), :], 0, 1) for i in range(0, pack, 8)]
            for y in range(rows):
                high, low = split(jnp.concatenate([cube[y] for cube in cubes], axis=0))
                parts_ref[p, j : j + pack, y * cols : (y + 1) * cols] = high
                parts_ref[p, atoms + j : atoms + j + pack, y * cols : (y + 1) * cols] = low
        return carry

    lax.fori_loop(0, chunk, arrange, 0, unroll=2)

    def products(p, total):
        return total + lax.dot_general(
            parts_ref[p], parts_ref[p], (((1,), (1,)), ((), ())), preferred_element_type=jnp.float32
        )

    total = lax.fori_loop(0, chunk, products, jnp.zeros((2 * atoms, 2 * atoms), jnp.float32), unroll=8)
    overlap[...] = total[:atoms, :atoms] + total[:atoms, atoms:] + total[atoms:, :atoms]

    apart = jnp.abs(
        lax.broadcasted_iota(jnp.int32, (cols, cols), 0) - lax.broadcasted_iota(jnp.int32, (cols, cols), 1)
    )
    band = jnp.zeros((cols, cols), jnp.float32)
    for d in range(1, RADIUS + 1):
        band = jnp.where(apart == d, stencil_weights[d], band)
    band_high, band_low = split(band)
    shift_ref[:cols, :cols] = band_high
    shift_ref[cols:, :cols] = band_high
    shift_ref[:cols, cols:] = band_low
    shift_ref[cols:, cols:] = jnp.zeros((cols, cols), jnp.bfloat16)

    def relayout(src, src_at, dst, dst_at, count):
        def at_plane(n, carry):
            cube = jnp.swapaxes(src[:, rows_at(src_at + n, 1), :], 0, 1)
            for y in range(rows):
                dst[dst_at + n, :, y * cols : (y + 1) * cols] = cube[y]
            return carry

        lax.fori_loop(0, count, at_plane, 0)

    wide = coef_mine.shape[-1]

    def cells(plane):
        return [plane[:, y * cols : (y + 1) * cols] for y in range(rows)]

    def stack(one, two, axis):
        return jnp.concatenate([one.astype(jnp.float32), two.astype(jnp.float32)], axis=axis).astype(jnp.bfloat16)

    def project(src, src_at, proj_at, count):
        total = jnp.zeros((2 * half, 2 * atoms), jnp.float32)
        for n in range(count):
            total = total + lax.dot_general(
                stack(*split(src[src_at + n]), 0), parts_ref[proj_at + n], (((1,), (1,)), ((), ())),
                preferred_element_type=jnp.float32,
            )
        return widen(total[:half, :atoms] + total[:half, atoms:] + total[half:, :atoms])

    def widen(result):
        if wide == atoms:
            return result
        return jnp.concatenate([result, jnp.zeros((half, wide - atoms), jnp.float32)], axis=1)

    def sum_across(k):
        rows_all = jnp.concatenate([cell for p in range(chunk) for cell in cells(field[k, RADIUS + p])], axis=0)
        both_parts = lax.dot_general(
            jnp.concatenate(split(rows_all), axis=1), shift_ref[...], (((1,), (0,)), ((), ())),
            preferred_element_type=jnp.float32,
        )
        z = both_parts[:, :cols] + both_parts[:, cols:]
        for p in range(chunk):
            for y in range(rows):
                at = (p * rows + y) * half
                across[p, :, y * cols : (y + 1) * cols] = z[at : at + half]

    def local_part(k, p, a, b, low=chunk, high=chunk):
        src = field.at[k]
        cell = cells(src[p + RADIUS])
        line = cells(across[p])
        ring = [None]
        for d in range(1, RADIUS + 1):
            near = [src[p + RADIUS + s * d] for s, room in ((1, high), (-1, low)) if d <= room]
            ring.append(near[0] + near[1] if len(near) == 2 else near[0] if near else None)
        weight = [-0.5 * a * w for w in stencil_weights]
        result = []
        for y in range(rows):
            v = cell[y]
            t = v * (a * pot[p, y : y + 1, :] + (3.0 * weight[0] + b)) + (-0.5 * a) * line[y]
            for d in range(1, RADIUS + 1):
                terms = [cell[y + s * d] for s in (1, -1) if 0 <= y + s * d < rows]
                if ring[d] is not None:
                    terms.append(ring[d][:, y * cols : (y + 1) * cols])
                if terms:
                    t = t + weight[d] * functools.reduce(jnp.add, terms)
            result.append(t)
        return result

    def store(k, p, tiles):
        for y in range(rows):
            field[k, p + RADIUS, :, y * cols : (y + 1) * cols] = tiles[y]

    def stored(k, p):
        return cells(field[k, p + RADIUS])

    cuts, early_cuts = 4, 3
    halo_slots, coef_slots = slots(2 * cuts * (DEGREE + 1)), slots(2 * (DEGREE + 1))

    def cut(g):
        return slice(g * (area // cuts), (g + 1) * (area // cuts))

    def halo_up(k, g):
        slot = halo_slots + 2 * (cuts * k + g)
        return remote(field.at[k, chunk : chunk + RADIUS, :, cut(g)], field.at[k, 0:RADIUS, :, cut(g)], slot, slot, up)

    def halo_down(k, g):
        slot = halo_slots + 2 * (cuts * k + g) + 1
        return remote(
            field.at[k, RADIUS : 2 * RADIUS, :, cut(g)],
            field.at[k, chunk + RADIUS : chunk + 2 * RADIUS, :, cut(g)], slot, slot, down,
        )

    def coef_up(k):
        slot = coef_slots + 2 * k
        return remote(coef_mine.at[k], coef_far.at[k, 0], slot, slot, up)

    def coef_down(k):
        slot = coef_slots + 2 * k + 1
        return remote(coef_mine.at[k], coef_far.at[k, 1], slot, slot, down)

    first_slots = slots(5)
    other_mine = coef_mine.at[DEGREE + 1]
    early = [
        (None, remote(other_mine, coef_first.at[0], first_slots, first_slots, partner)),
        (has_up, remote(coef_mine.at[0], coef_first.at[1], first_slots + 1, first_slots + 1, up)),
        (has_up, remote(other_mine, coef_first.at[2], first_slots + 2, first_slots + 2, up_other)),
        (has_down, remote(coef_mine.at[0], coef_first.at[3], first_slots + 3, first_slots + 3, down)),
        (has_down, remote(other_mine, coef_first.at[4], first_slots + 4, first_slots + 4, down_other)),
    ]

    own[1].wait()
    relayout(spare_raw, 0, spare, 0, planes)
    coef_mine[DEGREE + 1] = project(spare, 0, side * planes, planes)
    own[0].wait()
    relayout(raw, RADIUS + side * planes, field.at[0], RADIUS + side * planes, planes)
    coef_mine[0] = project(field.at[0], RADIUS + side * planes, side * planes, planes)
    for ready, copy in early:
        if ready is None:
            copy.start()
        else:
            pl.when(ready)(copy.start)

    def spread_of(weights):
        high, low = split(weights)
        return stack(stack(high, high, 1), stack(low, jnp.zeros_like(low), 1), 0)

    def add_nonlocal(k, spread, first_plane, count):
        for p in range(first_plane, first_plane + count):
            both_parts = lax.dot_general(
                spread, parts_ref[p], (((1,), (0,)), ((), ())), preferred_element_type=jnp.float32
            )
            field[k, p + RADIUS] = field[k, p + RADIUS] + (both_parts[:half] + both_parts[half:])

    own[4].wait()
    own[5].wait()
    swaps[0].wait_recv()
    relayout(raw, RADIUS + other * (chunk - RADIUS), field.at[0], RADIUS + other * (chunk - RADIUS), RADIUS)
    swaps[1].wait_recv()
    relayout(
        raw, 2 * RADIUS + other * (planes - RADIUS), field.at[0], 2 * RADIUS + other * (planes - RADIUS),
        planes - RADIUS,
    )
    pot_swap.wait_recv()
    early[0][1].wait_recv()

    def wait_below():
        remote(
            states.at[pl.ds(0, half), rows_at(0, RADIUS)], raw.at[:, rows_at(0, RADIUS)], first, first, partner
        ).wait_recv()
        early[1][1].wait_recv()
        early[2][1].wait_recv()
        relayout(raw, 0, field.at[0], 0, RADIUS)

    def wait_above():
        remote(
            states.at[pl.ds(0, half), rows_at(0, RADIUS)], raw.at[:, rows_at(0, RADIUS)], first, first + 1, partner
        ).wait_recv()
        early[3][1].wait_recv()
        early[4][1].wait_recv()
        relayout(raw, RADIUS + chunk, field.at[0], RADIUS + chunk, RADIUS)

    def clear(at):
        def go():
            field[0, at : at + RADIUS] = jnp.zeros((RADIUS, half, area), jnp.float32)

        return go

    pl.when(has_down)(wait_below)
    pl.when(has_up)(wait_above)
    pl.when(jnp.logical_not(has_down))(clear(0))
    pl.when(jnp.logical_not(has_up))(clear(RADIUS + chunk))
    for k in range(1, DEGREE + 1):
        pl.when(jnp.logical_not(has_down))(
            functools.partial(field.__setitem__, (k, slice(0, RADIUS)), jnp.zeros((RADIUS, half, area), jnp.float32))
        )
        pl.when(jnp.logical_not(has_up))(
            functools.partial(
                field.__setitem__, (k, slice(RADIUS + chunk, 2 * RADIUS + chunk)),
                jnp.zeros((RADIUS, half, area), jnp.float32),
            )
        )

    scale0 = 1.0 / filter_half
    total = coef_mine[0]
    for n in range(5):
        total = total + coef_first[n]
    spread0 = spread_of(total[:, :atoms] * strength_ref[...] * scale0)
    sum_across(0)

    def whole(p, carry):
        store(1, p, local_part(0, p, scale0, -filter_centre * scale0))
        return carry

    lax.fori_loop(0, RADIUS, whole, 0)
    add_nonlocal(1, spread0, 0, RADIUS)
    for g in range(early_cuts):
        pl.when(has_down)(halo_down(1, g).start)
    lax.fori_loop(chunk - RADIUS, chunk, whole, 0)
    add_nonlocal(1, spread0, chunk - RADIUS, RADIUS)
    for g in range(early_cuts):
        pl.when(has_up)(halo_up(1, g).start)
    lax.fori_loop(RADIUS, chunk - RADIUS, whole, 0)
    add_nonlocal(1, spread0, RADIUS, chunk - 2 * RADIUS)

    def send_coefs(k):
        pl.when(has_up)(coef_up(k).start)
        pl.when(has_down)(coef_down(k).start)

    coef_mine[1] = project(field.at[1], RADIUS, 0, chunk)
    send_coefs(1)
    for g in range(early_cuts, cuts):
        pl.when(has_down)(halo_down(1, g).start)
        pl.when(has_up)(halo_up(1, g).start)

    def send_halos(k, g):
        pl.when(has_down)(halo_down(k, g).start)
        pl.when(has_up)(halo_up(k, g).start)

    def apply(k, final):
        scale = 1.0 if final else 2.0 / filter_half
        shift = 0.0 if final else -filter_centre * scale
        sum_across(k)

        def with_last(p, tiles):
            if final:
                return tiles
            old = cells(field[k - 1, p + RADIUS])
            return [tiles[y] - old[y] for y in range(rows)]

        def inner(p, carry):
            store(k + 1, p, with_last(p, local_part(k, p, scale, shift)))
            return carry

        for n in range(RADIUS):
            for p, low, high in ((n, n, chunk), (chunk - 1 - n, chunk, n)):
                store(k + 1, p, with_last(p, local_part(k, p, scale, shift, low, high)))
        lax.fori_loop(RADIUS, chunk - RADIUS, inner, 0)

        ahead = None if final else project(field.at[k + 1], RADIUS, 0, chunk)
        pl.when(has_down)(coef_up(k).wait_recv)
        pl.when(has_up)(coef_down(k).wait_recv)
        coefs = coef_mine[k] + coef_far[k, 0] + coef_far[k, 1]
        weights = coefs[:, :atoms] * strength_ref[...] * scale
        spread = spread_of(weights)
        if not final:
            ahead = ahead + widen(
                lax.dot_general(
                    weights, overlap[...], (((1,), (0,)), ((), ())),
                    precision=lax.Precision.HIGHEST, preferred_element_type=jnp.float32,
                )
            )

        def add_halo(p, at, g, planes_in):
            tiles = None
            for w, plane in planes_in:
                term = (-0.5 * scale * w) * field[k, plane, :, cut(g)]
                tiles = term if tiles is None else tiles + term
            if not final:
                extra[at, :, cut(g)] = tiles
            field[k + 1, p + RADIUS, :, cut(g)] = field[k + 1, p + RADIUS, :, cut(g)] + tiles

        def edges():
            add_nonlocal(k + 1, spread, 0, RADIUS)
            add_nonlocal(k + 1, spread, chunk - RADIUS, RADIUS)

        def lower(g):
            pl.when(has_down)(halo_up(k, g).wait_recv)
            for p in range(RADIUS):
                add_halo(p, p, g, [(stencil_weights[d], RADIUS + p - d) for d in range(p + 1, RADIUS + 1)])

        def upper(g):
            pl.when(has_up)(halo_down(k, g).wait_recv)
            for n in range(RADIUS):
                p = chunk - 1 - n
                add_halo(
                    p, 2 * RADIUS - 1 - n, g,
                    [(stencil_weights[d], RADIUS + p + d) for d in range(n + 1, RADIUS + 1)],
                )

        def middle():
            add_nonlocal(k + 1, spread, RADIUS, chunk - 2 * RADIUS)

        return ahead, edges, lower, middle, upper

    def step(k, carry):
        ahead, edges, lower, middle, upper = apply(k, False)
        edges()
        for g in range(cuts):
            lower(g)
            upper(g)
            if g < early_cuts:
                send_halos(k + 1, g)
        coef_mine[k + 1] = (
            ahead + project(extra, 0, 0, RADIUS) + project(extra, RADIUS, chunk - RADIUS, RADIUS)
        )
        send_coefs(k + 1)
        for g in range(early_cuts, cuts):
            send_halos(k + 1, g)
        middle()
        return carry

    lax.fori_loop(1, DEGREE, step, 0)

    part = planes // bands
    shares = 2 * bands
    y_out, y_in, h_out, h_in = slots(shares), slots(shares), slots(shares), slots(shares)
    mine_at = me_b * 2 + side

    def share(which, q):
        src = field.at[DEGREE + which, RADIUS + q * part : RADIUS + (q + 1) * part]
        dst = both.at[which, :, group(mine_at)]
        is_mine = jnp.logical_and(me_b == q % bands, side == q // bands)
        away = remote(
            src, dst, (y_out, h_out)[which] + q, (y_in, h_in)[which] + mine_at, (q % bands, 2 * pair + q // bands)
        )
        return is_mine, away, pltpu.make_async_copy(src, dst, local.at[which])

    def send_share(which, q):
        is_mine, away, keep = share(which, q)
        pl.when(is_mine)(keep.start)
        pl.when(jnp.logical_not(is_mine))(away.start)

    def take_shares(which):
        for q in range(shares):
            sender = q
            is_mine = jnp.logical_and(me_b == sender // 2, side == sender % 2)
            src = field.at[DEGREE + which, RADIUS : RADIUS + part]
            dst = both.at[which, :, pl.ds(sender * half, half)]
            come = remote(src, dst, y_out, (y_in, h_in)[which] + sender, partner)
            pl.when(is_mine)(pltpu.make_async_copy(src, dst, local.at[which]).wait)
            pl.when(jnp.logical_not(is_mine))(come.wait_recv)

    def sent_shares(which):
        for q in range(shares):
            is_mine, away, keep = share(which, q)
            pl.when(jnp.logical_not(is_mine))(away.wait_send)

    for q in range(shares):
        send_share(0, q)
    ahead, edges, lower, middle, upper = apply(DEGREE, True)
    inside = [q for q in range(shares) if q * part >= RADIUS and (q + 1) * part <= chunk - RADIUS]
    middle()
    for q in inside:
        send_share(1, q)
    edges()
    for g in range(cuts):
        lower(g)
    for q in range(shares // 2):
        if q not in inside:
            send_share(1, q)
    for g in range(cuts):
        upper(g)
    for q in range(shares // 2, shares):
        if q not in inside:
            send_share(1, q)

    back_slot = slots(bands)
    my_planes = back_y.at[pl.ds(me_b * part, part)]

    def gathered_of(b):
        return both.at[0, :, group(b * 2 + other)]

    backs = [
        remote(
            gathered_of(lax.rem(me_b + d, bands)), my_planes, back_slot + d, back_slot + d,
            (lax.rem(me_b + d, bands), me_g),
        )
        for d in range(1, bands)
    ]
    backs.append(pltpu.make_async_copy(gathered_of(me_b), my_planes, local.at[2]))

    def start_backs():
        for copy in backs:
            copy.start()

    def inner_rows(left, right):
        return lax.dot_general(
            left, right, (((1,), (1,)), ((), ())),
            precision=lax.Precision.HIGH, preferred_element_type=jnp.float32,
        )

    states_all = bands * 2 * half
    take_shares(0)
    total = inner_rows(both[0, 0], both[0, 0])
    for i in range(1, part):
        total = total + inner_rows(both[0, i], both[0, i])
    prod[:, :states_all] = total
    take_shares(1)
    total = inner_rows(both[1, 0], both[0, 0])
    for i in range(1, part):
        total = total + inner_rows(both[1, i], both[0, i])
    prod[:, states_all:] = total

    rows_of = 2 * half
    r_slot, g_slot = slots(bands), slots(slabs)
    band_copies = []
    for d in range(1, bands):
        to_b = lax.rem(me_b + d, bands)
        copy = remote(
            prod.at[pl.ds(pl.multiple_of(to_b * rows_of, rows_of), rows_of)], band_sum.at[d],
            r_slot + d, r_slot + d, (to_b, me_g),
        )
        copy.start()
        band_copies.append(copy)
    start_backs()
    total = prod[pl.ds(pl.multiple_of(me_b * rows_of, rows_of), rows_of), :]
    for copy in band_copies:
        copy.wait_recv()
    for d in range(1, bands):
        total = total + band_sum[d]
    mine[...] = total
    grid_copies = []
    for d in range(1, slabs):
        copy = remote(mine, grid_sum.at[d], g_slot + d, g_slot + d, (me_b, lax.rem(me_g + d, slabs)))
        copy.start()
        grid_copies.append(copy)

    def put_out(src, src_at, g):
        def at_plane(p, carry):
            cube = jnp.stack(cells(src[src_at + p]))
            out_ref[group(g), rows_at(p, 1), :] = jnp.swapaxes(cube, 0, 1)
            return carry

        lax.fori_loop(0, planes, at_plane, 0)

    put_out(field.at[DEGREE], RADIUS + side * planes, side)
    for copy in backs[:-1]:
        copy.wait_recv()
    backs[-1].wait()
    put_out(back_y, 0, other)
    for copy in swaps + [pot_swap, early[0][1]] + backs[:-1] + band_copies:
        copy.wait_send()
    for copy in fringes:
        pl.when(can)(copy.wait_send)
    for ready, copy in early[1:]:
        pl.when(ready)(copy.wait_send)
    for k in range(1, DEGREE + 1):
        copies = [(has_up, coef_up(k)), (has_down, coef_down(k))]
        for g in range(cuts):
            copies += [(has_up, halo_up(k, g)), (has_down, halo_down(k, g))]
        for ready, copy in copies:
            pl.when(ready)(copy.wait_send)
    sent_shares(0)
    sent_shares(1)
    for copy in grid_copies:
        copy.wait_recv()
    for d in range(1, slabs):
        total = total + grid_sum[d]
    total = total / total_points
    gram_ref[...] = total[:, :states_all]
    ham_ref[...] = total[:, states_all:]

    for copy in grid_copies:
        copy.wait_send()


def per_device(bands, slabs, states, potential, proj_index, proj_value, proj_strength):
    state_count, planes, rows, cols = states.shape
    area = rows * cols
    points = planes * area
    atoms, support = proj_index.shape
    half = state_count // 2
    chunk = 2 * planes
    wide = -(-atoms // LANES) * LANES
    all_states = bands * state_count
    strength = proj_strength.reshape(1, atoms)
    slots = 5 + 10 * (DEGREE + 1) + 5 + 10 * bands + slabs
    vmem, hbm = pl.BlockSpec(memory_space=pltpu.VMEM), pl.BlockSpec(memory_space=pltpu.HBM)
    f32 = jnp.float32
    out, gram, ham = pl.pallas_call(
        functools.partial(
            kernel, bands, slabs, planes, rows, cols, atoms, float(points * slabs)
        ),
        out_shape=(
            jax.ShapeDtypeStruct((state_count, planes * rows, cols), f32),
            jax.ShapeDtypeStruct((state_count, all_states), f32),
            jax.ShapeDtypeStruct((state_count, all_states), f32),
        ),
        in_specs=[hbm, hbm, hbm, hbm, hbm],
        out_specs=(vmem, vmem, vmem),
        scratch_shapes=[
            pltpu.VMEM((half, (chunk + 2 * RADIUS) * rows, cols), f32),
            pltpu.VMEM((half, planes * rows, cols), f32),
            pltpu.VMEM((DEGREE + 2, chunk + 2 * RADIUS, half, area), f32),
            pltpu.VMEM((planes, half, area), f32),
            pltpu.VMEM((chunk, rows, cols), f32),
            pltpu.VMEM((atoms, support), jnp.int32),
            pltpu.VMEM((atoms, support), f32),
            pltpu.VMEM((1, atoms), f32),
            pltpu.VMEM((atoms, chunk * rows, cols), f32),
            pltpu.VMEM((chunk, 2 * atoms, area), jnp.bfloat16),
            pltpu.VMEM((2 * cols, 2 * cols), jnp.bfloat16),
            pltpu.VMEM((chunk, half, area), f32),
            pltpu.VMEM((DEGREE + 2, half, wide), f32),
            pltpu.VMEM((DEGREE + 1, 2, half, wide), f32),
            pltpu.VMEM((5, half, wide), f32),
            pltpu.VMEM((atoms, atoms), f32),
            pltpu.VMEM((2 * RADIUS, half, area), f32),
            pltpu.VMEM((planes, half, area), f32),
            pltpu.VMEM((2, planes // bands, all_states, area), f32),
            pltpu.VMEM((all_states, 2 * all_states), f32),
            pltpu.VMEM((bands, state_count, 2 * all_states), f32),
            pltpu.VMEM((state_count, 2 * all_states), f32),
            pltpu.VMEM((slabs, state_count, 2 * all_states), f32),
            pltpu.SemaphoreType.DMA((slots,)),
            pltpu.SemaphoreType.DMA((slots,)),
            pltpu.SemaphoreType.DMA((6,)),
        ],
        compiler_params=pltpu.CompilerParams(
            collective_id=0, has_side_effects=True, vmem_limit_bytes=48 * 1024 * 1024
        ),
    )(*(pltpu.with_memory_space_constraint(x, pltpu.HBM) for x in (states.reshape(state_count, planes * rows, cols), potential, proj_index, proj_value, strength)))

    def place(*refs):
        moves = [pltpu.make_async_copy(refs[n], refs[3 + n], refs[6].at[n]) for n in range(3)]
        for move in moves:
            move.start()
        for move in moves:
            move.wait()

    out, gram, ham = pl.pallas_call(
        place,
        out_shape=tuple(jax.ShapeDtypeStruct(x.shape, f32) for x in (out, gram, ham)),
        in_specs=[vmem] * 3,
        out_specs=(hbm,) * 3,
        scratch_shapes=[pltpu.SemaphoreType.DMA((3,))],
    )(*(pltpu.with_memory_space_constraint(x, pltpu.VMEM) for x in (out, gram, ham)))
    return out.reshape(states.shape), gram, ham


def solution(mesh):
    in_specs = (P("band", "grid", None, None), P("grid", None, None), P(), P(), P())
    out_specs = (P("band", "grid", None, None), P("band", None), P("band", None))
    return jax.shard_map(
        functools.partial(per_device, mesh.shape["band"], mesh.shape["grid"]),
        mesh=mesh, in_specs=in_specs, out_specs=out_specs, check_vma=False,
    )
```

```python
import functools

import jax
import jax.numpy as jnp
from jax import lax
from jax.experimental import pallas as pl
from jax.experimental.pallas import tpu as pltpu
from jax.sharding import PartitionSpec as P

RADIUS = 4
DEGREE = 4
LANES = 128
MESH = pl.DeviceIdType.MESH

stencil_weights = (-205.0 / 72.0, 1.6, -0.2, 8.0 / 315.0, -1.0 / 560.0)
filter_centre = 10.0
filter_half = 6.0


def kernel(
    bands, slabs, planes, rows, cols, atoms, total_points,
    states, potential, index_in, value_in, strength_in,
    out_ref, gram_ref, ham_ref,
    raw, spare_raw, field, spare, pot, index_ref, value_ref, strength_ref, proj, parts_ref, shift_ref, across,
    coef_mine, coef_far, coef_first, overlap, extra, back_y, both, prod, band_sum, mine, grid_sum,
    send, recv, local,
):
    half = states.shape[0] // 2
    area = rows * cols
    chunk = 2 * planes
    me_b, me_g = lax.axis_index("band"), lax.axis_index("grid")
    pair, side = me_g // 2, me_g % 2
    other = 1 - side
    last_pair = slabs // 2 - 1
    has_down, has_up = pair > 0, pair < last_pair
    counter = [0]

    def remote(src, dst, out_slot, in_slot, where):
        return pltpu.make_async_remote_copy(
            src_ref=src, dst_ref=dst, send_sem=send.at[out_slot], recv_sem=recv.at[in_slot],
            device_id=where, device_id_type=MESH,
        )

    def slots(count):
        first = counter[0]
        counter[0] += count
        return first

    def rows_at(plane, count):
        return pl.ds(pl.multiple_of(plane * rows, rows), count * rows)

    def group(g):
        return pl.ds(pl.multiple_of(g * half, half), half)

    partner = (me_b, 2 * pair + other)
    up, down = (me_b, me_g + 2), (me_b, me_g - 2)
    up_other, down_other = (me_b, 2 * pair + 2 + other), (me_b, 2 * pair - 2 + other)
    crossing = [
        (lax.rem(me_b + d, bands), 2 * pair + lax.rem(side + e, 2)) for d in range(1, bands) for e in range(2)
    ]
    barrier = pltpu.get_barrier_semaphore()

    def greet(where):
        pl.semaphore_signal(barrier, inc=1, device_id=where, device_id_type=MESH)

    def greet_pair(one, two):
        greet(one)
        greet(two)

    coef_far[...] = jnp.zeros_like(coef_far)
    coef_first[...] = jnp.zeros_like(coef_first)

    if last_pair > DEGREE:
        for d in range(1, slabs):
            greet((me_b, lax.rem(me_g + d, slabs)))
        expected = len(crossing) + slabs - 1
    else:
        greet(partner)
        pl.when(has_up)(lambda: greet_pair(up, up_other))
        pl.when(has_down)(lambda: greet_pair(down, down_other))
        expected = len(crossing) + 1 + 2 * (has_up.astype(jnp.int32) + has_down.astype(jnp.int32))
    for peer in crossing:
        greet(peer)

    own = [
        pltpu.make_async_copy(states.at[group(side)], raw.at[:, rows_at(RADIUS + side * planes, planes)], local.at[0]),
        pltpu.make_async_copy(states.at[group(other)], spare_raw, local.at[1]),
        pltpu.make_async_copy(index_in, index_ref, local.at[2]),
        pltpu.make_async_copy(value_in, value_ref, local.at[3]),
        pltpu.make_async_copy(potential, pot.at[pl.ds(side * planes, planes)], local.at[4]),
        pltpu.make_async_copy(strength_in, strength_ref, local.at[5]),
    ]
    for copy in own:
        copy.start()

    pl.semaphore_wait(barrier, expected)

    first = slots(5)
    toward, can = 2 * side - 1, jnp.where(side == 1, pair < last_pair, pair > 0)
    outer_at, inner_at = side * (planes - RADIUS), other * RADIUS
    fringes = [
        remote(
            states.at[pl.ds(h * half, half), rows_at(outer_at, RADIUS)],
            raw.at[:, rows_at(other * (RADIUS + chunk), RADIUS)],
            first + h, first + other, (me_b, 2 * (pair + toward) + h),
        )
        for h in range(2)
    ]
    swaps = [
        remote(
            states.at[group(other), rows_at(start, count)], raw.at[:, rows_at(RADIUS + side * planes + start, count)],
            first + 2 + n, first + 2 + n, partner,
        )
        for n, (start, count) in enumerate(((outer_at, RADIUS), (inner_at, planes - RADIUS)))
    ]
    pot_swap = remote(potential, pot.at[pl.ds(side * planes, planes)], first + 4, first + 4, partner)

    def start_fringes():
        for copy in fringes:
            copy.start()

    pl.when(can)(start_fringes)
    for copy in swaps:
        copy.start()
    pot_swap.start()

    points = index_ref.shape[1]
    row_iota = lax.broadcasted_iota(jnp.int32, (chunk * rows, points), 0) + pair * (chunk * rows)
    col_iota = lax.broadcasted_iota(jnp.int32, (cols, points), 0)

    def build(a, carry):
        idx = index_ref[pl.ds(a, 1), :]
        row = lax.div(idx, cols)
        here = row_iota == row
        onehot = jnp.where(col_iota == idx - row * cols, 1.0, 0.0).astype(jnp.bfloat16)
        rest = value_ref[pl.ds(a, 1), :]
        parts = []
        for _ in range(3):
            part = rest.astype(jnp.bfloat16).astype(jnp.float32)
            rest = rest - part
            parts.append(jnp.where(here, part, 0.0).astype(jnp.bfloat16))
        proj[a] = lax.dot_general(
            jnp.concatenate(parts, axis=1), jnp.concatenate([onehot] * 3, axis=1), (((1,), (1,)), ((), ())),
            preferred_element_type=jnp.float32,
        )
        return carry

    own[2].wait()
    own[3].wait()
    lax.fori_loop(0, atoms, build, 0, unroll=4)
    pack = 16

    def split(v):
        high = v.astype(jnp.bfloat16)
        return high, (v - high.astype(jnp.float32)).astype(jnp.bfloat16)

    def arrange(p, carry):
        for j in range(0, atoms, pack):
            cubes = [jnp.swapaxes(proj[j + i : j + i + 8, rows_at(p, 1), :], 0, 1) for i in range(0, pack, 8)]
            for y in range(rows):
                high, low = split(jnp.concatenate([cube[y] for cube in cubes], axis=0))
                parts_ref[p, j : j + pack, y * cols : (y + 1) * cols] = high
                parts_ref[p, atoms + j : atoms + j + pack, y * cols : (y + 1) * cols] = low
        return carry

    lax.fori_loop(0, chunk, arrange, 0, unroll=2)

    def products(p, total):
        return total + lax.dot_general(
            parts_ref[p], parts_ref[p], (((1,), (1,)), ((), ())), preferred_element_type=jnp.float32
        )

    total = lax.fori_loop(0, chunk, products, jnp.zeros((2 * atoms, 2 * atoms), jnp.float32), unroll=8)
    overlap[...] = total[:atoms, :atoms] + total[:atoms, atoms:] + total[atoms:, :atoms]

    apart = jnp.abs(
        lax.broadcasted_iota(jnp.int32, (cols, cols), 0) - lax.broadcasted_iota(jnp.int32, (cols, cols), 1)
    )
    band = jnp.zeros((cols, cols), jnp.float32)
    for d in range(1, RADIUS + 1):
        band = jnp.where(apart == d, stencil_weights[d], band)
    band_high, band_low = split(band)
    shift_ref[:cols, :cols] = band_high
    shift_ref[cols:, :cols] = band_high
    shift_ref[:cols, cols:] = band_low
    shift_ref[cols:, cols:] = jnp.zeros((cols, cols), jnp.bfloat16)

    def relayout(src, src_at, dst, dst_at, count):
        def at_plane(n, carry):
            cube = jnp.swapaxes(src[:, rows_at(src_at + n, 1), :], 0, 1)
            for y in range(rows):
                dst[dst_at + n, :, y * cols : (y + 1) * cols] = cube[y]
            return carry

        lax.fori_loop(0, count, at_plane, 0)

    wide = coef_mine.shape[-1]

    def cells(plane):
        return [plane[:, y * cols : (y + 1) * cols] for y in range(rows)]

    def stack(one, two, axis):
        return jnp.concatenate([one.astype(jnp.float32), two.astype(jnp.float32)], axis=axis).astype(jnp.bfloat16)

    def project(src, src_at, proj_at, count):
        total = jnp.zeros((2 * half, 2 * atoms), jnp.float32)
        for n in range(count):
            total = total + lax.dot_general(
                stack(*split(src[src_at + n]), 0), parts_ref[proj_at + n], (((1,), (1,)), ((), ())),
                preferred_element_type=jnp.float32,
            )
        return widen(total[:half, :atoms] + total[:half, atoms:] + total[half:, :atoms])

    def widen(result):
        if wide == atoms:
            return result
        return jnp.concatenate([result, jnp.zeros((half, wide - atoms), jnp.float32)], axis=1)

    def sum_across(k):
        rows_all = jnp.concatenate([cell for p in range(chunk) for cell in cells(field[k, RADIUS + p])], axis=0)
        both_parts = lax.dot_general(
            jnp.concatenate(split(rows_all), axis=1), shift_ref[...], (((1,), (0,)), ((), ())),
            preferred_element_type=jnp.float32,
        )
        z = both_parts[:, :cols] + both_parts[:, cols:]
        for p in range(chunk):
            for y in range(rows):
                at = (p * rows + y) * half
                across[p, :, y * cols : (y + 1) * cols] = z[at : at + half]

    def local_part(k, p, a, b, low=chunk, high=chunk):
        src = field.at[k]
        cell = cells(src[p + RADIUS])
        line = cells(across[p])
        ring = [None]
        for d in range(1, RADIUS + 1):
            near = [src[p + RADIUS + s * d] for s, room in ((1, high), (-1, low)) if d <= room]
            ring.append(near[0] + near[1] if len(near) == 2 else near[0] if near else None)
        weight = [-0.5 * a * w for w in stencil_weights]
        result = []
        for y in range(rows):
            v = cell[y]
            t = v * (a * pot[p, y : y + 1, :] + (3.0 * weight[0] + b)) + (-0.5 * a) * line[y]
            for d in range(1, RADIUS + 1):
                terms = [cell[y + s * d] for s in (1, -1) if 0 <= y + s * d < rows]
                if ring[d] is not None:
                    terms.append(ring[d][:, y * cols : (y + 1) * cols])
                if terms:
                    t = t + weight[d] * functools.reduce(jnp.add, terms)
            result.append(t)
        return result

    def store(k, p, tiles):
        for y in range(rows):
            field[k, p + RADIUS, :, y * cols : (y + 1) * cols] = tiles[y]

    def stored(k, p):
        return cells(field[k, p + RADIUS])

    cuts, early_cuts = 4, 3
    halo_slots, coef_slots = slots(2 * cuts * (DEGREE + 1)), slots(2 * (DEGREE + 1))

    def cut(g):
        return slice(g * (area // cuts), (g + 1) * (area // cuts))

    def halo_up(k, g):
        slot = halo_slots + 2 * (cuts * k + g)
        return remote(field.at[k, chunk : chunk + RADIUS, :, cut(g)], field.at[k, 0:RADIUS, :, cut(g)], slot, slot, up)

    def halo_down(k, g):
        slot = halo_slots + 2 * (cuts * k + g) + 1
        return remote(
            field.at[k, RADIUS : 2 * RADIUS, :, cut(g)],
            field.at[k, chunk + RADIUS : chunk + 2 * RADIUS, :, cut(g)], slot, slot, down,
        )

    def coef_up(k):
        slot = coef_slots + 2 * k
        return remote(coef_mine.at[k], coef_far.at[k, 0], slot, slot, up)

    def coef_down(k):
        slot = coef_slots + 2 * k + 1
        return remote(coef_mine.at[k], coef_far.at[k, 1], slot, slot, down)

    first_slots = slots(5)
    other_mine = coef_mine.at[DEGREE + 1]
    early = [
        (None, remote(other_mine, coef_first.at[0], first_slots, first_slots, partner)),
        (has_up, remote(coef_mine.at[0], coef_first.at[1], first_slots + 1, first_slots + 1, up)),
        (has_up, remote(other_mine, coef_first.at[2], first_slots + 2, first_slots + 2, up_other)),
        (has_down, remote(coef_mine.at[0], coef_first.at[3], first_slots + 3, first_slots + 3, down)),
        (has_down, remote(other_mine, coef_first.at[4], first_slots + 4, first_slots + 4, down_other)),
    ]

    own[1].wait()
    relayout(spare_raw, 0, spare, 0, planes)
    coef_mine[DEGREE + 1] = project(spare, 0, side * planes, planes)
    own[0].wait()
    relayout(raw, RADIUS + side * planes, field.at[0], RADIUS + side * planes, planes)
    coef_mine[0] = project(field.at[0], RADIUS + side * planes, side * planes, planes)
    for ready, copy in early:
        if ready is None:
            copy.start()
        else:
            pl.when(ready)(copy.start)

    def spread_of(weights):
        high, low = split(weights)
        return stack(stack(high, high, 1), stack(low, jnp.zeros_like(low), 1), 0)

    def add_nonlocal(k, spread, first_plane, count):
        for p in range(first_plane, first_plane + count):
            both_parts = lax.dot_general(
                spread, parts_ref[p], (((1,), (0,)), ((), ())), preferred_element_type=jnp.float32
            )
            field[k, p + RADIUS] = field[k, p + RADIUS] + (both_parts[:half] + both_parts[half:])

    own[4].wait()
    own[5].wait()
    swaps[0].wait_recv()
    relayout(raw, RADIUS + other * (chunk - RADIUS), field.at[0], RADIUS + other * (chunk - RADIUS), RADIUS)
    swaps[1].wait_recv()
    relayout(
        raw, 2 * RADIUS + other * (planes - RADIUS), field.at[0], 2 * RADIUS + other * (planes - RADIUS),
        planes - RADIUS,
    )
    pot_swap.wait_recv()
    early[0][1].wait_recv()

    def wait_below():
        remote(
            states.at[pl.ds(0, half), rows_at(0, RADIUS)], raw.at[:, rows_at(0, RADIUS)], first, first, partner
        ).wait_recv()
        early[1][1].wait_recv()
        early[2][1].wait_recv()
        relayout(raw, 0, field.at[0], 0, RADIUS)

    def wait_above():
        remote(
            states.at[pl.ds(0, half), rows_at(0, RADIUS)], raw.at[:, rows_at(0, RADIUS)], first, first + 1, partner
        ).wait_recv()
        early[3][1].wait_recv()
        early[4][1].wait_recv()
        relayout(raw, RADIUS + chunk, field.at[0], RADIUS + chunk, RADIUS)

    def clear(at):
        def go():
            field[0, at : at + RADIUS] = jnp.zeros((RADIUS, half, area), jnp.float32)

        return go

    pl.when(has_down)(wait_below)
    pl.when(has_up)(wait_above)
    pl.when(jnp.logical_not(has_down))(clear(0))
    pl.when(jnp.logical_not(has_up))(clear(RADIUS + chunk))
    for k in range(1, DEGREE + 1):
        pl.when(jnp.logical_not(has_down))(
            functools.partial(field.__setitem__, (k, slice(0, RADIUS)), jnp.zeros((RADIUS, half, area), jnp.float32))
        )
        pl.when(jnp.logical_not(has_up))(
            functools.partial(
                field.__setitem__, (k, slice(RADIUS + chunk, 2 * RADIUS + chunk)),
                jnp.zeros((RADIUS, half, area), jnp.float32),
            )
        )

    scale0 = 1.0 / filter_half
    total = coef_mine[0]
    for n in range(5):
        total = total + coef_first[n]
    spread0 = spread_of(total[:, :atoms] * strength_ref[...] * scale0)
    sum_across(0)

    def whole(p, carry):
        store(1, p, local_part(0, p, scale0, -filter_centre * scale0))
        return carry

    lax.fori_loop(0, RADIUS, whole, 0)
    add_nonlocal(1, spread0, 0, RADIUS)
    for g in range(early_cuts):
        pl.when(has_down)(halo_down(1, g).start)
    lax.fori_loop(chunk - RADIUS, chunk, whole, 0)
    add_nonlocal(1, spread0, chunk - RADIUS, RADIUS)
    for g in range(early_cuts):
        pl.when(has_up)(halo_up(1, g).start)
    lax.fori_loop(RADIUS, chunk - RADIUS, whole, 0)
    add_nonlocal(1, spread0, RADIUS, chunk - 2 * RADIUS)

    def send_coefs(k):
        pl.when(has_up)(coef_up(k).start)
        pl.when(has_down)(coef_down(k).start)

    coef_mine[1] = project(field.at[1], RADIUS, 0, chunk)
    send_coefs(1)
    for g in range(early_cuts, cuts):
        pl.when(has_down)(halo_down(1, g).start)
        pl.when(has_up)(halo_up(1, g).start)

    def send_halos(k, g):
        pl.when(has_down)(halo_down(k, g).start)
        pl.when(has_up)(halo_up(k, g).start)

    def apply(k, final):
        scale = 1.0 if final else 2.0 / filter_half
        shift = 0.0 if final else -filter_centre * scale
        sum_across(k)

        def with_last(p, tiles):
            if final:
                return tiles
            old = cells(field[k - 1, p + RADIUS])
            return [tiles[y] - old[y] for y in range(rows)]

        def inner(p, carry):
            store(k + 1, p, with_last(p, local_part(k, p, scale, shift)))
            return carry

        for n in range(RADIUS):
            for p, low, high in ((n, n, chunk), (chunk - 1 - n, chunk, n)):
                store(k + 1, p, with_last(p, local_part(k, p, scale, shift, low, high)))
        lax.fori_loop(RADIUS, chunk - RADIUS, inner, 0)

        ahead = None if final else project(field.at[k + 1], RADIUS, 0, chunk)
        pl.when(has_down)(coef_up(k).wait_recv)
        pl.when(has_up)(coef_down(k).wait_recv)
        coefs = coef_mine[k] + coef_far[k, 0] + coef_far[k, 1]
        weights = coefs[:, :atoms] * strength_ref[...] * scale
        spread = spread_of(weights)
        if not final:
            ahead = ahead + widen(
                lax.dot_general(
                    weights, overlap[...], (((1,), (0,)), ((), ())),
                    precision=lax.Precision.HIGHEST, preferred_element_type=jnp.float32,
                )
            )

        def add_halo(p, at, g, planes_in):
            tiles = None
            for w, plane in planes_in:
                term = (-0.5 * scale * w) * field[k, plane, :, cut(g)]
                tiles = term if tiles is None else tiles + term
            if not final:
                extra[at, :, cut(g)] = tiles
            field[k + 1, p + RADIUS, :, cut(g)] = field[k + 1, p + RADIUS, :, cut(g)] + tiles

        def edges():
            add_nonlocal(k + 1, spread, 0, RADIUS)
            add_nonlocal(k + 1, spread, chunk - RADIUS, RADIUS)

        def lower(g):
            pl.when(has_down)(halo_up(k, g).wait_recv)
            for p in range(RADIUS):
                add_halo(p, p, g, [(stencil_weights[d], RADIUS + p - d) for d in range(p + 1, RADIUS + 1)])

        def upper(g):
            pl.when(has_up)(halo_down(k, g).wait_recv)
            for n in range(RADIUS):
                p = chunk - 1 - n
                add_halo(
                    p, 2 * RADIUS - 1 - n, g,
                    [(stencil_weights[d], RADIUS + p + d) for d in range(n + 1, RADIUS + 1)],
                )

        def middle():
            add_nonlocal(k + 1, spread, RADIUS, chunk - 2 * RADIUS)

        return ahead, edges, lower, middle, upper

    def step(k, carry):
        ahead, edges, lower, middle, upper = apply(k, False)
        edges()
        for g in range(cuts):
            lower(g)
            upper(g)
            if g < early_cuts:
                send_halos(k + 1, g)
        coef_mine[k + 1] = (
            ahead + project(extra, 0, 0, RADIUS) + project(extra, RADIUS, chunk - RADIUS, RADIUS)
        )
        send_coefs(k + 1)
        for g in range(early_cuts, cuts):
            send_halos(k + 1, g)
        middle()
        return carry

    lax.fori_loop(1, DEGREE, step, 0)

    part = planes // bands
    shares = 2 * bands
    y_out, y_in, h_out, h_in = slots(shares), slots(shares), slots(shares), slots(shares)
    mine_at = me_b * 2 + side

    def share(which, q):
        src = field.at[DEGREE + which, RADIUS + q * part : RADIUS + (q + 1) * part]
        dst = both.at[which, :, group(mine_at)]
        is_mine = jnp.logical_and(me_b == q % bands, side == q // bands)
        away = remote(
            src, dst, (y_out, h_out)[which] + q, (y_in, h_in)[which] + mine_at, (q % bands, 2 * pair + q // bands)
        )
        return is_mine, away, pltpu.make_async_copy(src, dst, local.at[which])

    def send_share(which, q):
        is_mine, away, keep = share(which, q)
        pl.when(is_mine)(keep.start)
        pl.when(jnp.logical_not(is_mine))(away.start)

    def take_shares(which):
        for q in range(shares):
            sender = q
            is_mine = jnp.logical_and(me_b == sender // 2, side == sender % 2)
            src = field.at[DEGREE + which, RADIUS : RADIUS + part]
            dst = both.at[which, :, pl.ds(sender * half, half)]
            come = remote(src, dst, y_out, (y_in, h_in)[which] + sender, partner)
            pl.when(is_mine)(pltpu.make_async_copy(src, dst, local.at[which]).wait)
            pl.when(jnp.logical_not(is_mine))(come.wait_recv)

    def sent_shares(which):
        for q in range(shares):
            is_mine, away, keep = share(which, q)
            pl.when(jnp.logical_not(is_mine))(away.wait_send)

    for q in range(shares):
        send_share(0, q)
    ahead, edges, lower, middle, upper = apply(DEGREE, True)
    inside = [q for q in range(shares) if q * part >= RADIUS and (q + 1) * part <= chunk - RADIUS]
    middle()
    for q in inside:
        send_share(1, q)
    edges()
    for g in range(cuts):
        lower(g)
    for q in range(shares // 2):
        if q not in inside:
            send_share(1, q)
    for g in range(cuts):
        upper(g)
    for q in range(shares // 2, shares):
        if q not in inside:
            send_share(1, q)

    back_slot = slots(bands)
    my_planes = back_y.at[pl.ds(me_b * part, part)]

    def gathered_of(b):
        return both.at[0, :, group(b * 2 + other)]

    backs = [
        remote(
            gathered_of(lax.rem(me_b + d, bands)), my_planes, back_slot + d, back_slot + d,
            (lax.rem(me_b + d, bands), me_g),
        )
        for d in range(1, bands)
    ]
    backs.append(pltpu.make_async_copy(gathered_of(me_b), my_planes, local.at[2]))

    def start_backs():
        for copy in backs:
            copy.start()

    def inner_rows(left, right):
        return lax.dot_general(
            left, right, (((1,), (1,)), ((), ())),
            precision=lax.Precision.HIGH, preferred_element_type=jnp.float32,
        )

    states_all = bands * 2 * half
    for copy in swaps + [pot_swap, early[0][1]]:
        copy.wait_send()
    for copy in fringes:
        pl.when(can)(copy.wait_send)
    for ready, copy in early[1:]:
        pl.when(ready)(copy.wait_send)
    for k in range(1, DEGREE + 1):
        copies = [(has_up, coef_up(k)), (has_down, coef_down(k))]
        for g in range(cuts):
            copies += [(has_up, halo_up(k, g)), (has_down, halo_down(k, g))]
        for ready, copy in copies:
            pl.when(ready)(copy.wait_send)
    sent_shares(0)
    sent_shares(1)
    def put_out(src, src_at, g):
        def at_plane(p, carry):
            cube = jnp.stack(cells(src[src_at + p]))
            out_ref[group(g), rows_at(p, 1), :] = jnp.swapaxes(cube, 0, 1)
            return carry

        lax.fori_loop(0, planes, at_plane, 0)

    put_out(field.at[DEGREE], RADIUS + side * planes, side)
    take_shares(0)
    total = inner_rows(both[0, 0], both[0, 0])
    for i in range(1, part):
        total = total + inner_rows(both[0, i], both[0, i])
    prod[:, :states_all] = total
    take_shares(1)
    total = inner_rows(both[1, 0], both[0, 0])
    for i in range(1, part):
        total = total + inner_rows(both[1, i], both[0, i])
    prod[:, states_all:] = total

    rows_of = 2 * half
    r_slot, g_slot = slots(bands), slots(slabs)
    band_copies = []
    for d in range(1, bands):
        to_b = lax.rem(me_b + d, bands)
        copy = remote(
            prod.at[pl.ds(pl.multiple_of(to_b * rows_of, rows_of), rows_of)], band_sum.at[d],
            r_slot + d, r_slot + d, (to_b, me_g),
        )
        copy.start()
        band_copies.append(copy)
    start_backs()
    total = prod[pl.ds(pl.multiple_of(me_b * rows_of, rows_of), rows_of), :]
    for copy in band_copies:
        copy.wait_recv()
    for d in range(1, bands):
        total = total + band_sum[d]
    mine[...] = total
    grid_copies = []
    for d in range(1, slabs):
        copy = remote(mine, grid_sum.at[d], g_slot + d, g_slot + d, (me_b, lax.rem(me_g + d, slabs)))
        copy.start()
        grid_copies.append(copy)

    for copy in backs[:-1]:
        copy.wait_recv()
    backs[-1].wait()
    put_out(back_y, 0, other)
    for copy in backs[:-1] + band_copies:
        copy.wait_send()
    for copy in grid_copies:
        copy.wait_recv()
    for d in range(1, slabs):
        total = total + grid_sum[d]
    total = total / total_points
    gram_ref[...] = total[:, :states_all]
    ham_ref[...] = total[:, states_all:]

    for copy in grid_copies:
        copy.wait_send()


def per_device(bands, slabs, states, potential, proj_index, proj_value, proj_strength):
    state_count, planes, rows, cols = states.shape
    area = rows * cols
    points = planes * area
    atoms, support = proj_index.shape
    half = state_count // 2
    chunk = 2 * planes
    wide = -(-atoms // LANES) * LANES
    all_states = bands * state_count
    strength = proj_strength.reshape(1, atoms)
    slots = 5 + 10 * (DEGREE + 1) + 5 + 10 * bands + slabs
    vmem, hbm = pl.BlockSpec(memory_space=pltpu.VMEM), pl.BlockSpec(memory_space=pltpu.HBM)
    f32 = jnp.float32
    out, gram, ham = pl.pallas_call(
        functools.partial(
            kernel, bands, slabs, planes, rows, cols, atoms, float(points * slabs)
        ),
        out_shape=(
            jax.ShapeDtypeStruct((state_count, planes * rows, cols), f32),
            jax.ShapeDtypeStruct((state_count, all_states), f32),
            jax.ShapeDtypeStruct((state_count, all_states), f32),
        ),
        in_specs=[hbm, hbm, hbm, hbm, hbm],
        out_specs=(vmem, vmem, vmem),
        scratch_shapes=[
            pltpu.VMEM((half, (chunk + 2 * RADIUS) * rows, cols), f32),
            pltpu.VMEM((half, planes * rows, cols), f32),
            pltpu.VMEM((DEGREE + 2, chunk + 2 * RADIUS, half, area), f32),
            pltpu.VMEM((planes, half, area), f32),
            pltpu.VMEM((chunk, rows, cols), f32),
            pltpu.VMEM((atoms, support), jnp.int32),
            pltpu.VMEM((atoms, support), f32),
            pltpu.VMEM((1, atoms), f32),
            pltpu.VMEM((atoms, chunk * rows, cols), f32),
            pltpu.VMEM((chunk, 2 * atoms, area), jnp.bfloat16),
            pltpu.VMEM((2 * cols, 2 * cols), jnp.bfloat16),
            pltpu.VMEM((chunk, half, area), f32),
            pltpu.VMEM((DEGREE + 2, half, wide), f32),
            pltpu.VMEM((DEGREE + 1, 2, half, wide), f32),
            pltpu.VMEM((5, half, wide), f32),
            pltpu.VMEM((atoms, atoms), f32),
            pltpu.VMEM((2 * RADIUS, half, area), f32),
            pltpu.VMEM((planes, half, area), f32),
            pltpu.VMEM((2, planes // bands, all_states, area), f32),
            pltpu.VMEM((all_states, 2 * all_states), f32),
            pltpu.VMEM((bands, state_count, 2 * all_states), f32),
            pltpu.VMEM((state_count, 2 * all_states), f32),
            pltpu.VMEM((slabs, state_count, 2 * all_states), f32),
            pltpu.SemaphoreType.DMA((slots,)),
            pltpu.SemaphoreType.DMA((slots,)),
            pltpu.SemaphoreType.DMA((6,)),
        ],
        compiler_params=pltpu.CompilerParams(
            collective_id=0, has_side_effects=True, vmem_limit_bytes=48 * 1024 * 1024
        ),
    )(*(pltpu.with_memory_space_constraint(x, pltpu.HBM) for x in (states.reshape(state_count, planes * rows, cols), potential, proj_index, proj_value, strength)))

    def place(*refs):
        moves = [pltpu.make_async_copy(refs[n], refs[3 + n], refs[6].at[n]) for n in range(3)]
        for move in moves:
            move.start()
        for move in moves:
            move.wait()

    out, gram, ham = pl.pallas_call(
        place,
        out_shape=tuple(jax.ShapeDtypeStruct(x.shape, f32) for x in (out, gram, ham)),
        in_specs=[vmem] * 3,
        out_specs=(hbm,) * 3,
        scratch_shapes=[pltpu.SemaphoreType.DMA((3,))],
    )(*(pltpu.with_memory_space_constraint(x, pltpu.VMEM) for x in (out, gram, ham)))
    return out.reshape(states.shape), gram, ham


def solution(mesh):
    in_specs = (P("band", "grid", None, None), P("grid", None, None), P(), P(), P())
    out_specs = (P("band", "grid", None, None), P("band", None), P("band", None))
    return jax.shard_map(
        functools.partial(per_device, mesh.shape["band"], mesh.shape["grid"]),
        mesh=mesh, in_specs=in_specs, out_specs=out_specs, check_vma=False,
    )
```

```python
import functools

import jax
import jax.numpy as jnp
from jax import lax
from jax.experimental import pallas as pl
from jax.experimental.pallas import tpu as pltpu
from jax.sharding import PartitionSpec as P

RADIUS = 4
DEGREE = 4
LANES = 128
MESH = pl.DeviceIdType.MESH

stencil_weights = (-205.0 / 72.0, 1.6, -0.2, 8.0 / 315.0, -1.0 / 560.0)
filter_centre = 10.0
filter_half = 6.0


def kernel(
    bands, slabs, planes, rows, cols, atoms, total_points,
    states, potential, index_in, value_in, strength_in,
    out_ref, gram_ref, ham_ref,
    raw, spare_raw, field, spare, pot, index_ref, value_ref, strength_ref, proj, parts_ref, shift_ref, across,
    coef_mine, coef_far, coef_first, overlap, extra, back_y, both, prod, band_sum, mine, grid_sum,
    send, recv, local,
):
    half = states.shape[0] // 2
    area = rows * cols
    chunk = 2 * planes
    me_b, me_g = lax.axis_index("band"), lax.axis_index("grid")
    pair, side = me_g // 2, me_g % 2
    other = 1 - side
    last_pair = slabs // 2 - 1
    has_down, has_up = pair > 0, pair < last_pair
    counter = [0]

    def remote(src, dst, out_slot, in_slot, where):
        return pltpu.make_async_remote_copy(
            src_ref=src, dst_ref=dst, send_sem=send.at[out_slot], recv_sem=recv.at[in_slot],
            device_id=where, device_id_type=MESH,
        )

    def slots(count):
        first = counter[0]
        counter[0] += count
        return first

    def rows_at(plane, count):
        return pl.ds(pl.multiple_of(plane * rows, rows), count * rows)

    def group(g):
        return pl.ds(pl.multiple_of(g * half, half), half)

    partner = (me_b, 2 * pair + other)
    up, down = (me_b, me_g + 2), (me_b, me_g - 2)
    up_other, down_other = (me_b, 2 * pair + 2 + other), (me_b, 2 * pair - 2 + other)
    crossing = [
        (lax.rem(me_b + d, bands), 2 * pair + lax.rem(side + e, 2)) for d in range(1, bands) for e in range(2)
    ]
    barrier = pltpu.get_barrier_semaphore()

    def greet(where):
        pl.semaphore_signal(barrier, inc=1, device_id=where, device_id_type=MESH)

    def greet_pair(one, two):
        greet(one)
        greet(two)

    coef_far[...] = jnp.zeros_like(coef_far)
    coef_first[...] = jnp.zeros_like(coef_first)

    if last_pair > DEGREE:
        for d in range(1, slabs):
            greet((me_b, lax.rem(me_g + d, slabs)))
        expected = len(crossing) + slabs - 1
    else:
        greet(partner)
        pl.when(has_up)(lambda: greet_pair(up, up_other))
        pl.when(has_down)(lambda: greet_pair(down, down_other))
        expected = len(crossing) + 1 + 2 * (has_up.astype(jnp.int32) + has_down.astype(jnp.int32))
    for peer in crossing:
        greet(peer)

    own = [
        pltpu.make_async_copy(states.at[group(side)], raw.at[:, rows_at(RADIUS + side * planes, planes)], local.at[0]),
        pltpu.make_async_copy(states.at[group(other)], spare_raw, local.at[1]),
        pltpu.make_async_copy(index_in, index_ref, local.at[2]),
        pltpu.make_async_copy(value_in, value_ref, local.at[3]),
        pltpu.make_async_copy(potential, pot.at[pl.ds(side * planes, planes)], local.at[4]),
        pltpu.make_async_copy(strength_in, strength_ref, local.at[5]),
    ]
    for copy in own:
        copy.start()

    pl.semaphore_wait(barrier, expected)

    first = slots(5)
    toward, can = 2 * side - 1, jnp.where(side == 1, pair < last_pair, pair > 0)
    outer_at, inner_at = side * (planes - RADIUS), other * RADIUS
    fringes = [
        remote(
            states.at[pl.ds(h * half, half), rows_at(outer_at, RADIUS)],
            raw.at[:, rows_at(other * (RADIUS + chunk), RADIUS)],
            first + h, first + other, (me_b, 2 * (pair + toward) + h),
        )
        for h in range(2)
    ]
    swaps = [
        remote(
            states.at[group(other), rows_at(start, count)], raw.at[:, rows_at(RADIUS + side * planes + start, count)],
            first + 2 + n, first + 2 + n, partner,
        )
        for n, (start, count) in enumerate(((outer_at, RADIUS), (inner_at, planes - RADIUS)))
    ]
    pot_swap = remote(potential, pot.at[pl.ds(side * planes, planes)], first + 4, first + 4, partner)

    def start_fringes():
        for copy in fringes:
            copy.start()

    pl.when(can)(start_fringes)
    for copy in swaps:
        copy.start()
    pot_swap.start()

    points = index_ref.shape[1]
    row_iota = lax.broadcasted_iota(jnp.int32, (chunk * rows, points), 0) + pair * (chunk * rows)
    col_iota = lax.broadcasted_iota(jnp.int32, (cols, points), 0)

    def build(a, carry):
        idx = index_ref[pl.ds(a, 1), :]
        row = lax.div(idx, cols)
        here = row_iota == row
        onehot = jnp.where(col_iota == idx - row * cols, 1.0, 0.0).astype(jnp.bfloat16)
        rest = value_ref[pl.ds(a, 1), :]
        parts = []
        for _ in range(3):
            part = rest.astype(jnp.bfloat16).astype(jnp.float32)
            rest = rest - part
            parts.append(jnp.where(here, part, 0.0).astype(jnp.bfloat16))
        proj[a] = lax.dot_general(
            jnp.concatenate(parts, axis=1), jnp.concatenate([onehot] * 3, axis=1), (((1,), (1,)), ((), ())),
            preferred_element_type=jnp.float32,
        )
        return carry

    own[2].wait()
    own[3].wait()
    lax.fori_loop(0, atoms, build, 0, unroll=4)
    pack = 16

    def split(v):
        high = v.astype(jnp.bfloat16)
        return high, (v - high.astype(jnp.float32)).astype(jnp.bfloat16)

    def arrange(p, carry):
        for j in range(0, atoms, pack):
            cubes = [jnp.swapaxes(proj[j + i : j + i + 8, rows_at(p, 1), :], 0, 1) for i in range(0, pack, 8)]
            for y in range(rows):
                high, low = split(jnp.concatenate([cube[y] for cube in cubes], axis=0))
                parts_ref[p, j : j + pack, y * cols : (y + 1) * cols] = high
                parts_ref[p, atoms + j : atoms + j + pack, y * cols : (y + 1) * cols] = low
        return carry

    lax.fori_loop(0, chunk, arrange, 0, unroll=2)

    def products(p, total):
        return total + lax.dot_general(
            parts_ref[p], parts_ref[p], (((1,), (1,)), ((), ())), preferred_element_type=jnp.float32
        )

    total = lax.fori_loop(0, chunk, products, jnp.zeros((2 * atoms, 2 * atoms), jnp.float32), unroll=8)
    overlap[...] = total[:atoms, :atoms] + total[:atoms, atoms:] + total[atoms:, :atoms]

    apart = jnp.abs(
        lax.broadcasted_iota(jnp.int32, (cols, cols), 0) - lax.broadcasted_iota(jnp.int32, (cols, cols), 1)
    )
    band = jnp.zeros((cols, cols), jnp.float32)
    for d in range(1, RADIUS + 1):
        band = jnp.where(apart == d, stencil_weights[d], band)
    band_high, band_low = split(band)
    shift_ref[:cols, :cols] = band_high
    shift_ref[cols:, :cols] = band_high
    shift_ref[:cols, cols:] = band_low
    shift_ref[cols:, cols:] = jnp.zeros((cols, cols), jnp.bfloat16)

    def relayout(src, src_at, dst, dst_at, count):
        def at_plane(n, carry):
            cube = jnp.swapaxes(src[:, rows_at(src_at + n, 1), :], 0, 1)
            for y in range(rows):
                dst[dst_at + n, :, y * cols : (y + 1) * cols] = cube[y]
            return carry

        lax.fori_loop(0, count, at_plane, 0)

    wide = coef_mine.shape[-1]

    def cells(plane):
        return [plane[:, y * cols : (y + 1) * cols] for y in range(rows)]

    def stack(one, two, axis):
        return jnp.concatenate([one.astype(jnp.float32), two.astype(jnp.float32)], axis=axis).astype(jnp.bfloat16)

    def project(src, src_at, proj_at, count):
        total = jnp.zeros((2 * half, 2 * atoms), jnp.float32)
        for n in range(count):
            total = total + lax.dot_general(
                stack(*split(src[src_at + n]), 0), parts_ref[proj_at + n], (((1,), (1,)), ((), ())),
                preferred_element_type=jnp.float32,
            )
        return widen(total[:half, :atoms] + total[:half, atoms:] + total[half:, :atoms])

    def widen(result):
        if wide == atoms:
            return result
        return jnp.concatenate([result, jnp.zeros((half, wide - atoms), jnp.float32)], axis=1)

    def sum_across(k, first_plane, count):
        rows_all = jnp.concatenate(
            [cell for p in range(count) for cell in cells(field[k, RADIUS + first_plane + p])], axis=0
        )
        both_parts = lax.dot_general(
            jnp.concatenate(split(rows_all), axis=1), shift_ref[...], (((1,), (0,)), ((), ())),
            preferred_element_type=jnp.float32,
        )
        z = both_parts[:, :cols] + both_parts[:, cols:]
        for p in range(count):
            for y in range(rows):
                at = (p * rows + y) * half
                across[first_plane + p, :, y * cols : (y + 1) * cols] = z[at : at + half]

    def local_part(k, p, a, b, low=chunk, high=chunk):
        src = field.at[k]
        cell = cells(src[p + RADIUS])
        line = cells(across[p])
        ring = [None]
        for d in range(1, RADIUS + 1):
            near = [src[p + RADIUS + s * d] for s, room in ((1, high), (-1, low)) if d <= room]
            ring.append(near[0] + near[1] if len(near) == 2 else near[0] if near else None)
        weight = [-0.5 * a * w for w in stencil_weights]
        result = []
        for y in range(rows):
            v = cell[y]
            t = v * (a * pot[p, y : y + 1, :] + (3.0 * weight[0] + b)) + (-0.5 * a) * line[y]
            for d in range(1, RADIUS + 1):
                terms = [cell[y + s * d] for s in (1, -1) if 0 <= y + s * d < rows]
                if ring[d] is not None:
                    terms.append(ring[d][:, y * cols : (y + 1) * cols])
                if terms:
                    t = t + weight[d] * functools.reduce(jnp.add, terms)
            result.append(t)
        return result

    def store(k, p, tiles):
        for y in range(rows):
            field[k, p + RADIUS, :, y * cols : (y + 1) * cols] = tiles[y]

    def stored(k, p):
        return cells(field[k, p + RADIUS])

    cuts, early_cuts = 4, 3
    halo_slots, coef_slots = slots(2 * cuts * (DEGREE + 1)), slots(2 * (DEGREE + 1))

    def cut(g):
        return slice(g * (area // cuts), (g + 1) * (area // cuts))

    def halo_up(k, g):
        slot = halo_slots + 2 * (cuts * k + g)
        return remote(field.at[k, chunk : chunk + RADIUS, :, cut(g)], field.at[k, 0:RADIUS, :, cut(g)], slot, slot, up)

    def halo_down(k, g):
        slot = halo_slots + 2 * (cuts * k + g) + 1
        return remote(
            field.at[k, RADIUS : 2 * RADIUS, :, cut(g)],
            field.at[k, chunk + RADIUS : chunk + 2 * RADIUS, :, cut(g)], slot, slot, down,
        )

    def coef_up(k):
        slot = coef_slots + 2 * k
        return remote(coef_mine.at[k], coef_far.at[k, 0], slot, slot, up)

    def coef_down(k):
        slot = coef_slots + 2 * k + 1
        return remote(coef_mine.at[k], coef_far.at[k, 1], slot, slot, down)

    first_slots = slots(5)
    other_mine = coef_mine.at[DEGREE + 1]
    early = [
        (None, remote(other_mine, coef_first.at[0], first_slots, first_slots, partner)),
        (has_up, remote(coef_mine.at[0], coef_first.at[1], first_slots + 1, first_slots + 1, up)),
        (has_up, remote(other_mine, coef_first.at[2], first_slots + 2, first_slots + 2, up_other)),
        (has_down, remote(coef_mine.at[0], coef_first.at[3], first_slots + 3, first_slots + 3, down)),
        (has_down, remote(other_mine, coef_first.at[4], first_slots + 4, first_slots + 4, down_other)),
    ]

    own[1].wait()
    relayout(spare_raw, 0, spare, 0, planes)
    coef_mine[DEGREE + 1] = project(spare, 0, side * planes, planes)
    own[0].wait()
    relayout(raw, RADIUS + side * planes, field.at[0], RADIUS + side * planes, planes)
    coef_mine[0] = project(field.at[0], RADIUS + side * planes, side * planes, planes)
    for ready, copy in early:
        if ready is None:
            copy.start()
        else:
            pl.when(ready)(copy.start)

    def spread_of(weights):
        high, low = split(weights)
        return stack(stack(high, high, 1), stack(low, jnp.zeros_like(low), 1), 0)

    def add_nonlocal(k, spread, first_plane, count):
        for p in range(first_plane, first_plane + count):
            both_parts = lax.dot_general(
                spread, parts_ref[p], (((1,), (0,)), ((), ())), preferred_element_type=jnp.float32
            )
            field[k, p + RADIUS] = field[k, p + RADIUS] + (both_parts[:half] + both_parts[half:])

    for k in range(1, DEGREE + 1):
        pl.when(jnp.logical_not(has_down))(
            functools.partial(field.__setitem__, (k, slice(0, RADIUS)), jnp.zeros((RADIUS, half, area), jnp.float32))
        )
        pl.when(jnp.logical_not(has_up))(
            functools.partial(
                field.__setitem__, (k, slice(RADIUS + chunk, 2 * RADIUS + chunk)),
                jnp.zeros((RADIUS, half, area), jnp.float32),
            )
        )
    sum_across(0, side * planes, planes)
    own[4].wait()
    own[5].wait()
    swaps[0].wait_recv()
    relayout(raw, RADIUS + other * (chunk - RADIUS), field.at[0], RADIUS + other * (chunk - RADIUS), RADIUS)
    swaps[1].wait_recv()
    relayout(
        raw, 2 * RADIUS + other * (planes - RADIUS), field.at[0], 2 * RADIUS + other * (planes - RADIUS),
        planes - RADIUS,
    )
    sum_across(0, other * planes, planes)
    pot_swap.wait_recv()
    early[0][1].wait_recv()

    def wait_below():
        remote(
            states.at[pl.ds(0, half), rows_at(0, RADIUS)], raw.at[:, rows_at(0, RADIUS)], first, first, partner
        ).wait_recv()
        early[1][1].wait_recv()
        early[2][1].wait_recv()
        relayout(raw, 0, field.at[0], 0, RADIUS)

    def wait_above():
        remote(
            states.at[pl.ds(0, half), rows_at(0, RADIUS)], raw.at[:, rows_at(0, RADIUS)], first, first + 1, partner
        ).wait_recv()
        early[3][1].wait_recv()
        early[4][1].wait_recv()
        relayout(raw, RADIUS + chunk, field.at[0], RADIUS + chunk, RADIUS)

    def clear(at):
        def go():
            field[0, at : at + RADIUS] = jnp.zeros((RADIUS, half, area), jnp.float32)

        return go

    pl.when(has_down)(wait_below)
    pl.when(has_up)(wait_above)
    pl.when(jnp.logical_not(has_down))(clear(0))
    pl.when(jnp.logical_not(has_up))(clear(RADIUS + chunk))
    scale0 = 1.0 / filter_half
    total = coef_mine[0]
    for n in range(5):
        total = total + coef_first[n]
    spread0 = spread_of(total[:, :atoms] * strength_ref[...] * scale0)

    def whole(p, carry):
        store(1, p, local_part(0, p, scale0, -filter_centre * scale0))
        return carry

    lax.fori_loop(0, RADIUS, whole, 0)
    add_nonlocal(1, spread0, 0, RADIUS)
    for g in range(early_cuts):
        pl.when(has_down)(halo_down(1, g).start)
    lax.fori_loop(chunk - RADIUS, chunk, whole, 0)
    add_nonlocal(1, spread0, chunk - RADIUS, RADIUS)
    for g in range(early_cuts):
        pl.when(has_up)(halo_up(1, g).start)
    lax.fori_loop(RADIUS, chunk - RADIUS, whole, 0)
    add_nonlocal(1, spread0, RADIUS, chunk - 2 * RADIUS)

    def send_coefs(k):
        pl.when(has_up)(coef_up(k).start)
        pl.when(has_down)(coef_down(k).start)

    coef_mine[1] = project(field.at[1], RADIUS, 0, chunk)
    send_coefs(1)
    for g in range(early_cuts, cuts):
        pl.when(has_down)(halo_down(1, g).start)
        pl.when(has_up)(halo_up(1, g).start)

    def send_halos(k, g):
        pl.when(has_down)(halo_down(k, g).start)
        pl.when(has_up)(halo_up(k, g).start)

    def apply(k, final):
        scale = 1.0 if final else 2.0 / filter_half
        shift = 0.0 if final else -filter_centre * scale
        sum_across(k, 0, chunk)

        def with_last(p, tiles):
            if final:
                return tiles
            old = cells(field[k - 1, p + RADIUS])
            return [tiles[y] - old[y] for y in range(rows)]

        def inner(p, carry):
            store(k + 1, p, with_last(p, local_part(k, p, scale, shift)))
            return carry

        for n in range(RADIUS):
            for p, low, high in ((n, n, chunk), (chunk - 1 - n, chunk, n)):
                store(k + 1, p, with_last(p, local_part(k, p, scale, shift, low, high)))
        lax.fori_loop(RADIUS, chunk - RADIUS, inner, 0)

        ahead = None if final else project(field.at[k + 1], RADIUS, 0, chunk)
        pl.when(has_down)(coef_up(k).wait_recv)
        pl.when(has_up)(coef_down(k).wait_recv)
        coefs = coef_mine[k] + coef_far[k, 0] + coef_far[k, 1]
        weights = coefs[:, :atoms] * strength_ref[...] * scale
        spread = spread_of(weights)
        if not final:
            ahead = ahead + widen(
                lax.dot_general(
                    weights, overlap[...], (((1,), (0,)), ((), ())),
                    precision=lax.Precision.HIGHEST, preferred_element_type=jnp.float32,
                )
            )

        def add_halo(p, at, g, planes_in):
            tiles = None
            for w, plane in planes_in:
                term = (-0.5 * scale * w) * field[k, plane, :, cut(g)]
                tiles = term if tiles is None else tiles + term
            if not final:
                extra[at, :, cut(g)] = tiles
            field[k + 1, p + RADIUS, :, cut(g)] = field[k + 1, p + RADIUS, :, cut(g)] + tiles

        def edges():
            add_nonlocal(k + 1, spread, 0, RADIUS)
            add_nonlocal(k + 1, spread, chunk - RADIUS, RADIUS)

        def lower(g):
            pl.when(has_down)(halo_up(k, g).wait_recv)
            for p in range(RADIUS):
                add_halo(p, p, g, [(stencil_weights[d], RADIUS + p - d) for d in range(p + 1, RADIUS + 1)])

        def upper(g):
            pl.when(has_up)(halo_down(k, g).wait_recv)
            for n in range(RADIUS):
                p = chunk - 1 - n
                add_halo(
                    p, 2 * RADIUS - 1 - n, g,
                    [(stencil_weights[d], RADIUS + p + d) for d in range(n + 1, RADIUS + 1)],
                )

        def middle():
            add_nonlocal(k + 1, spread, RADIUS, chunk - 2 * RADIUS)

        return ahead, edges, lower, middle, upper

    def step(k, carry):
        ahead, edges, lower, middle, upper = apply(k, False)
        edges()
        for g in range(cuts):
            lower(g)
            upper(g)
            if g < early_cuts:
                send_halos(k + 1, g)
        coef_mine[k + 1] = (
            ahead + project(extra, 0, 0, RADIUS) + project(extra, RADIUS, chunk - RADIUS, RADIUS)
        )
        send_coefs(k + 1)
        for g in range(early_cuts, cuts):
            send_halos(k + 1, g)
        middle()
        return carry

    lax.fori_loop(1, DEGREE, step, 0)

    part = planes // bands
    shares = 2 * bands
    y_out, y_in, h_out, h_in = slots(shares), slots(shares), slots(shares), slots(shares)
    mine_at = me_b * 2 + side

    def share(which, q):
        src = field.at[DEGREE + which, RADIUS + q * part : RADIUS + (q + 1) * part]
        dst = both.at[which, :, group(mine_at)]
        is_mine = jnp.logical_and(me_b == q % bands, side == q // bands)
        away = remote(
            src, dst, (y_out, h_out)[which] + q, (y_in, h_in)[which] + mine_at, (q % bands, 2 * pair + q // bands)
        )
        return is_mine, away, pltpu.make_async_copy(src, dst, local.at[which])

    def send_share(which, q):
        is_mine, away, keep = share(which, q)
        pl.when(is_mine)(keep.start)
        pl.when(jnp.logical_not(is_mine))(away.start)

    def take_shares(which):
        for q in range(shares):
            sender = q
            is_mine = jnp.logical_and(me_b == sender // 2, side == sender % 2)
            src = field.at[DEGREE + which, RADIUS : RADIUS + part]
            dst = both.at[which, :, pl.ds(sender * half, half)]
            come = remote(src, dst, y_out, (y_in, h_in)[which] + sender, partner)
            pl.when(is_mine)(pltpu.make_async_copy(src, dst, local.at[which]).wait)
            pl.when(jnp.logical_not(is_mine))(come.wait_recv)

    def sent_shares(which):
        for q in range(shares):
            is_mine, away, keep = share(which, q)
            pl.when(jnp.logical_not(is_mine))(away.wait_send)

    for q in range(shares):
        send_share(0, q)
    ahead, edges, lower, middle, upper = apply(DEGREE, True)
    inside = [q for q in range(shares) if q * part >= RADIUS and (q + 1) * part <= chunk - RADIUS]
    middle()
    for q in inside:
        send_share(1, q)
    edges()
    for g in range(cuts):
        lower(g)
    for q in range(shares // 2):
        if q not in inside:
            send_share(1, q)
    for g in range(cuts):
        upper(g)
    for q in range(shares // 2, shares):
        if q not in inside:
            send_share(1, q)

    back_slot = slots(bands)
    my_planes = back_y.at[pl.ds(me_b * part, part)]

    def gathered_of(b):
        return both.at[0, :, group(b * 2 + other)]

    backs = [
        remote(
            gathered_of(lax.rem(me_b + d, bands)), my_planes, back_slot + d, back_slot + d,
            (lax.rem(me_b + d, bands), me_g),
        )
        for d in range(1, bands)
    ]
    backs.append(pltpu.make_async_copy(gathered_of(me_b), my_planes, local.at[2]))

    def start_backs():
        for copy in backs:
            copy.start()

    def inner_rows(left, right):
        return lax.dot_general(
            left, right, (((1,), (1,)), ((), ())),
            precision=lax.Precision.HIGH, preferred_element_type=jnp.float32,
        )

    states_all = bands * 2 * half
    for copy in swaps + [pot_swap, early[0][1]]:
        copy.wait_send()
    for copy in fringes:
        pl.when(can)(copy.wait_send)
    for ready, copy in early[1:]:
        pl.when(ready)(copy.wait_send)
    for k in range(1, DEGREE + 1):
        copies = [(has_up, coef_up(k)), (has_down, coef_down(k))]
        for g in range(cuts):
            copies += [(has_up, halo_up(k, g)), (has_down, halo_down(k, g))]
        for ready, copy in copies:
            pl.when(ready)(copy.wait_send)
    sent_shares(0)
    sent_shares(1)
    def put_out(src, src_at, g):
        def at_plane(p, carry):
            cube = jnp.stack(cells(src[src_at + p]))
            out_ref[group(g), rows_at(p, 1), :] = jnp.swapaxes(cube, 0, 1)
            return carry

        lax.fori_loop(0, planes, at_plane, 0)

    put_out(field.at[DEGREE], RADIUS + side * planes, side)
    take_shares(0)
    total = inner_rows(both[0, 0], both[0, 0])
    for i in range(1, part):
        total = total + inner_rows(both[0, i], both[0, i])
    prod[:, :states_all] = total
    take_shares(1)
    total = inner_rows(both[1, 0], both[0, 0])
    for i in range(1, part):
        total = total + inner_rows(both[1, i], both[0, i])
    prod[:, states_all:] = total

    rows_of = 2 * half
    r_slot, g_slot = slots(bands), slots(slabs)
    band_copies = []
    for d in range(1, bands):
        to_b = lax.rem(me_b + d, bands)
        copy = remote(
            prod.at[pl.ds(pl.multiple_of(to_b * rows_of, rows_of), rows_of)], band_sum.at[d],
            r_slot + d, r_slot + d, (to_b, me_g),
        )
        copy.start()
        band_copies.append(copy)
    start_backs()
    total = prod[pl.ds(pl.multiple_of(me_b * rows_of, rows_of), rows_of), :]
    for copy in band_copies:
        copy.wait_recv()
    for d in range(1, bands):
        total = total + band_sum[d]
    mine[...] = total
    grid_copies = []
    for d in range(1, slabs):
        copy = remote(mine, grid_sum.at[d], g_slot + d, g_slot + d, (me_b, lax.rem(me_g + d, slabs)))
        copy.start()
        grid_copies.append(copy)

    for copy in backs[:-1]:
        copy.wait_recv()
    backs[-1].wait()
    put_out(back_y, 0, other)
    for copy in backs[:-1] + band_copies:
        copy.wait_send()
    for copy in grid_copies:
        copy.wait_recv()
    for d in range(1, slabs):
        total = total + grid_sum[d]
    total = total / total_points
    gram_ref[...] = total[:, :states_all]
    ham_ref[...] = total[:, states_all:]

    for copy in grid_copies:
        copy.wait_send()


def per_device(bands, slabs, states, potential, proj_index, proj_value, proj_strength):
    state_count, planes, rows, cols = states.shape
    area = rows * cols
    points = planes * area
    atoms, support = proj_index.shape
    half = state_count // 2
    chunk = 2 * planes
    wide = -(-atoms // LANES) * LANES
    all_states = bands * state_count
    strength = proj_strength.reshape(1, atoms)
    slots = 5 + 10 * (DEGREE + 1) + 5 + 10 * bands + slabs
    vmem, hbm = pl.BlockSpec(memory_space=pltpu.VMEM), pl.BlockSpec(memory_space=pltpu.HBM)
    f32 = jnp.float32
    out, gram, ham = pl.pallas_call(
        functools.partial(
            kernel, bands, slabs, planes, rows, cols, atoms, float(points * slabs)
        ),
        out_shape=(
            jax.ShapeDtypeStruct((state_count, planes * rows, cols), f32),
            jax.ShapeDtypeStruct((state_count, all_states), f32),
            jax.ShapeDtypeStruct((state_count, all_states), f32),
        ),
        in_specs=[hbm, hbm, hbm, hbm, hbm],
        out_specs=(vmem, vmem, vmem),
        scratch_shapes=[
            pltpu.VMEM((half, (chunk + 2 * RADIUS) * rows, cols), f32),
            pltpu.VMEM((half, planes * rows, cols), f32),
            pltpu.VMEM((DEGREE + 2, chunk + 2 * RADIUS, half, area), f32),
            pltpu.VMEM((planes, half, area), f32),
            pltpu.VMEM((chunk, rows, cols), f32),
            pltpu.VMEM((atoms, support), jnp.int32),
            pltpu.VMEM((atoms, support), f32),
            pltpu.VMEM((1, atoms), f32),
            pltpu.VMEM((atoms, chunk * rows, cols), f32),
            pltpu.VMEM((chunk, 2 * atoms, area), jnp.bfloat16),
            pltpu.VMEM((2 * cols, 2 * cols), jnp.bfloat16),
            pltpu.VMEM((chunk, half, area), f32),
            pltpu.VMEM((DEGREE + 2, half, wide), f32),
            pltpu.VMEM((DEGREE + 1, 2, half, wide), f32),
            pltpu.VMEM((5, half, wide), f32),
            pltpu.VMEM((atoms, atoms), f32),
            pltpu.VMEM((2 * RADIUS, half, area), f32),
            pltpu.VMEM((planes, half, area), f32),
            pltpu.VMEM((2, planes // bands, all_states, area), f32),
            pltpu.VMEM((all_states, 2 * all_states), f32),
            pltpu.VMEM((bands, state_count, 2 * all_states), f32),
            pltpu.VMEM((state_count, 2 * all_states), f32),
            pltpu.VMEM((slabs, state_count, 2 * all_states), f32),
            pltpu.SemaphoreType.DMA((slots,)),
            pltpu.SemaphoreType.DMA((slots,)),
            pltpu.SemaphoreType.DMA((6,)),
        ],
        compiler_params=pltpu.CompilerParams(
            collective_id=0, has_side_effects=True, vmem_limit_bytes=48 * 1024 * 1024
        ),
    )(*(pltpu.with_memory_space_constraint(x, pltpu.HBM) for x in (states.reshape(state_count, planes * rows, cols), potential, proj_index, proj_value, strength)))

    def place(*refs):
        moves = [pltpu.make_async_copy(refs[n], refs[3 + n], refs[6].at[n]) for n in range(3)]
        for move in moves:
            move.start()
        for move in moves:
            move.wait()

    out, gram, ham = pl.pallas_call(
        place,
        out_shape=tuple(jax.ShapeDtypeStruct(x.shape, f32) for x in (out, gram, ham)),
        in_specs=[vmem] * 3,
        out_specs=(hbm,) * 3,
        scratch_shapes=[pltpu.SemaphoreType.DMA((3,))],
    )(*(pltpu.with_memory_space_constraint(x, pltpu.VMEM) for x in (out, gram, ham)))
    return out.reshape(states.shape), gram, ham


def solution(mesh):
    in_specs = (P("band", "grid", None, None), P("grid", None, None), P(), P(), P())
    out_specs = (P("band", "grid", None, None), P("band", None), P("band", None))
    return jax.shard_map(
        functools.partial(per_device, mesh.shape["band"], mesh.shape["grid"]),
        mesh=mesh, in_specs=in_specs, out_specs=out_specs, check_vma=False,
    )
```

```python
import functools

import jax
import jax.numpy as jnp
from jax import lax
from jax.experimental import pallas as pl
from jax.experimental.pallas import tpu as pltpu
from jax.sharding import PartitionSpec as P

RADIUS = 4
DEGREE = 4
LANES = 128
MESH = pl.DeviceIdType.MESH

stencil_weights = (-205.0 / 72.0, 1.6, -0.2, 8.0 / 315.0, -1.0 / 560.0)
filter_centre = 10.0
filter_half = 6.0


def kernel(
    bands, slabs, planes, rows, cols, atoms, total_points,
    states, potential, index_in, value_in, strength_in,
    out_ref, gram_ref, ham_ref,
    raw, spare_raw, field, spare, pot, index_ref, value_ref, strength_ref, proj, parts_ref, shift_ref, across,
    coef_mine, coef_far, coef_first, overlap, extra, back_y, both, prod, band_sum, mine, grid_sum,
    send, recv, local,
):
    half = states.shape[0] // 2
    area = rows * cols
    chunk = 2 * planes
    me_b, me_g = lax.axis_index("band"), lax.axis_index("grid")
    pair, side = me_g // 2, me_g % 2
    other = 1 - side
    last_pair = slabs // 2 - 1
    has_down, has_up = pair > 0, pair < last_pair
    counter = [0]

    def remote(src, dst, out_slot, in_slot, where):
        return pltpu.make_async_remote_copy(
            src_ref=src, dst_ref=dst, send_sem=send.at[out_slot], recv_sem=recv.at[in_slot],
            device_id=where, device_id_type=MESH,
        )

    def slots(count):
        first = counter[0]
        counter[0] += count
        return first

    def rows_at(plane, count):
        return pl.ds(pl.multiple_of(plane * rows, rows), count * rows)

    def group(g):
        return pl.ds(pl.multiple_of(g * half, half), half)

    partner = (me_b, 2 * pair + other)
    up, down = (me_b, me_g + 2), (me_b, me_g - 2)
    up_other, down_other = (me_b, 2 * pair + 2 + other), (me_b, 2 * pair - 2 + other)
    crossing = [
        (lax.rem(me_b + d, bands), 2 * pair + lax.rem(side + e, 2)) for d in range(1, bands) for e in range(2)
    ]
    barrier = pltpu.get_barrier_semaphore()

    def greet(where):
        pl.semaphore_signal(barrier, inc=1, device_id=where, device_id_type=MESH)

    def greet_pair(one, two):
        greet(one)
        greet(two)

    coef_far[...] = jnp.zeros_like(coef_far)
    coef_first[...] = jnp.zeros_like(coef_first)

    if last_pair > DEGREE:
        for d in range(1, slabs):
            greet((me_b, lax.rem(me_g + d, slabs)))
        expected = len(crossing) + slabs - 1
    else:
        greet(partner)
        pl.when(has_up)(lambda: greet_pair(up, up_other))
        pl.when(has_down)(lambda: greet_pair(down, down_other))
        expected = len(crossing) + 1 + 2 * (has_up.astype(jnp.int32) + has_down.astype(jnp.int32))
    for peer in crossing:
        greet(peer)

    own = [
        pltpu.make_async_copy(states.at[group(side)], raw.at[:, rows_at(RADIUS + side * planes, planes)], local.at[0]),
        pltpu.make_async_copy(states.at[group(other)], spare_raw, local.at[1]),
        pltpu.make_async_copy(index_in, index_ref, local.at[2]),
        pltpu.make_async_copy(value_in, value_ref, local.at[3]),
        pltpu.make_async_copy(potential, pot.at[pl.ds(side * planes, planes)], local.at[4]),
        pltpu.make_async_copy(strength_in, strength_ref, local.at[5]),
    ]
    for copy in own:
        copy.start()

    pl.semaphore_wait(barrier, expected)

    first = slots(5)
    toward, can = 2 * side - 1, jnp.where(side == 1, pair < last_pair, pair > 0)
    outer_at, inner_at = side * (planes - RADIUS), other * RADIUS
    fringes = [
        remote(
            states.at[pl.ds(h * half, half), rows_at(outer_at, RADIUS)],
            raw.at[:, rows_at(other * (RADIUS + chunk), RADIUS)],
            first + h, first + other, (me_b, 2 * (pair + toward) + h),
        )
        for h in range(2)
    ]
    swaps = [
        remote(
            states.at[group(other), rows_at(start, count)], raw.at[:, rows_at(RADIUS + side * planes + start, count)],
            first + 2 + n, first + 2 + n, partner,
        )
        for n, (start, count) in enumerate(((outer_at, RADIUS), (inner_at, planes - RADIUS)))
    ]
    pot_swap = remote(potential, pot.at[pl.ds(side * planes, planes)], first + 4, first + 4, partner)

    def start_fringes():
        for copy in fringes:
            copy.start()

    pl.when(can)(start_fringes)
    for copy in swaps:
        copy.start()
    pot_swap.start()

    points = index_ref.shape[1]
    row_iota = lax.broadcasted_iota(jnp.int32, (chunk * rows, points), 0) + pair * (chunk * rows)
    col_iota = lax.broadcasted_iota(jnp.int32, (cols, points), 0)

    def build(a, carry):
        idx = index_ref[pl.ds(a, 1), :]
        row = lax.div(idx, cols)
        here = row_iota == row
        onehot = jnp.where(col_iota == idx - row * cols, 1.0, 0.0).astype(jnp.bfloat16)
        rest = value_ref[pl.ds(a, 1), :]
        parts = []
        for _ in range(3):
            part = rest.astype(jnp.bfloat16).astype(jnp.float32)
            rest = rest - part
            parts.append(jnp.where(here, part, 0.0).astype(jnp.bfloat16))
        proj[a] = lax.dot_general(
            jnp.concatenate(parts, axis=1), jnp.concatenate([onehot] * 3, axis=1), (((1,), (1,)), ((), ())),
            preferred_element_type=jnp.float32,
        )
        return carry

    own[2].wait()
    own[3].wait()
    lax.fori_loop(0, atoms, build, 0, unroll=4)
    pack = 16

    def split(v):
        high = v.astype(jnp.bfloat16)
        return high, (v - high.astype(jnp.float32)).astype(jnp.bfloat16)

    def arrange(p, carry):
        for j in range(0, atoms, pack):
            cubes = [jnp.swapaxes(proj[j + i : j + i + 8, rows_at(p, 1), :], 0, 1) for i in range(0, pack, 8)]
            for y in range(rows):
                high, low = split(jnp.concatenate([cube[y] for cube in cubes], axis=0))
                parts_ref[p, j : j + pack, y * cols : (y + 1) * cols] = high
                parts_ref[p, atoms + j : atoms + j + pack, y * cols : (y + 1) * cols] = low
        return carry

    lax.fori_loop(0, chunk, arrange, 0, unroll=2)

    def products(p, total):
        return total + lax.dot_general(
            parts_ref[p], parts_ref[p], (((1,), (1,)), ((), ())), preferred_element_type=jnp.float32
        )

    total = lax.fori_loop(0, chunk, products, jnp.zeros((2 * atoms, 2 * atoms), jnp.float32), unroll=8)
    overlap[...] = total[:atoms, :atoms] + total[:atoms, atoms:] + total[atoms:, :atoms]

    apart = jnp.abs(
        lax.broadcasted_iota(jnp.int32, (cols, cols), 0) - lax.broadcasted_iota(jnp.int32, (cols, cols), 1)
    )
    band = jnp.zeros((cols, cols), jnp.float32)
    for d in range(1, RADIUS + 1):
        band = jnp.where(apart == d, stencil_weights[d], band)
    band_high, band_low = split(band)
    shift_ref[:cols, :cols] = band_high
    shift_ref[cols:, :cols] = band_high
    shift_ref[:cols, cols:] = band_low
    shift_ref[cols:, cols:] = jnp.zeros((cols, cols), jnp.bfloat16)

    def relayout(src, src_at, dst, dst_at, count):
        def at_plane(n, carry):
            cube = jnp.swapaxes(src[:, rows_at(src_at + n, 1), :], 0, 1)
            for y in range(rows):
                dst[dst_at + n, :, y * cols : (y + 1) * cols] = cube[y]
            return carry

        lax.fori_loop(0, count, at_plane, 0)

    wide = coef_mine.shape[-1]

    def cells(plane):
        return [plane[:, y * cols : (y + 1) * cols] for y in range(rows)]

    def stack(one, two, axis):
        return jnp.concatenate([one.astype(jnp.float32), two.astype(jnp.float32)], axis=axis).astype(jnp.bfloat16)

    def project(src, src_at, proj_at, count):
        total = jnp.zeros((2 * half, 2 * atoms), jnp.float32)
        for n in range(count):
            total = total + lax.dot_general(
                stack(*split(src[src_at + n]), 0), parts_ref[proj_at + n], (((1,), (1,)), ((), ())),
                preferred_element_type=jnp.float32,
            )
        return widen(total[:half, :atoms] + total[:half, atoms:] + total[half:, :atoms])

    def widen(result):
        if wide == atoms:
            return result
        return jnp.concatenate([result, jnp.zeros((half, wide - atoms), jnp.float32)], axis=1)

    def sum_across(k, first_plane, count):
        rows_all = jnp.concatenate(
            [cell for p in range(count) for cell in cells(field[k, RADIUS + first_plane + p])], axis=0
        )
        both_parts = lax.dot_general(
            jnp.concatenate(split(rows_all), axis=1), shift_ref[...], (((1,), (0,)), ((), ())),
            preferred_element_type=jnp.float32,
        )
        z = both_parts[:, :cols] + both_parts[:, cols:]
        for p in range(count):
            for y in range(rows):
                at = (p * rows + y) * half
                across[first_plane + p, :, y * cols : (y + 1) * cols] = z[at : at + half]

    def local_part(k, p, a, b, low=chunk, high=chunk):
        src = field.at[k]
        cell = cells(src[p + RADIUS])
        line = cells(across[p])
        ring = [None]
        for d in range(1, RADIUS + 1):
            near = [src[p + RADIUS + s * d] for s, room in ((1, high), (-1, low)) if d <= room]
            ring.append(near[0] + near[1] if len(near) == 2 else near[0] if near else None)
        weight = [-0.5 * a * w for w in stencil_weights]
        result = []
        for y in range(rows):
            v = cell[y]
            t = v * (a * pot[p, y : y + 1, :] + (3.0 * weight[0] + b)) + (-0.5 * a) * line[y]
            for d in range(1, RADIUS + 1):
                terms = [cell[y + s * d] for s in (1, -1) if 0 <= y + s * d < rows]
                if ring[d] is not None:
                    terms.append(ring[d][:, y * cols : (y + 1) * cols])
                if terms:
                    t = t + weight[d] * functools.reduce(jnp.add, terms)
            result.append(t)
        return result

    def store(k, p, tiles):
        for y in range(rows):
            field[k, p + RADIUS, :, y * cols : (y + 1) * cols] = tiles[y]

    def stored(k, p):
        return cells(field[k, p + RADIUS])

    cuts, early_cuts = 4, 3
    halo_slots, coef_slots = slots(2 * cuts * (DEGREE + 1)), slots(2 * (DEGREE + 1))

    def cut(g):
        return slice(g * (area // cuts), (g + 1) * (area // cuts))

    def halo_up(k, g):
        slot = halo_slots + 2 * (cuts * k + g)
        return remote(field.at[k, chunk : chunk + RADIUS, :, cut(g)], field.at[k, 0:RADIUS, :, cut(g)], slot, slot, up)

    def halo_down(k, g):
        slot = halo_slots + 2 * (cuts * k + g) + 1
        return remote(
            field.at[k, RADIUS : 2 * RADIUS, :, cut(g)],
            field.at[k, chunk + RADIUS : chunk + 2 * RADIUS, :, cut(g)], slot, slot, down,
        )

    def coef_up(k):
        slot = coef_slots + 2 * k
        return remote(coef_mine.at[k], coef_far.at[k, 0], slot, slot, up)

    def coef_down(k):
        slot = coef_slots + 2 * k + 1
        return remote(coef_mine.at[k], coef_far.at[k, 1], slot, slot, down)

    first_slots = slots(5)
    other_mine = coef_mine.at[DEGREE + 1]
    early = [
        (None, remote(other_mine, coef_first.at[0], first_slots, first_slots, partner)),
        (has_up, remote(coef_mine.at[0], coef_first.at[1], first_slots + 1, first_slots + 1, up)),
        (has_up, remote(other_mine, coef_first.at[2], first_slots + 2, first_slots + 2, up_other)),
        (has_down, remote(coef_mine.at[0], coef_first.at[3], first_slots + 3, first_slots + 3, down)),
        (has_down, remote(other_mine, coef_first.at[4], first_slots + 4, first_slots + 4, down_other)),
    ]

    own[1].wait()
    relayout(spare_raw, 0, spare, 0, planes)
    coef_mine[DEGREE + 1] = project(spare, 0, side * planes, planes)
    own[0].wait()
    relayout(raw, RADIUS + side * planes, field.at[0], RADIUS + side * planes, planes)
    coef_mine[0] = project(field.at[0], RADIUS + side * planes, side * planes, planes)
    for ready, copy in early:
        if ready is None:
            copy.start()
        else:
            pl.when(ready)(copy.start)

    def spread_of(weights):
        high, low = split(weights)
        return stack(stack(high, high, 1), stack(low, jnp.zeros_like(low), 1), 0)

    def add_nonlocal(k, spread, first_plane, count):
        for p in range(first_plane, first_plane + count):
            both_parts = lax.dot_general(
                spread, parts_ref[p], (((1,), (0,)), ((), ())), preferred_element_type=jnp.float32
            )
            field[k, p + RADIUS] = field[k, p + RADIUS] + (both_parts[:half] + both_parts[half:])

    for k in range(1, DEGREE + 1):
        pl.when(jnp.logical_not(has_down))(
            functools.partial(field.__setitem__, (k, slice(0, RADIUS)), jnp.zeros((RADIUS, half, area), jnp.float32))
        )
        pl.when(jnp.logical_not(has_up))(
            functools.partial(
                field.__setitem__, (k, slice(RADIUS + chunk, 2 * RADIUS + chunk)),
                jnp.zeros((RADIUS, half, area), jnp.float32),
            )
        )
    sum_across(0, side * planes, planes)
    own[4].wait()
    own[5].wait()
    def wait_below():
        remote(
            states.at[pl.ds(0, half), rows_at(0, RADIUS)], raw.at[:, rows_at(0, RADIUS)], first, first, partner
        ).wait_recv()
        early[1][1].wait_recv()
        early[2][1].wait_recv()
        relayout(raw, 0, field.at[0], 0, RADIUS)

    def wait_above():
        remote(
            states.at[pl.ds(0, half), rows_at(0, RADIUS)], raw.at[:, rows_at(0, RADIUS)], first, first + 1, partner
        ).wait_recv()
        early[3][1].wait_recv()
        early[4][1].wait_recv()
        relayout(raw, RADIUS + chunk, field.at[0], RADIUS + chunk, RADIUS)

    pl.when(has_down)(wait_below)
    pl.when(has_up)(wait_above)
    swaps[0].wait_recv()
    relayout(raw, RADIUS + other * (chunk - RADIUS), field.at[0], RADIUS + other * (chunk - RADIUS), RADIUS)
    swaps[1].wait_recv()
    relayout(
        raw, 2 * RADIUS + other * (planes - RADIUS), field.at[0], 2 * RADIUS + other * (planes - RADIUS),
        planes - RADIUS,
    )
    sum_across(0, other * planes, planes)
    pot_swap.wait_recv()
    early[0][1].wait_recv()

    def clear(at):
        def go():
            field[0, at : at + RADIUS] = jnp.zeros((RADIUS, half, area), jnp.float32)

        return go

    pl.when(jnp.logical_not(has_down))(clear(0))
    pl.when(jnp.logical_not(has_up))(clear(RADIUS + chunk))
    scale0 = 1.0 / filter_half
    total = coef_mine[0]
    for n in range(5):
        total = total + coef_first[n]
    spread0 = spread_of(total[:, :atoms] * strength_ref[...] * scale0)

    def whole(p, carry):
        store(1, p, local_part(0, p, scale0, -filter_centre * scale0))
        return carry

    lax.fori_loop(0, RADIUS, whole, 0)
    add_nonlocal(1, spread0, 0, RADIUS)
    for g in range(early_cuts):
        pl.when(has_down)(halo_down(1, g).start)
    lax.fori_loop(chunk - RADIUS, chunk, whole, 0)
    add_nonlocal(1, spread0, chunk - RADIUS, RADIUS)
    for g in range(early_cuts):
        pl.when(has_up)(halo_up(1, g).start)
    lax.fori_loop(RADIUS, chunk - RADIUS, whole, 0)
    add_nonlocal(1, spread0, RADIUS, chunk - 2 * RADIUS)

    def send_coefs(k):
        pl.when(has_up)(coef_up(k).start)
        pl.when(has_down)(coef_down(k).start)

    coef_mine[1] = project(field.at[1], RADIUS, 0, chunk)
    send_coefs(1)
    for g in range(early_cuts, cuts):
        pl.when(has_down)(halo_down(1, g).start)
        pl.when(has_up)(halo_up(1, g).start)

    def send_halos(k, g):
        pl.when(has_down)(halo_down(k, g).start)
        pl.when(has_up)(halo_up(k, g).start)

    def apply(k, final):
        scale = 1.0 if final else 2.0 / filter_half
        shift = 0.0 if final else -filter_centre * scale
        sum_across(k, 0, chunk)

        def with_last(p, tiles):
            if final:
                return tiles
            old = cells(field[k - 1, p + RADIUS])
            return [tiles[y] - old[y] for y in range(rows)]

        def inner(p, carry):
            store(k + 1, p, with_last(p, local_part(k, p, scale, shift)))
            return carry

        for n in range(RADIUS):
            for p, low, high in ((n, n, chunk), (chunk - 1 - n, chunk, n)):
                store(k + 1, p, with_last(p, local_part(k, p, scale, shift, low, high)))
        lax.fori_loop(RADIUS, chunk - RADIUS, inner, 0)

        ahead = None if final else project(field.at[k + 1], RADIUS, 0, chunk)
        pl.when(has_down)(coef_up(k).wait_recv)
        pl.when(has_up)(coef_down(k).wait_recv)
        coefs = coef_mine[k] + coef_far[k, 0] + coef_far[k, 1]
        weights = coefs[:, :atoms] * strength_ref[...] * scale
        spread = spread_of(weights)
        if not final:
            ahead = ahead + widen(
                lax.dot_general(
                    weights, overlap[...], (((1,), (0,)), ((), ())),
                    precision=lax.Precision.HIGHEST, preferred_element_type=jnp.float32,
                )
            )

        def add_halo(p, at, g, planes_in):
            tiles = None
            for w, plane in planes_in:
                term = (-0.5 * scale * w) * field[k, plane, :, cut(g)]
                tiles = term if tiles is None else tiles + term
            if not final:
                extra[at, :, cut(g)] = tiles
            field[k + 1, p + RADIUS, :, cut(g)] = field[k + 1, p + RADIUS, :, cut(g)] + tiles

        def edges():
            add_nonlocal(k + 1, spread, 0, RADIUS)
            add_nonlocal(k + 1, spread, chunk - RADIUS, RADIUS)

        def lower(g):
            pl.when(has_down)(halo_up(k, g).wait_recv)
            for p in range(RADIUS):
                add_halo(p, p, g, [(stencil_weights[d], RADIUS + p - d) for d in range(p + 1, RADIUS + 1)])

        def upper(g):
            pl.when(has_up)(halo_down(k, g).wait_recv)
            for n in range(RADIUS):
                p = chunk - 1 - n
                add_halo(
                    p, 2 * RADIUS - 1 - n, g,
                    [(stencil_weights[d], RADIUS + p + d) for d in range(n + 1, RADIUS + 1)],
                )

        def middle():
            add_nonlocal(k + 1, spread, RADIUS, chunk - 2 * RADIUS)

        return ahead, edges, lower, middle, upper

    def step(k, carry):
        ahead, edges, lower, middle, upper = apply(k, False)
        edges()
        for g in range(cuts):
            lower(g)
            upper(g)
            if g < early_cuts:
                send_halos(k + 1, g)
        coef_mine[k + 1] = (
            ahead + project(extra, 0, 0, RADIUS) + project(extra, RADIUS, chunk - RADIUS, RADIUS)
        )
        send_coefs(k + 1)
        for g in range(early_cuts, cuts):
            send_halos(k + 1, g)
        middle()
        return carry

    lax.fori_loop(1, DEGREE, step, 0)

    part = planes // bands
    shares = 2 * bands
    y_out, y_in, h_out, h_in = slots(shares), slots(shares), slots(shares), slots(shares)
    mine_at = me_b * 2 + side

    def share(which, q):
        src = field.at[DEGREE + which, RADIUS + q * part : RADIUS + (q + 1) * part]
        dst = both.at[which, :, group(mine_at)]
        is_mine = jnp.logical_and(me_b == q % bands, side == q // bands)
        away = remote(
            src, dst, (y_out, h_out)[which] + q, (y_in, h_in)[which] + mine_at, (q % bands, 2 * pair + q // bands)
        )
        return is_mine, away, pltpu.make_async_copy(src, dst, local.at[which])

    def send_share(which, q):
        is_mine, away, keep = share(which, q)
        pl.when(is_mine)(keep.start)
        pl.when(jnp.logical_not(is_mine))(away.start)

    def take_shares(which):
        for q in range(shares):
            sender = q
            is_mine = jnp.logical_and(me_b == sender // 2, side == sender % 2)
            src = field.at[DEGREE + which, RADIUS : RADIUS + part]
            dst = both.at[which, :, pl.ds(sender * half, half)]
            come = remote(src, dst, y_out, (y_in, h_in)[which] + sender, partner)
            pl.when(is_mine)(pltpu.make_async_copy(src, dst, local.at[which]).wait)
            pl.when(jnp.logical_not(is_mine))(come.wait_recv)

    def sent_shares(which):
        for q in range(shares):
            is_mine, away, keep = share(which, q)
            pl.when(jnp.logical_not(is_mine))(away.wait_send)

    for q in range(shares):
        send_share(0, q)
    ahead, edges, lower, middle, upper = apply(DEGREE, True)
    inside = [q for q in range(shares) if q * part >= RADIUS and (q + 1) * part <= chunk - RADIUS]
    middle()
    for q in inside:
        send_share(1, q)
    edges()
    for g in range(cuts):
        lower(g)
    for q in range(shares // 2):
        if q not in inside:
            send_share(1, q)
    for g in range(cuts):
        upper(g)
    for q in range(shares // 2, shares):
        if q not in inside:
            send_share(1, q)

    back_slot = slots(bands)
    my_planes = back_y.at[pl.ds(me_b * part, part)]

    def gathered_of(b):
        return both.at[0, :, group(b * 2 + other)]

    backs = [
        remote(
            gathered_of(lax.rem(me_b + d, bands)), my_planes, back_slot + d, back_slot + d,
            (lax.rem(me_b + d, bands), me_g),
        )
        for d in range(1, bands)
    ]
    backs.append(pltpu.make_async_copy(gathered_of(me_b), my_planes, local.at[2]))

    def start_backs():
        for copy in backs:
            copy.start()

    def inner_rows(left, right):
        return lax.dot_general(
            left, right, (((1,), (1,)), ((), ())),
            precision=lax.Precision.HIGH, preferred_element_type=jnp.float32,
        )

    states_all = bands * 2 * half
    for copy in swaps + [pot_swap, early[0][1]]:
        copy.wait_send()
    for copy in fringes:
        pl.when(can)(copy.wait_send)
    for ready, copy in early[1:]:
        pl.when(ready)(copy.wait_send)
    for k in range(1, DEGREE + 1):
        copies = [(has_up, coef_up(k)), (has_down, coef_down(k))]
        for g in range(cuts):
            copies += [(has_up, halo_up(k, g)), (has_down, halo_down(k, g))]
        for ready, copy in copies:
            pl.when(ready)(copy.wait_send)
    sent_shares(0)
    sent_shares(1)
    def put_out(src, src_at, g):
        def at_plane(p, carry):
            cube = jnp.stack(cells(src[src_at + p]))
            out_ref[group(g), rows_at(p, 1), :] = jnp.swapaxes(cube, 0, 1)
            return carry

        lax.fori_loop(0, planes, at_plane, 0)

    put_out(field.at[DEGREE], RADIUS + side * planes, side)
    take_shares(0)
    total = inner_rows(both[0, 0], both[0, 0])
    for i in range(1, part):
        total = total + inner_rows(both[0, i], both[0, i])
    prod[:, :states_all] = total
    take_shares(1)
    total = inner_rows(both[1, 0], both[0, 0])
    for i in range(1, part):
        total = total + inner_rows(both[1, i], both[0, i])
    prod[:, states_all:] = total

    rows_of = 2 * half
    r_slot, g_slot = slots(bands), slots(slabs)
    band_copies = []
    for d in range(1, bands):
        to_b = lax.rem(me_b + d, bands)
        copy = remote(
            prod.at[pl.ds(pl.multiple_of(to_b * rows_of, rows_of), rows_of)], band_sum.at[d],
            r_slot + d, r_slot + d, (to_b, me_g),
        )
        copy.start()
        band_copies.append(copy)
    start_backs()
    total = prod[pl.ds(pl.multiple_of(me_b * rows_of, rows_of), rows_of), :]
    for copy in band_copies:
        copy.wait_recv()
    for d in range(1, bands):
        total = total + band_sum[d]
    mine[...] = total
    grid_copies = []
    for d in range(1, slabs):
        copy = remote(mine, grid_sum.at[d], g_slot + d, g_slot + d, (me_b, lax.rem(me_g + d, slabs)))
        copy.start()
        grid_copies.append(copy)

    for copy in backs[:-1]:
        copy.wait_recv()
    backs[-1].wait()
    put_out(back_y, 0, other)
    for copy in backs[:-1] + band_copies:
        copy.wait_send()
    for copy in grid_copies:
        copy.wait_recv()
    for d in range(1, slabs):
        total = total + grid_sum[d]
    total = total / total_points
    gram_ref[...] = total[:, :states_all]
    ham_ref[...] = total[:, states_all:]

    for copy in grid_copies:
        copy.wait_send()


def per_device(bands, slabs, states, potential, proj_index, proj_value, proj_strength):
    state_count, planes, rows, cols = states.shape
    area = rows * cols
    points = planes * area
    atoms, support = proj_index.shape
    half = state_count // 2
    chunk = 2 * planes
    wide = -(-atoms // LANES) * LANES
    all_states = bands * state_count
    strength = proj_strength.reshape(1, atoms)
    slots = 5 + 10 * (DEGREE + 1) + 5 + 10 * bands + slabs
    vmem, hbm = pl.BlockSpec(memory_space=pltpu.VMEM), pl.BlockSpec(memory_space=pltpu.HBM)
    f32 = jnp.float32
    out, gram, ham = pl.pallas_call(
        functools.partial(
            kernel, bands, slabs, planes, rows, cols, atoms, float(points * slabs)
        ),
        out_shape=(
            jax.ShapeDtypeStruct((state_count, planes * rows, cols), f32),
            jax.ShapeDtypeStruct((state_count, all_states), f32),
            jax.ShapeDtypeStruct((state_count, all_states), f32),
        ),
        in_specs=[hbm, hbm, hbm, hbm, hbm],
        out_specs=(vmem, vmem, vmem),
        scratch_shapes=[
            pltpu.VMEM((half, (chunk + 2 * RADIUS) * rows, cols), f32),
            pltpu.VMEM((half, planes * rows, cols), f32),
            pltpu.VMEM((DEGREE + 2, chunk + 2 * RADIUS, half, area), f32),
            pltpu.VMEM((planes, half, area), f32),
            pltpu.VMEM((chunk, rows, cols), f32),
            pltpu.VMEM((atoms, support), jnp.int32),
            pltpu.VMEM((atoms, support), f32),
            pltpu.VMEM((1, atoms), f32),
            pltpu.VMEM((atoms, chunk * rows, cols), f32),
            pltpu.VMEM((chunk, 2 * atoms, area), jnp.bfloat16),
            pltpu.VMEM((2 * cols, 2 * cols), jnp.bfloat16),
            pltpu.VMEM((chunk, half, area), f32),
            pltpu.VMEM((DEGREE + 2, half, wide), f32),
            pltpu.VMEM((DEGREE + 1, 2, half, wide), f32),
            pltpu.VMEM((5, half, wide), f32),
            pltpu.VMEM((atoms, atoms), f32),
            pltpu.VMEM((2 * RADIUS, half, area), f32),
            pltpu.VMEM((planes, half, area), f32),
            pltpu.VMEM((2, planes // bands, all_states, area), f32),
            pltpu.VMEM((all_states, 2 * all_states), f32),
            pltpu.VMEM((bands, state_count, 2 * all_states), f32),
            pltpu.VMEM((state_count, 2 * all_states), f32),
            pltpu.VMEM((slabs, state_count, 2 * all_states), f32),
            pltpu.SemaphoreType.DMA((slots,)),
            pltpu.SemaphoreType.DMA((slots,)),
            pltpu.SemaphoreType.DMA((6,)),
        ],
        compiler_params=pltpu.CompilerParams(
            collective_id=0, has_side_effects=True, vmem_limit_bytes=48 * 1024 * 1024
        ),
    )(*(pltpu.with_memory_space_constraint(x, pltpu.HBM) for x in (states.reshape(state_count, planes * rows, cols), potential, proj_index, proj_value, strength)))

    def place(*refs):
        moves = [pltpu.make_async_copy(refs[n], refs[3 + n], refs[6].at[n]) for n in range(3)]
        for move in moves:
            move.start()
        for move in moves:
            move.wait()

    out, gram, ham = pl.pallas_call(
        place,
        out_shape=tuple(jax.ShapeDtypeStruct(x.shape, f32) for x in (out, gram, ham)),
        in_specs=[vmem] * 3,
        out_specs=(hbm,) * 3,
        scratch_shapes=[pltpu.SemaphoreType.DMA((3,))],
    )(*(pltpu.with_memory_space_constraint(x, pltpu.VMEM) for x in (out, gram, ham)))
    return out.reshape(states.shape), gram, ham


def solution(mesh):
    in_specs = (P("band", "grid", None, None), P("grid", None, None), P(), P(), P())
    out_specs = (P("band", "grid", None, None), P("band", None), P("band", None))
    return jax.shard_map(
        functools.partial(per_device, mesh.shape["band"], mesh.shape["grid"]),
        mesh=mesh, in_specs=in_specs, out_specs=out_specs, check_vma=False,
    )
```
